32 devices in a mesh: dp: 8 (over z, x), tensor: 4 (over y, core).
Axes of the slice: x: 2, y: 2, z: 4, core: 2. Of those that a mesh axis runs over, the one named last changes fastest.
Arguments:
- inputs: bfloat16 [8192, 1024], P(('dp', 'tensor')), may hold values from -6 to 6, as said below
- teacher: bfloat16 [8192, 1024], P(('dp', 'tensor')), may hold values from -9 to 9, as said below
- query_weight: bfloat16 [1024, 1024], P('dp', 'tensor'), may hold values from -0.25 to 0.25
- key_weight: bfloat16 [1024, 1024], P('dp', 'tensor'), may hold values from -0.25 to 0.25
- value_weight: bfloat16 [1024, 1024], P('dp', 'tensor'), may hold values from -0.1875 to 0.1875
- out_weight: bfloat16 [1024, 1024], P('tensor', 'dp'), may hold values from -1 to 1
- up_weight: bfloat16 [1024, 4096], P('dp', 'tensor'), may hold values from -0.1875 to 0.1875
- down_weight: bfloat16 [4096, 1024], P('tensor', 'dp'), may hold values from -0.125 to 0.125
- query_bias: float32 [1024], replicated, may hold values from -3 to 3
- value_bias: float32 [1024], replicated, may hold values from -0.18 to 0.18
- out_bias: float32 [1024], replicated, may hold values from -0.3 to 0.3
- up_bias: float32 [4096], replicated, may hold values from -1.2 to -0.6
- down_bias: float32 [1024], replicated, may hold values from -0.3 to 0.3
- first_gain: float32 [1024], replicated, may hold values from 0.5 to 1.5
- first_shift: float32 [1024], replicated, may hold values from -0.3 to 0.3
- second_gain: float32 [1024], replicated, may hold values from 0.5 to 1.5
- second_shift: float32 [1024], replicated, may hold values from -0.3 to 0.3
Outputs:
- output: bfloat16 [8192, 1024], P(('dp', 'tensor'))
- loss: float32 [], replicated
- grad_inputs: float32 [8192, 1024], P(('dp', 'tensor'))
- grad_query_weight: float32 [1024, 1024], P('dp', 'tensor')
- grad_key_weight: float32 [1024, 1024], P('dp', 'tensor')
- grad_value_weight: float32 [1024, 1024], P('dp', 'tensor')
- grad_out_weight: float32 [1024, 1024], P('tensor', 'dp')
- grad_up_weight: float32 [1024, 4096], P('dp', 'tensor')
- grad_down_weight: float32 [4096, 1024], P('tensor', 'dp')
- grad_query_bias: float32 [1024], replicated
- grad_value_bias: float32 [1024], replicated
- grad_out_bias: float32 [1024], replicated
- grad_up_bias: float32 [4096], replicated
- grad_down_bias: float32 [1024], replicated
- grad_first_gain: float32 [1024], replicated
- grad_first_shift: float32 [1024], replicated
- grad_second_gain: float32 [1024], replicated
- grad_second_shift: float32 [1024], replicated
The draws below stay inside these ranges and needn't reach their ends.
Inputs may be any that keep to these rules, and one draw needn't show every extreme that they name: `inputs`: states of order one. `teacher`: target states of order one.
All inputs are finite; a program needn't handle non-finite values.
Results may differ from the reference program's by a relative error of at most 0.02.
Values may be sent and summed in bfloat16 or wider, within the bound.
A program may use at most 128 MiB of HBM per device.

```python
import math
import jax
import jax.numpy as jnp
from jax import lax

D = 1024
HEADS = 16
HEAD_DIM = 64
FF = 4096
SEQ = 512
TOKENS = 8192


def state_field(key, spread, limit):
    sampled = jax.random.normal(key, (TOKENS, D), jnp.float32) * spread
    return jnp.clip(sampled, -limit, limit)


def draw_inputs(key, part):
    return state_field(jax.random.fold_in(key, 11), 1.0, 6.0).astype(jnp.bfloat16)


def draw_teacher(key, part):
    return state_field(jax.random.fold_in(key, 23), 1.5, 9.0).astype(jnp.bfloat16)


def shard_levels(key, dims, shards, low, top_value):
    level = 1.0
    for position, parts in shards:
        draws = jax.random.uniform(jax.random.fold_in(jax.random.fold_in(key, 6), position), (parts,), jnp.float32, low / len(shards), top_value / len(shards))
        level = level * jnp.repeat(jnp.exp(draws), dims[position] // parts).reshape((-1,) + (1,) * (len(dims) - 1 - position))
    return level


def bell_draw(stream_key, extent, scale, bound, cuts=(), held_as=jnp.bfloat16):
    array = jax.random.normal(stream_key, extent, jnp.float32) * scale
    if len(cuts) > 0:
        array = shard_levels(stream_key, extent, cuts, -0.22, 0.18) * array
    return jnp.clip(array, min=-bound, max=bound).astype(held_as)


def setup_inputs(seed: int = 0) -> dict:
    key_of = jax.random.split(jax.random.key(seed), 18)
    return {
        "inputs": draw_inputs(jax.random.fold_in(key_of[17], 71), 0),
        "teacher": draw_teacher(jax.random.fold_in(key_of[17], 71), 0),
        "query_weight": bell_draw(key_of[2], (D, D), (D // 2) ** -0.5, 0.25, ((0, 8), (1, 4))),
        "key_weight": bell_draw(key_of[3], (D, D), (D // 2) ** -0.5, 0.25, ((0, 8), (1, 4))),
        "value_weight": bell_draw(key_of[4], (D, D), D ** -0.5, 0.1875, ((0, 8), (1, 4))),
        "out_weight": bell_draw(key_of[5], (D, D), (D // 32) ** -0.5, 1.0, ((0, 4), (1, 8))),
        "up_weight": bell_draw(key_of[6], (D, FF), D ** -0.5, 0.1875, ((0, 8), (1, 4))),
        "down_weight": bell_draw(key_of[7], (FF, D), (FF // 2) ** -0.5, 0.125, ((0, 4), (1, 8))),
        "query_bias": bell_draw(key_of[8], (D,), 0.5, 3.0, (), jnp.float32),
        "value_bias": bell_draw(key_of[9], (D,), 0.03, 0.18, (), jnp.float32),
        "out_bias": bell_draw(key_of[10], (D,), 0.05, 0.3, (), jnp.float32),
        "up_bias": jnp.clip(jax.random.uniform(key_of[11], (FF,), jnp.float32, -1.2, -0.6), -1.2, -0.6),
        "down_bias": bell_draw(key_of[12], (D,), 0.05, 0.3, (), jnp.float32),
        "first_gain": jnp.clip(1.0 + 0.1 * jax.random.normal(key_of[13], (D,), jnp.float32), 0.5, 1.5),
        "first_shift": bell_draw(key_of[14], (D,), 0.05, 0.3, (), jnp.float32),
        "second_gain": jnp.clip(1.0 + 0.1 * jax.random.normal(key_of[15], (D,), jnp.float32), 0.5, 1.5),
        "second_shift": bell_draw(key_of[16], (D,), 0.05, 0.3, (), jnp.float32),
    }


@jax.custom_vjp
def low(v):
    return lax.optimization_barrier(v.astype(jnp.bfloat16)).astype(jnp.float32)

@jax.custom_vjp
def low_back(v):
    return v

def low_keep(v):
    return (low(v), None)

def low_pass(kept, grad):
    return (grad,)

def back_keep(v):
    return (v, None)

def back_low(kept, grad):
    return (low(grad),)
low.defvjp(low_keep, low_pass)
low_back.defvjp(back_keep, back_low)
EPSILON = 1e-05

def matmul(left, right):
    return jnp.dot(left, right, precision=lax.Precision.HIGHEST)

def norm_rows(values, gain, shift):
    center = values - lax.optimization_barrier(jnp.mean(values, axis=-1, keepdims=True))
    variance = lax.optimization_barrier(jnp.mean(center * center, axis=-1, keepdims=True))
    return center * lax.rsqrt(variance + EPSILON) * gain + shift

def forward(params, states, targets):
    query_weight, key_weight, value_weight, out_weight, up_weight, down_weight, query_bias, value_bias, out_bias, up_bias, down_bias, first_gain, first_shift, second_gain, second_shift = params
    row_count = states.shape[0]
    seq_count = row_count // SEQ
    query = low(low_back(matmul(states, query_weight) + query_bias))
    keys = low(low_back(matmul(states, key_weight)))
    values = low(low_back(matmul(states, value_weight) + value_bias))
    query_heads = query.reshape(seq_count, SEQ, HEADS, HEAD_DIM)
    key_heads = keys.reshape(seq_count, SEQ, HEADS, HEAD_DIM)
    value_heads = values.reshape(seq_count, SEQ, HEADS, HEAD_DIM)
    scores = low_back(jnp.einsum('bqhd,bkhd->bhqk', query_heads, key_heads, precision=lax.Precision.HIGHEST) / math.sqrt(HEAD_DIM))
    probs = jax.nn.softmax(scores, axis=-1)
    context = jnp.einsum('bhqk,bkhd->bqhd', low(probs), value_heads, precision=lax.Precision.HIGHEST).reshape(row_count, D)
    context = low(low_back(context))
    attended = low_back(matmul(context, out_weight)) + out_bias
    hidden = norm_rows(states + attended, first_gain, first_shift)
    upper = low_back(matmul(low(hidden), up_weight) + up_bias)
    activated = low(0.5 * upper * (1.0 + jax.scipy.special.erf(upper / math.sqrt(2.0))))
    mixed = low_back(matmul(activated, down_weight)) + down_bias
    result = norm_rows(hidden + mixed, second_gain, second_shift)
    diff = result - targets
    return (result, 0.5 * jnp.sum(diff * diff))

def reference(inputs, teacher, query_weight, key_weight, value_weight, out_weight, up_weight, down_weight, query_bias, value_bias, out_bias, up_bias, down_bias, first_gain, first_shift, second_gain, second_shift):
    params = tuple((p.astype(jnp.float32) for p in (query_weight, key_weight, value_weight, out_weight, up_weight, down_weight, query_bias, value_bias, out_bias, up_bias, down_bias, first_gain, first_shift, second_gain, second_shift)))
    total_seqs = TOKENS // SEQ
    group = math.gcd(total_seqs, max(1, 4096 // SEQ))
    group_rows = group * SEQ
    blocks = TOKENS // group_rows
    state_blocks = inputs.astype(jnp.float32).reshape(blocks, group_rows, D)
    target_blocks = teacher.astype(jnp.float32).reshape(blocks, group_rows, D)

    def step(carry, item):
        grad_sums, loss_sum = carry
        state_block, target_block = item

        def local(param_set, states):
            return forward(param_set, states, target_block)
        (result, loss_part), pullback = jax.vjp(local, params, state_block)
        grad_params, grad_states = pullback((jnp.zeros_like(result), jnp.ones_like(loss_part)))
        grad_sums = jax.tree.map(lambda a, b: a + b, grad_sums, grad_params)
        return ((grad_sums, loss_sum + loss_part), (result.astype(jnp.bfloat16), grad_states))
    start = (jax.tree.map(jnp.zeros_like, params), jnp.zeros((), jnp.float32))
    (grad_sums, loss_sum), (results, grad_states) = lax.scan(step, start, (state_blocks, target_blocks))
    output = results.reshape(TOKENS, D)
    grad_inputs = grad_states.reshape(TOKENS, D)
    loss = loss_sum / TOKENS
    return (output, loss, grad_inputs) + tuple(grad_sums)
```

```python
import functools
import math

import jax
import jax.numpy as jnp
from jax import lax
from jax.experimental import pallas as pl
from jax.experimental.pallas import tpu as pltpu
from jax.sharding import PartitionSpec as P

HEAD_DIM = 64
SEQ = 512
EPSILON = 1e-05
MESH = pl.DeviceIdType.MESH
F32 = jnp.float32
BF16 = jnp.bfloat16
NN = ((1,), (0,))
NT = ((1,), (1,))
TN = ((0,), (0,))
CHUNK = 32
ROOT_TWO = math.sqrt(2.0)
ROOT_TWO_PI = math.sqrt(2.0 * math.pi)
VECTORS = 16


def dot(left, right, dims):
    return lax.dot_general(left, right, (dims, ((), ())), preferred_element_type=F32)


def remote(src, dst, send, recv, peer):
    return pltpu.make_async_remote_copy(
        src_ref=src, dst_ref=dst, send_sem=send, recv_sem=recv, device_id=peer, device_id_type=MESH
    )


class Place:
    def __init__(self, outer):
        self.outer = outer
        self.dp = lax.axis_index("dp")
        self.t = lax.axis_index("tensor")
        self.z, self.x = self.dp // 2, self.dp % 2
        self.y, self.c = self.t // 2, self.t % 2
        self.x_peer = (self.z * 2 + 1 - self.x, self.t)
        self.y_peer = (self.dp, (1 - self.y) * 2 + self.c)
        self.c_peer = (self.dp, self.y * 2 + 1 - self.c)
        self.diag = (1 - self.y) * 2 + 1 - self.c
        self.diag_peer = (self.dp, self.diag)

    def z_peer(self, step):
        return (lax.rem(self.z + step, self.outer) * 2 + self.x, self.t)

    def enter(self):
        barrier = pltpu.get_barrier_semaphore()

        def greet(step, carry):
            pl.semaphore_signal(barrier, inc=1, device_id=self.z_peer(step), device_id_type=MESH)
            return carry

        lax.fori_loop(1, self.outer, greet, 0)
        for peer in (self.x_peer, self.y_peer, self.diag_peer, self.c_peer):
            pl.semaphore_signal(barrier, inc=1, device_id=peer, device_id_type=MESH)
        pl.semaphore_wait(barrier, self.outer + 3)


def columns(piece, width):
    start = piece * width
    if not isinstance(start, int):
        start = pl.multiple_of(start, width)
    return pl.ds(start, width)


class Weights:
    def __init__(self, k, w, full, send, recv, width):
        self.k, self.w, self.full, self.send, self.recv, self.width = k, w, full, send, recv, width

    def first(self, p, step):
        k, cols = self.k, columns(p, self.width)
        return remote(
            self.w.at[:, cols],
            self.full.at[k.z, k.x, :, cols],
            self.send.at[0, p],
            self.recv.at[0, p],
            k.z_peer(step),
        )

    def all_first(self, p):
        block = self.full.at[pl.ds(0, self.k.outer - 1), 0, :, columns(p, self.width)]
        return remote(block, block, self.send.at[0, p], self.recv.at[0, p], self.k.x_peer)

    def second(self, p):
        block = self.full.at[:, self.k.x, :, columns(p, self.width)]
        return remote(block, block, self.send.at[1, p], self.recv.at[1, p], self.k.x_peer)

    def start(self, pieces):
        def piece(p, carry):
            def one(step, inner):
                self.first(p, step).start()
                return inner

            return lax.fori_loop(1, self.k.outer, one, carry)

        lax.fori_loop(0, pieces, piece, 0)

    def forward(self, p):
        self.all_first(p).wait_recv()
        self.second(p).start()

    def arrive(self, p):
        self.second(p).wait_recv()

    def drain(self, pieces):
        def piece(p, carry):
            self.all_first(p).wait_send()
            self.second(p).wait_send()
            return carry

        lax.fori_loop(0, pieces, piece, 0)


class Gradients:
    def __init__(self, k, part, near, far, out, send, recv, width):
        self.k, self.part, self.near, self.far, self.out = k, part, near, far, out
        self.send, self.recv, self.width = send, recv, width

    def one(self, p):
        k, cols = self.k, columns(p, self.width)
        return remote(
            self.part.at[:, 1 - k.x, :, cols],
            self.near.at[:, :, cols],
            self.send.at[0, p],
            self.recv.at[0, p],
            k.x_peer,
        )

    def two(self, p, step):
        k, cols = self.k, columns(p, self.width)
        return remote(
            self.part.at[lax.rem(k.z + step, k.outer), k.x, :, cols],
            self.far.at[step - 1, :, cols],
            self.send.at[1, p],
            self.recv.at[1, p],
            k.z_peer(step),
        )

    def all_two(self, p):
        block = self.far.at[:, :, columns(p, self.width)]
        return remote(block, block, self.send.at[1, p], self.recv.at[1, p], self.k.x_peer)

    def start(self, p):
        self.one(p).start()

    def forward(self, p):
        k, cols = self.k, columns(p, self.width)
        self.one(p).wait_recv()
        here = self.part[:, k.x, :, cols].astype(F32)
        self.part[:, k.x, :, cols] = (here + self.near[:, :, cols].astype(F32)).astype(BF16)

        def send(step, carry):
            self.two(p, step).start()
            return carry

        lax.fori_loop(1, k.outer, send, 0)

    def finish(self, p):
        k, cols = self.k, columns(p, self.width)
        self.all_two(p).wait_recv()

        def add(i, total):
            return total + self.far[i, :, cols].astype(F32)

        total = self.part[k.z, k.x, :, cols].astype(F32)
        self.out[:, cols] = lax.fori_loop(0, k.outer - 1, add, total)

    def drain(self, pieces):
        def piece(p, carry):
            self.one(p).wait_send()
            self.all_two(p).wait_send()
            return carry

        lax.fori_loop(0, pieces, piece, 0)


class Spread:
    def __init__(self, k, blocks, send, recv, phase):
        self.k, self.blocks, self.send, self.recv, self.phase = k, blocks, send, recv, phase

    def copy(self, number, block, peer):
        ref = self.blocks.at[block]
        return remote(
            ref, ref, self.send.at[self.phase, number], self.recv.at[self.phase, number], peer
        )

    def near(self):
        return self.copy(0, self.k.t, self.k.c_peer)

    def far(self):
        return self.copy(1, self.k.t, self.k.diag_peer)

    def relay(self):
        return self.copy(2, self.k.diag, self.k.c_peer)

    def start(self):
        self.far().start()
        self.near().start()

    def own(self):
        self.near().wait_recv()

    def other(self):
        self.far().wait_recv()
        self.relay().start()
        self.relay().wait_recv()

    def drain(self):
        self.near().wait_send()
        self.far().wait_send()
        self.relay().wait_send()


class Reduce:
    def __init__(self, k, out, inbox, keep, send, recv, phase):
        self.k, self.out, self.inbox, self.keep = k, out, inbox, keep
        self.send, self.recv, self.phase = send, recv, phase

    def copy(self, number, phase=None):
        peer = self.k.y_peer if number == 2 else self.k.c_peer
        phase = self.phase if phase is None else phase
        return remote(
            self.out.at[number],
            self.inbox.at[number],
            self.send.at[phase, number],
            self.recv.at[phase, number],
            peer,
        )

    def free(self, number):
        if self.phase > 0:
            self.copy(number, self.phase - 1).wait_send()

    def across(self, value):
        self.free(0)
        self.out[0] = value.astype(BF16)
        self.copy(0).start()

    def theirs(self, value):
        self.free(2)
        self.copy(0).wait_recv()
        self.out[2] = (value + self.inbox[0].astype(F32)).astype(BF16)
        self.copy(2).start()

    def partner(self, value):
        self.free(1)
        self.out[1] = value.astype(BF16)
        self.copy(1).start()

    def mine(self, value):
        self.keep[...] = value

    def wait(self):
        self.copy(1).wait_recv()
        self.copy(2).wait_recv()

    def total(self, rows):
        return self.keep[rows, :] + (
            self.inbox[1, rows, :].astype(F32) + self.inbox[2, rows, :].astype(F32)
        )

    def drain(self):
        for number in range(3):
            self.copy(number).wait_send()


def fold(values):
    rows, width = values.shape
    return jnp.sum(values.reshape(rows // 8, 8, width), axis=0)


def mean(values):
    return jnp.sum(values, axis=-1, keepdims=True) * (1.0 / values.shape[-1])


def body(
    outer,
    x_ref,
    teacher_ref,
    w_ref,
    vec_ref,
    out_ref,
    gin_ref,
    gsh_ref,
    gvec_ref,
    W,
    G,
    near,
    far,
    X,
    H,
    MX,
    GF,
    Q,
    K,
    V,
    C,
    GC,
    DQKV,
    PT,
    SL,
    ACT,
    GU,
    OWN,
    HID,
    N1,
    R1,
    GS,
    SUMS,
    ACC,
    OUTBOX,
    INBOX,
    VA,
    VR,
    VZ,
    w_send,
    w_recv,
    g_send,
    g_recv,
    s_send,
    s_recv,
    r_send,
    r_recv,
    v_send,
    v_recv,
    own_sem,
):
    k = Place(outer)
    model = x_ref.shape[1]
    rows = x_ref.shape[0]
    heads_width = Q.shape[2]
    inner = ACT.shape[2]
    heads = heads_width // HEAD_DIM
    width = heads_width
    up_piece = 4
    down_piece = 4 + inner // width
    pieces = 4 + 2 * (inner // width)
    scale = 1.0 / math.sqrt(HEAD_DIM)
    mine, theirs = k.y, 1 - k.y

    weights = Weights(k, w_ref, W, w_send, w_recv, width)
    grads = Gradients(k, G, near, far, gsh_ref, g_send, g_recv, width)

    def spread(blocks, phase):
        return Spread(k, blocks, s_send, s_recv, phase)

    def reduce(phase):
        return Reduce(k, OUTBOX, INBOX, OWN, r_send, r_recv, phase)

    def matrix(start, size):
        return W[:, :, :, pl.ds(start, size)].reshape(model, size)

    def vector(row):
        return vec_ref[pl.ds(row, 1), :]

    def pair(blocks, seq):
        return blocks[pl.ds(2 * seq, 2)].reshape(2 * rows, model)

    def part_rows(core):
        return pl.ds(pl.multiple_of(core * rows, rows), rows)

    def norm_loop(step):
        def one(i, carry):
            step(pl.ds(pl.multiple_of(i * CHUNK, CHUNK), CHUNK))
            return carry

        lax.fori_loop(0, rows // CHUNK, one, 0)

    own_w = pltpu.make_async_copy(w_ref, W.at[k.z, k.x], own_sem.at[0])
    own_x = pltpu.make_async_copy(x_ref, X.at[k.t], own_sem.at[1])
    own_w.start()
    own_x.start()
    SUMS[...] = jnp.zeros_like(SUMS)
    VA[0] = jnp.zeros_like(VA[0])
    k.enter()
    own_x.wait()
    s0 = spread(X, 0)
    s0.start()
    weights.start(pieces)
    own_w.wait()
    s0.own()
    s0.other()

    weights.forward(0)
    weights.forward(1)
    for p, held in ((0, Q), (1, K), (2, V)):
        weights.arrive(p)
        weights.forward(p + 2)
        for seq in range(2):
            product = dot(X[pl.ds(2 * seq, 2)].reshape(2 * rows, model), matrix(p * width, width), NN)
            if p != 1:
                bias = vec_ref[p // 2 : p // 2 + 1, pl.ds(pl.multiple_of(k.t * width, width), width)]
                product = product + bias
            held[seq] = product.astype(BF16)

    def head_mask(h):
        lane = lax.broadcasted_iota(jnp.int32, (1, width), 1)
        inside = (lane >= h * HEAD_DIM) & (lane < (h + 1) * HEAD_DIM)
        return jnp.where(inside, 1.0, 0.0).astype(BF16)

    def attend(seq):
        ACC[0] = jnp.zeros_like(ACC[0])

        def head(h, carry):
            mask = head_mask(h)
            scores = dot(K[seq], Q[seq] * mask, NT) * scale
            raised = jnp.exp(scores - jnp.max(scores, axis=0, keepdims=True))
            probs = (raised * (1.0 / jnp.sum(raised, axis=0, keepdims=True))).astype(BF16)
            PT[seq, h] = probs
            ACC[0] += dot(probs, V[seq] * mask, TN)
            return carry

        lax.fori_loop(0, heads, head, 0)
        C[seq] = ACC[0].astype(BF16)

    def out_block(seq, core):
        return dot(C[seq, part_rows(core), :], matrix(3 * width, width), NT)

    r0 = reduce(0)
    attend(theirs)
    weights.arrive(3)
    r0.across(out_block(theirs, 1 - k.c))
    r0.theirs(out_block(theirs, k.c))
    weights.forward(5)
    attend(mine)
    r0.partner(out_block(mine, 1 - k.c))
    r0.mine(out_block(mine, k.c))
    weights.forward(6)
    r0.wait()

    def first_norm(r):
        first = x_ref[r, :].astype(F32) + r0.total(r) + vector(2)
        center = first - mean(first)
        scaling = lax.rsqrt(mean(center * center) + EPSILON)
        normed = center * scaling
        hidden = normed * vector(8) + vector(9)
        N1[r, :] = normed
        R1[r, :] = jnp.broadcast_to(scaling, (CHUNK, R1.shape[1]))
        HID[r, :] = hidden
        H[k.t, r, :] = hidden.astype(BF16)

    norm_loop(first_norm)
    s1 = spread(H, 1)
    s1.start()
    weights.forward(7)
    for p in range(4, 8):
        weights.arrive(p)
    s1.own()

    def up(seq):
        def part(n, carry):
            cols = pl.ds(pl.multiple_of(n * width, width), width)
            wide = pl.ds(pl.multiple_of((up_piece + n) * width, width), width)
            upper = dot(pair(H, seq), W[:, :, :, wide].reshape(model, width), NN)
            upper = upper + vec_ref[pl.ds(3 + k.t, 1), cols]
            erf_part = 1.0 + lax.erf(upper * (1.0 / ROOT_TWO))
            ACT[seq, :, cols] = (0.5 * upper * erf_part).astype(BF16)
            SL[seq, :, cols] = 0.5 * erf_part + upper * jnp.exp(-0.5 * upper * upper) * (
                1.0 / ROOT_TWO_PI
            )
            return carry

        lax.fori_loop(0, inner // width, part, 0)

    def down_block(seq, core):
        return dot(ACT[seq, part_rows(core), :], matrix(down_piece * width, inner), NT)

    up(mine)
    weights.forward(8)
    weights.forward(9)
    s1.other()
    up(theirs)
    weights.forward(10)
    weights.forward(11)
    for p in range(8, 12):
        weights.arrive(p)
    r1 = reduce(1)
    r1.across(down_block(theirs, 1 - k.c))
    r1.theirs(down_block(theirs, k.c))
    r1.partner(down_block(mine, 1 - k.c))
    r1.mine(down_block(mine, k.c))
    r1.wait()

    def norm_back(d, gain, normed, scaling):
        e = d * gain
        return scaling * (e - mean(e) - normed * mean(e * normed))

    def second_norm(r):
        second = HID[r, :] + r1.total(r) + vector(7)
        center = second - mean(second)
        scaling = lax.rsqrt(mean(center * center) + EPSILON)
        normed = center * scaling
        result = normed * vector(10) + vector(11)
        out_ref[r, :] = result.astype(BF16)
        diff = result - teacher_ref[r, :].astype(F32)
        grad = norm_back(diff, vector(10), normed, scaling)
        GS[r, :] = grad
        MX[k.t, r, :] = grad.astype(BF16)
        SUMS[0] += fold(grad)
        SUMS[1] += fold(diff * normed)
        SUMS[2] += fold(diff)
        SUMS[3] += fold(diff * diff)

    norm_loop(second_norm)
    s2 = spread(MX, 2)
    s2.start()
    s2.own()

    def back_up(seq):
        def part(n, carry):
            cols = pl.ds(pl.multiple_of(n * width, width), width)
            wide = pl.ds(pl.multiple_of((down_piece + n) * width, width), width)
            grad = dot(pair(MX, seq), W[:, :, :, wide].reshape(model, width), NN)
            grad = (grad * SL[seq, :, cols]).astype(BF16)
            GU[seq, :, cols] = grad
            SUMS[7, :, cols] += fold(grad.astype(F32))
            return carry

        lax.fori_loop(0, inner // width, part, 0)

    def hidden_block(seq, core):
        return dot(GU[seq, part_rows(core), :], matrix(up_piece * width, inner), NT)

    def weight_grad(left, right, first, count):
        def piece(n, carry):
            cols = pl.ds(pl.multiple_of(n * width, width), width)
            tokens = 4 * rows
            grad = dot(
                left[...].reshape(tokens, model), right[:, :, cols].reshape(tokens, width), TN
            )
            wide = pl.ds(pl.multiple_of((first + n) * width, width), width)
            G[:, :, :, wide] = grad.astype(BF16).reshape(outer, 2, model // (2 * outer), width)

            @pl.when(n > 0)
            def _():
                grads.start(first + n - 1)

            return carry

        lax.fori_loop(0, count, piece, 0)

    r2 = reduce(2)
    back_up(mine)
    s2.other()
    back_up(theirs)
    r2.across(hidden_block(theirs, 1 - k.c))
    r2.theirs(hidden_block(theirs, k.c))
    weight_grad(MX, ACT, down_piece, inner // width)
    r2.partner(hidden_block(mine, 1 - k.c))
    grads.start(down_piece + inner // width - 1)
    r2.mine(hidden_block(mine, k.c))
    weight_grad(H, GU, up_piece, inner // width)
    r2.wait()
    grads.start(up_piece + inner // width - 1)

    def first_back(r):
        grad_hidden = GS[r, :] + r2.total(r)
        normed = N1[r, :]
        grad = norm_back(grad_hidden, vector(8), normed, R1[r, :][:, :1])
        GS[r, :] = grad
        GF[k.t, r, :] = grad.astype(BF16)
        SUMS[4] += fold(grad)
        SUMS[5] += fold(grad_hidden * normed)
        SUMS[6] += fold(grad_hidden)

    norm_loop(first_back)
    s3 = spread(GF, 3)
    s3.start()
    for p in range(8, 12):
        grads.forward(p)
    s3.own()

    def attend_back(seq):
        GC[...] = dot(pair(GF, seq), matrix(3 * width, width), NN).astype(BF16)
        ACC[...] = jnp.zeros_like(ACC)

        def head(h, carry):
            mask = head_mask(h)
            context = GC[...] * mask
            low = PT[seq, h]
            ACC[2] += dot(low, context, NN)
            probs = low.astype(F32)
            grad = dot(V[seq], context, NT)
            across = jnp.sum(probs * grad, axis=0, keepdims=True)
            grad = (probs * (grad - across)).astype(BF16)
            ACC[1] += dot(grad, Q[seq] * mask, NN)
            ACC[0] += dot(grad, K[seq] * mask, TN)
            return carry

        lax.fori_loop(0, heads, head, 0)
        for n in range(3):
            grad = ACC[n] if n == 2 else ACC[n] * scale
            DQKV[seq, :, n * width : (n + 1) * width] = grad.astype(BF16)

    def input_block(seq, core):
        return dot(DQKV[seq, part_rows(core), :], matrix(0, 3 * width), NT)

    attend_back(mine)
    s3.other()
    for p in range(4, 8):
        grads.forward(p)
    attend_back(theirs)
    weight_grad(X, DQKV, 0, 3)
    r3 = reduce(3)
    r3.across(input_block(theirs, 1 - k.c))
    grads.start(2)
    r3.theirs(input_block(theirs, k.c))
    weight_grad(GF, C, 3, 1)
    r3.partner(input_block(mine, 1 - k.c))
    grads.start(3)
    r3.mine(input_block(mine, k.c))

    here = pl.ds(pl.multiple_of(k.t * width, width), width)
    for row, n in ((0, 0), (1, 2)):
        grad = DQKV[:, :, n * width : (n + 1) * width].reshape(4 * rows, width).astype(F32)
        VA[0, row : row + 1, here] = jnp.sum(grad, axis=0, keepdims=True)
    VA[0, pl.ds(3 + k.t, 1), :] = jnp.sum(SUMS[7], axis=0, keepdims=True)
    for row, n in ((7, 0), (10, 1), (11, 2), (12, 3), (2, 4), (8, 5), (9, 6)):
        VA[0, row : row + 1, :] = jnp.sum(SUMS[n], axis=0, keepdims=True)

    def vector_hop(n, peer):
        return remote(VA.at[n], VR.at[n], v_send.at[n], v_recv.at[n], peer)

    def vector_last(step):
        return remote(VA.at[3], VZ.at[k.z], v_send.at[3], v_recv.at[3], k.z_peer(step))

    hops = [vector_hop(n, peer) for n, peer in enumerate((k.c_peer, k.y_peer, k.x_peer))]
    grads.forward(0)
    for n, hop in enumerate(hops):
        hop.start()
        if n < 2:
            grads.forward(1 + n)
        hop.wait_recv()
        VA[n + 1] = VA[n] + VR[n]
    VZ[k.z] = VA[3]
    for p in (3,):
        grads.forward(p)

    def send_last(step, carry):
        vector_last(step).start()
        return carry

    lax.fori_loop(1, outer, send_last, 0)
    for p in (8, 9, 10, 11, 4, 5, 6, 7):
        grads.finish(p)
    r3.wait()

    def last(r):
        gin_ref[r, :] = GS[r, :] + r3.total(r)

    norm_loop(last)
    vz_all = VZ.at[pl.ds(0, outer - 1)]
    every = remote(vz_all, vz_all, v_send.at[3], v_recv.at[3], k.x_peer)
    every.wait_recv()

    def add(i, total):
        return total + VZ[i]

    gvec_ref[...] = lax.fori_loop(1, outer, add, VZ[0])
    for p in (0, 1, 2, 3):
        grads.finish(p)

    weights.drain(pieces)
    grads.drain(pieces)
    for s in (s0, s1, s2, s3):
        s.drain()
    r3.drain()
    for hop in hops:
        hop.wait_send()
    every.wait_send()


def layer(inputs, teacher, w, vec, outer, inner):
    rows, model = inputs.shape
    shard_rows, columns_all = w.shape
    width = (columns_all - 2 * inner) // 4
    heads = width // HEAD_DIM
    pieces = columns_all // width
    seq = 2 * rows
    vmem = pl.BlockSpec(memory_space=pltpu.VMEM)
    full = (outer, 2, shard_rows, columns_all)
    dma = pltpu.SemaphoreType.DMA
    return pl.pallas_call(
        functools.partial(body, outer),
        out_shape=(
            jax.ShapeDtypeStruct((rows, model), BF16),
            jax.ShapeDtypeStruct((rows, model), F32),
            jax.ShapeDtypeStruct((shard_rows, columns_all), F32),
            jax.ShapeDtypeStruct((VECTORS, model), F32),
        ),
        in_specs=[vmem] * 4,
        out_specs=(vmem,) * 4,
        scratch_shapes=[
            pltpu.VMEM(full, BF16),
            pltpu.VMEM(full, BF16),
            pltpu.VMEM((outer, shard_rows, columns_all), BF16),
            pltpu.VMEM((outer - 1, shard_rows, columns_all), BF16),
            pltpu.VMEM((4, rows, model), BF16),
            pltpu.VMEM((4, rows, model), BF16),
            pltpu.VMEM((4, rows, model), BF16),
            pltpu.VMEM((4, rows, model), BF16),
            pltpu.VMEM((2, seq, width), BF16),
            pltpu.VMEM((2, seq, width), BF16),
            pltpu.VMEM((2, seq, width), BF16),
            pltpu.VMEM((2, seq, width), BF16),
            pltpu.VMEM((seq, width), BF16),
            pltpu.VMEM((2, seq, 3 * width), BF16),
            pltpu.VMEM((2, heads, seq, seq), BF16),
            pltpu.VMEM((2, seq, inner), F32),
            pltpu.VMEM((2, seq, inner), BF16),
            pltpu.VMEM((2, seq, inner), BF16),
            pltpu.VMEM((rows, model), F32),
            pltpu.VMEM((rows, model), F32),
            pltpu.VMEM((rows, model), F32),
            pltpu.VMEM((rows, 128), F32),
            pltpu.VMEM((rows, model), F32),
            pltpu.VMEM((8, 8, model), F32),
            pltpu.VMEM((3, seq, width), F32),
            pltpu.VMEM((3, rows, model), BF16),
            pltpu.VMEM((3, rows, model), BF16),
            pltpu.VMEM((4, VECTORS, model), F32),
            pltpu.VMEM((3, VECTORS, model), F32),
            pltpu.VMEM((outer, VECTORS, model), F32),
            dma((2, pieces)),
            dma((2, pieces)),
            dma((2, pieces)),
            dma((2, pieces)),
            dma((4, 3)),
            dma((4, 3)),
            dma((4, 3)),
            dma((4, 3)),
            dma((4,)),
            dma((4,)),
            dma((2,)),
        ],
        compiler_params=pltpu.CompilerParams(
            collective_id=0, has_side_effects=True, vmem_limit_bytes=67043328
        ),
        name="layer",
    )(inputs, teacher, w, vec)


def shards(
    inputs,
    teacher,
    query_weight,
    key_weight,
    value_weight,
    out_weight,
    up_weight,
    down_weight,
    query_bias,
    value_bias,
    out_bias,
    up_bias,
    down_bias,
    first_gain,
    first_shift,
    second_gain,
    second_shift,
):
    local_rows, model = inputs.shape
    width = query_weight.shape[1]
    inner = up_weight.shape[1]
    outer = lax.axis_size("dp") // 2
    w = jnp.concatenate(
        [query_weight, key_weight, value_weight, out_weight.T, up_weight, down_weight.T], axis=1
    )
    vec = jnp.concatenate(
        [
            query_bias,
            value_bias,
            out_bias,
            up_bias,
            down_bias,
            first_gain,
            first_shift,
            second_gain,
            second_shift,
            jnp.zeros(((VECTORS - 12) * model,), F32),
        ]
    ).reshape(VECTORS, model)
    output, grad_inputs, shard, sums = layer(inputs, teacher, w, vec, outer, inner)
    token_total = local_rows * lax.axis_size("dp") * lax.axis_size("tensor")
    loss = 0.5 * jnp.sum(sums[12]) / token_total
    return (
        output,
        loss,
        grad_inputs,
        shard[:, :width],
        shard[:, width : 2 * width],
        shard[:, 2 * width : 3 * width],
        shard[:, 3 * width : 4 * width].T,
        shard[:, 4 * width : 4 * width + inner],
        shard[:, 4 * width + inner :].T,
        sums[0],
        sums[1],
        sums[2],
        sums[3:7].reshape(-1),
        sums[7],
        sums[8],
        sums[9],
        sums[10],
        sums[11],
    )


def solution(mesh):
    tokens = P(("dp", "tensor"), None)
    across, down = P("dp", "tensor"), P("tensor", "dp")
    in_specs = (tokens, tokens, across, across, across, down, across, down) + (P(),) * 9
    out_specs = (tokens, P(), tokens, across, across, across, down, across, down) + (P(),) * 9
    return jax.shard_map(shards, mesh=mesh, in_specs=in_specs, out_specs=out_specs, check_vma=False)
```

```python
import functools
import math

import jax
import jax.numpy as jnp
from jax import lax
from jax.experimental import pallas as pl
from jax.experimental.pallas import tpu as pltpu
from jax.sharding import PartitionSpec as P

HEAD_DIM = 64
SEQ = 512
EPSILON = 1e-05
MESH = pl.DeviceIdType.MESH
F32 = jnp.float32
BF16 = jnp.bfloat16
NN = ((1,), (0,))
NT = ((1,), (1,))
TN = ((0,), (0,))
CHUNK = 32
WINDOW = 3
ROOT_TWO = math.sqrt(2.0)
ROOT_TWO_PI = math.sqrt(2.0 * math.pi)
VECTORS = 16


def dot(left, right, dims):
    return lax.dot_general(left, right, (dims, ((), ())), preferred_element_type=F32)


def remote(src, dst, send, recv, peer):
    return pltpu.make_async_remote_copy(
        src_ref=src, dst_ref=dst, send_sem=send, recv_sem=recv, device_id=peer, device_id_type=MESH
    )


class Place:
    def __init__(self, outer):
        self.outer = outer
        self.dp = lax.axis_index("dp")
        self.t = lax.axis_index("tensor")
        self.z, self.x = self.dp // 2, self.dp % 2
        self.y, self.c = self.t // 2, self.t % 2
        self.x_peer = (self.z * 2 + 1 - self.x, self.t)
        self.y_peer = (self.dp, (1 - self.y) * 2 + self.c)
        self.c_peer = (self.dp, self.y * 2 + 1 - self.c)
        self.diag = (1 - self.y) * 2 + 1 - self.c
        self.diag_peer = (self.dp, self.diag)

    def z_peer(self, step):
        return (lax.rem(self.z + step, self.outer) * 2 + self.x, self.t)

    def greet(self):
        barrier = pltpu.get_barrier_semaphore()

        def one(step, carry):
            pl.semaphore_signal(barrier, inc=1, device_id=self.z_peer(step), device_id_type=MESH)
            return carry

        lax.fori_loop(1, self.outer, one, 0)
        for peer in (self.x_peer, self.y_peer, self.diag_peer, self.c_peer):
            pl.semaphore_signal(barrier, inc=1, device_id=peer, device_id_type=MESH)

    def enter(self):
        pl.semaphore_wait(pltpu.get_barrier_semaphore(), self.outer + 3)


def columns(piece, width):
    start = piece * width
    if not isinstance(start, int):
        start = pl.multiple_of(start, width)
    return pl.ds(start, width)


class Weights:
    def __init__(self, k, full, send, recv, width, pieces):
        self.k, self.full, self.send, self.recv, self.width = k, full, send, recv, width
        self.pieces = pieces

    def first(self, p, step):
        block = self.full.at[self.k.z, self.k.x, :, columns(p, self.width)]
        return remote(block, block, self.send.at[0, p], self.recv.at[0, p], self.k.z_peer(step))

    def all_first(self, p):
        block = self.full.at[pl.ds(0, self.k.outer - 1), 0, :, columns(p, self.width)]
        return remote(block, block, self.send.at[0, p], self.recv.at[0, p], self.k.x_peer)

    def second(self, p):
        block = self.full.at[:, self.k.x, :, columns(p, self.width)]
        return remote(block, block, self.send.at[1, p], self.recv.at[1, p], self.k.x_peer)

    def start(self, p):
        def one(step, carry):
            self.first(p, step).start()
            return carry

        lax.fori_loop(1, self.k.outer, one, 0)

    def forward(self, p):
        self.all_first(p).wait_recv()
        self.second(p).start()
        if p + WINDOW < self.pieces:
            self.start(p + WINDOW)

    def arrive(self, p):
        self.second(p).wait_recv()

    def drain(self, pieces):
        def piece(p, carry):
            self.all_first(p).wait_send()
            self.second(p).wait_send()
            return carry

        lax.fori_loop(0, pieces, piece, 0)


class Gradients:
    def __init__(self, k, part, near, far, out, send, recv, width):
        self.k, self.part, self.near, self.far, self.out = k, part, near, far, out
        self.send, self.recv, self.width = send, recv, width

    def one(self, p):
        k, cols = self.k, columns(p, self.width)
        return remote(
            self.part.at[:, 1 - k.x, :, cols],
            self.near.at[:, :, cols],
            self.send.at[0, p],
            self.recv.at[0, p],
            k.x_peer,
        )

    def two(self, p, step):
        k, cols = self.k, columns(p, self.width)
        return remote(
            self.part.at[lax.rem(k.z + step, k.outer), k.x, :, cols],
            self.far.at[step - 1, :, cols],
            self.send.at[1, p],
            self.recv.at[1, p],
            k.z_peer(step),
        )

    def all_two(self, p):
        block = self.far.at[:, :, columns(p, self.width)]
        return remote(block, block, self.send.at[1, p], self.recv.at[1, p], self.k.x_peer)

    def start(self, p):
        self.one(p).start()

    def forward(self, p):
        k, cols = self.k, columns(p, self.width)
        self.one(p).wait_recv()
        here = self.part[:, k.x, :, cols].astype(F32)
        self.part[:, k.x, :, cols] = (here + self.near[:, :, cols].astype(F32)).astype(BF16)

        def send(step, carry):
            self.two(p, step).start()
            return carry

        lax.fori_loop(1, k.outer, send, 0)

    def finish(self, p):
        k, cols = self.k, columns(p, self.width)
        self.all_two(p).wait_recv()

        def add(i, total):
            return total + self.far[i, :, cols].astype(F32)

        total = self.part[k.z, k.x, :, cols].astype(F32)
        total = lax.fori_loop(0, k.outer - 1, add, total)
        self.out(p, total)

    def drain(self, pieces):
        def piece(p, carry):
            self.one(p).wait_send()
            self.all_two(p).wait_send()
            return carry

        lax.fori_loop(0, pieces, piece, 0)


class Spread:
    def __init__(self, k, blocks, send, recv, phase):
        self.k, self.blocks, self.send, self.recv, self.phase = k, blocks, send, recv, phase

    def copy(self, number, block, peer):
        ref = self.blocks.at[block]
        return remote(
            ref, ref, self.send.at[self.phase, number], self.recv.at[self.phase, number], peer
        )

    def near(self):
        return self.copy(0, self.k.t, self.k.c_peer)

    def far(self):
        return self.copy(1, self.k.t, self.k.diag_peer)

    def relay(self):
        return self.copy(2, self.k.diag, self.k.c_peer)

    def start(self):
        self.far().start()
        self.near().start()

    def own(self):
        self.near().wait_recv()

    def pass_on(self):
        self.far().wait_recv()
        self.relay().start()

    def other(self):
        self.relay().wait_recv()

    def drain(self):
        self.near().wait_send()
        self.far().wait_send()
        self.relay().wait_send()


class Reduce:
    def __init__(self, k, out, inbox, keep, send, recv, phase):
        self.k, self.out, self.inbox, self.keep = k, out, inbox, keep
        self.send, self.recv, self.phase = send, recv, phase

    def copy(self, number, phase=None):
        peer = self.k.y_peer if number == 2 else self.k.c_peer
        phase = self.phase if phase is None else phase
        return remote(
            self.out.at[number],
            self.inbox.at[number],
            self.send.at[phase, number],
            self.recv.at[phase, number],
            peer,
        )

    def free(self, number):
        if self.phase > 0:
            self.copy(number, self.phase - 1).wait_send()

    def across(self, value):
        self.free(0)
        self.out[0] = value.astype(BF16)
        self.copy(0).start()

    def theirs(self, value):
        self.free(2)
        self.copy(0).wait_recv()
        self.out[2] = (value + self.inbox[0].astype(F32)).astype(BF16)
        self.copy(2).start()

    def partner(self, value):
        self.free(1)
        self.out[1] = value.astype(BF16)
        self.copy(1).start()

    def mine(self, value):
        self.keep[...] = value

    def wait(self):
        self.copy(1).wait_recv()
        self.copy(2).wait_recv()

    def total(self, rows):
        return self.keep[rows, :] + (
            self.inbox[1, rows, :].astype(F32) + self.inbox[2, rows, :].astype(F32)
        )

    def drain(self):
        for number in range(3):
            self.copy(number).wait_send()


def fold(values):
    rows, width = values.shape
    return jnp.sum(values.reshape(rows // 8, 8, width), axis=0)


def mean(values):
    return jnp.sum(values, axis=-1, keepdims=True) * (1.0 / values.shape[-1])


def body(
    outer,
    x_in,
    teacher_in,
    qw_in,
    kw_in,
    vw_in,
    ow_in,
    uw_in,
    dw_in,
    qb_in,
    vb_in,
    ob_in,
    ub_in,
    db_in,
    g1_in,
    b1_in,
    g2_in,
    b2_in,
    out_ref,
    gin_ref,
    gq_ref,
    gk_ref,
    gv_ref,
    go_ref,
    gu_ref,
    gd_ref,
    gvec_ref,
    W,
    G,
    near,
    far,
    X,
    H,
    MX,
    GF,
    Q,
    K,
    V,
    C,
    GC,
    DQKV,
    PT,
    SL,
    ACT,
    GU,
    OWN,
    HID,
    N1,
    R1,
    GS,
    SUMS,
    ACC,
    OUTBOX,
    INBOX,
    VA,
    VR,
    VZ,
    TEACH,
    OT,
    DT,
    VEC,
    w_send,
    w_recv,
    g_send,
    g_recv,
    s_send,
    s_recv,
    r_send,
    r_recv,
    v_send,
    v_recv,
    load_sem,
):
    k = Place(outer)
    rows, model = x_in.shape
    width = Q.shape[2]
    inner = ACT.shape[2]
    heads = width // HEAD_DIM
    steps = inner // width
    up_piece = 4
    down_piece = 4 + steps
    pieces = 4 + 2 * steps
    scale = 1.0 / math.sqrt(HEAD_DIM)
    mine, theirs = k.y, 1 - k.y

    own = W.at[k.z, k.x]
    loads = []

    def load(src, dst):
        copy = pltpu.make_async_copy(src, dst, load_sem.at[len(loads)])
        copy.start()
        loads.append(copy)

    load(x_in, X.at[k.t])
    load(qw_in, own.at[:, columns(0, width)])
    load(kw_in, own.at[:, columns(1, width)])
    load(vw_in, own.at[:, columns(2, width)])
    load(ow_in, OT)
    load(uw_in, own.at[:, pl.ds(4 * width, inner)])
    load(dw_in, DT)
    load(teacher_in, TEACH)
    for row, ref in enumerate((qb_in, vb_in, ob_in, db_in, g1_in, b1_in, g2_in, b2_in)):
        load(ref, VEC.at[pl.ds(row, 1), pl.ds(0, model)])
    load(ub_in, VEC.at[pl.ds(8, 1), :])
    k.greet()

    weights = Weights(k, W, w_send, w_recv, width, pieces)

    def keep(p, total):
        if p < 3:
            (gq_ref, gk_ref, gv_ref)[p][...] = total
        elif p == 3:
            go_ref[...] = total.T
        elif p < down_piece:
            gu_ref[:, (p - up_piece) * width : (p - up_piece + 1) * width] = total
        else:
            gd_ref[(p - down_piece) * width : (p - down_piece + 1) * width, :] = total.T

    grads = Gradients(k, G, near, far, keep, g_send, g_recv, width)

    def spread(blocks, phase):
        return Spread(k, blocks, s_send, s_recv, phase)

    def reduce(phase):
        return Reduce(k, OUTBOX, INBOX, OWN, r_send, r_recv, phase)

    def matrix(start, size):
        return W[:, :, :, pl.ds(start, size)].reshape(model, size)

    def vector(row):
        return VEC[row : row + 1, 0:model]

    def pair(blocks, seq):
        return blocks[pl.ds(2 * seq, 2)].reshape(2 * rows, model)

    def part_rows(core):
        return pl.ds(pl.multiple_of(core * rows, rows), rows)

    def norm_loop(step):
        def one(i, carry):
            step(pl.ds(pl.multiple_of(i * CHUNK, CHUNK), CHUNK))
            return carry

        lax.fori_loop(0, rows // CHUNK, one, 0)

    SUMS[...] = jnp.zeros_like(SUMS)
    VA[0] = jnp.zeros_like(VA[0])
    for copy in loads:
        copy.wait()
    own[:, columns(3, width)] = OT[...].T
    own[:, pl.ds(4 * width + inner, inner)] = DT[...].T
    s0 = spread(X, 0)
    k.enter()
    s0.start()
    for p in range(WINDOW):
        weights.start(p)

    def project(p, held):
        weights.arrive(p)
        for seq in range(2):
            tokens = X[2 * seq : 2 * seq + 2].reshape(2 * rows, model)
            product = dot(tokens, matrix(p * width, width), NN)
            if p != 1:
                here = pl.ds(pl.multiple_of(k.t * width, width), width)
                product = product + VEC[p // 2 : p // 2 + 1, here]
            held[seq] = product.astype(BF16)

    def head_mask(h):
        lane = lax.broadcasted_iota(jnp.int32, (1, width), 1)
        inside = (lane >= h * HEAD_DIM) & (lane < (h + 1) * HEAD_DIM)
        return jnp.where(inside, 1.0, 0.0).astype(BF16)

    def attend(seq):
        ACC[0] = jnp.zeros_like(ACC[0])

        def head(h, carry):
            mask = head_mask(h)
            scores = dot(K[seq], Q[seq] * mask, NT) * scale
            raised = jnp.exp(scores - jnp.max(scores, axis=0, keepdims=True))
            probs = (raised * (1.0 / jnp.sum(raised, axis=0, keepdims=True))).astype(BF16)
            PT[seq, h] = probs
            ACC[0] += dot(probs, V[seq] * mask, TN)
            return carry

        lax.fori_loop(0, heads, head, 0)
        C[seq] = ACC[0].astype(BF16)

    def out_block(seq, core):
        return dot(C[seq, part_rows(core), :], matrix(3 * width, width), NT)

    weights.forward(0)
    weights.forward(1)
    s0.pass_on()
    s0.own()
    s0.other()
    project(0, Q)
    weights.forward(2)
    project(1, K)
    weights.forward(3)
    project(2, V)
    r0 = reduce(0)
    attend(theirs)
    weights.forward(4)
    weights.arrive(3)
    r0.across(out_block(theirs, 1 - k.c))
    r0.theirs(out_block(theirs, k.c))
    attend(mine)
    weights.forward(5)
    r0.partner(out_block(mine, 1 - k.c))
    r0.mine(out_block(mine, k.c))
    weights.forward(6)
    r0.wait()

    def first_norm(r):
        first = X[k.t, r, :].astype(F32) + r0.total(r) + vector(2)
        center = first - mean(first)
        scaling = lax.rsqrt(mean(center * center) + EPSILON)
        normed = center * scaling
        hidden = normed * vector(4) + vector(5)
        N1[r, :] = normed
        R1[r, :] = jnp.broadcast_to(scaling, (CHUNK, R1.shape[1]))
        HID[r, :] = hidden
        H[k.t, r, :] = hidden.astype(BF16)

    norm_loop(first_norm)
    s1 = spread(H, 1)
    s1.start()
    weights.forward(7)
    weights.forward(8)
    s1.own()
    for p in range(up_piece, down_piece):
        weights.arrive(p)

    def up(seq):
        def part(n, carry):
            cols = pl.ds(pl.multiple_of(n * width, width), width)
            wide = pl.ds(pl.multiple_of((up_piece + n) * width, width), width)
            upper = dot(pair(H, seq), W[:, :, :, wide].reshape(model, width), NN)
            upper = upper + VEC[8:9, pl.ds(pl.multiple_of(k.t * inner + n * width, width), width)]
            erf_part = 1.0 + lax.erf(upper * (1.0 / ROOT_TWO))
            ACT[seq, :, cols] = (0.5 * upper * erf_part).astype(BF16)
            SL[seq, :, cols] = 0.5 * erf_part + upper * jnp.exp(-0.5 * upper * upper) * (
                1.0 / ROOT_TWO_PI
            )
            return carry

        lax.fori_loop(0, steps, part, 0)

    def down_block(seq, core):
        return dot(ACT[seq, part_rows(core), :], matrix(down_piece * width, inner), NT)

    up(mine)
    weights.forward(9)
    s1.pass_on()
    s1.other()
    up(theirs)
    weights.forward(10)
    weights.forward(11)
    for p in range(down_piece, pieces):
        weights.arrive(p)
    r1 = reduce(1)
    r1.across(down_block(theirs, 1 - k.c))
    r1.theirs(down_block(theirs, k.c))
    r1.partner(down_block(mine, 1 - k.c))
    r1.mine(down_block(mine, k.c))
    r1.wait()

    def norm_back(d, gain, normed, scaling):
        e = d * gain
        return scaling * (e - mean(e) - normed * mean(e * normed))

    def second_norm(r):
        second = HID[r, :] + r1.total(r) + vector(3)
        center = second - mean(second)
        scaling = lax.rsqrt(mean(center * center) + EPSILON)
        normed = center * scaling
        result = normed * vector(6) + vector(7)
        out_ref[r, :] = result.astype(BF16)
        diff = result - TEACH[r, :].astype(F32)
        grad = norm_back(diff, vector(6), normed, scaling)
        GS[r, :] = grad
        MX[k.t, r, :] = grad.astype(BF16)
        SUMS[0] += fold(grad)
        SUMS[1] += fold(diff * normed)
        SUMS[2] += fold(diff)
        SUMS[3] += fold(diff * diff)

    norm_loop(second_norm)
    s2 = spread(MX, 2)
    s2.start()
    s2.own()

    def back_up(seq):
        def part(n, carry):
            cols = pl.ds(pl.multiple_of(n * width, width), width)
            wide = pl.ds(pl.multiple_of((down_piece + n) * width, width), width)
            grad = dot(pair(MX, seq), W[:, :, :, wide].reshape(model, width), NN)
            grad = (grad * SL[seq, :, cols]).astype(BF16)
            GU[seq, :, cols] = grad
            SUMS[7, :, cols] += fold(grad.astype(F32))
            return carry

        lax.fori_loop(0, steps, part, 0)

    def hidden_block(seq, core):
        return dot(GU[seq, part_rows(core), :], matrix(up_piece * width, inner), NT)

    def weight_grad(left, right, first, begin, end):
        def piece(n, carry):
            cols = pl.ds(pl.multiple_of(n * width, width), width)
            tokens = 4 * rows
            grad = dot(
                left[...].reshape(tokens, model), right[:, :, cols].reshape(tokens, width), TN
            )
            wide = pl.ds(pl.multiple_of((first + n) * width, width), width)
            G[:, :, :, wide] = grad.astype(BF16).reshape(outer, 2, model // (2 * outer), width)

            @pl.when(n > begin)
            def _():
                grads.start(first + n - 1)

            return carry

        lax.fori_loop(begin, end, piece, 0)

    r2 = reduce(2)
    back_up(mine)
    r2.partner(hidden_block(mine, 1 - k.c))
    r2.mine(hidden_block(mine, k.c))
    s2.pass_on()
    s2.other()
    weight_grad(MX, ACT, down_piece, 0, 2)
    back_up(theirs)
    grads.start(down_piece + 1)
    r2.across(hidden_block(theirs, 1 - k.c))
    r2.theirs(hidden_block(theirs, k.c))
    weight_grad(MX, ACT, down_piece, 2, steps)
    grads.forward(8)
    grads.start(down_piece + steps - 1)
    weight_grad(H, GU, up_piece, 0, steps)
    grads.start(up_piece + steps - 1)
    grads.forward(9)
    grads.forward(10)
    r2.wait()

    def first_back(r):
        grad_hidden = GS[r, :] + r2.total(r)
        normed = N1[r, :]
        grad = norm_back(grad_hidden, vector(4), normed, R1[r, :][:, :1])
        GS[r, :] = grad
        GF[k.t, r, :] = grad.astype(BF16)
        SUMS[4] += fold(grad)
        SUMS[5] += fold(grad_hidden * normed)
        SUMS[6] += fold(grad_hidden)

    norm_loop(first_back)
    s3 = spread(GF, 3)
    s3.start()
    s3.own()

    def attend_back(seq):
        GC[...] = dot(pair(GF, seq), matrix(3 * width, width), NN).astype(BF16)
        ACC[...] = jnp.zeros_like(ACC)

        def head(h, carry):
            mask = head_mask(h)
            context = GC[...] * mask
            low = PT[seq, h]
            ACC[2] += dot(low, context, NN)
            probs = low.astype(F32)
            grad = dot(V[seq], context, NT)
            across = jnp.sum(probs * grad, axis=0, keepdims=True)
            grad = (probs * (grad - across)).astype(BF16)
            ACC[1] += dot(grad, Q[seq] * mask, NN)
            ACC[0] += dot(grad, K[seq] * mask, TN)
            return carry

        lax.fori_loop(0, heads, head, 0)
        for n in range(3):
            grad = ACC[n] if n == 2 else ACC[n] * scale
            DQKV[seq, :, n * width : (n + 1) * width] = grad.astype(BF16)

    def input_block(seq, core):
        return dot(DQKV[seq, part_rows(core), :], matrix(0, 3 * width), NT)

    attend_back(mine)
    grads.forward(11)
    s3.pass_on()
    grads.forward(4)
    s3.other()
    weight_grad(GF, C, 3, 0, 1)
    grads.forward(5)
    attend_back(theirs)
    grads.start(3)

    here = pl.ds(pl.multiple_of(k.t * width, width), width)
    for row, n in ((0, 0), (1, 2)):
        grad = DQKV[:, :, n * width : (n + 1) * width].reshape(4 * rows, width).astype(F32)
        VA[0, row : row + 1, here] = jnp.sum(grad, axis=0, keepdims=True)
    VA[0, pl.ds(3 + k.t, 1), :] = jnp.sum(SUMS[7], axis=0, keepdims=True)
    for row, n in ((7, 0), (10, 1), (11, 2), (12, 3), (2, 4), (8, 5), (9, 6)):
        VA[0, row : row + 1, :] = jnp.sum(SUMS[n], axis=0, keepdims=True)

    def vector_hop(n, peer):
        return remote(VA.at[n], VR.at[n], v_send.at[n], v_recv.at[n], peer)

    def vector_last(step):
        return remote(VA.at[3], VZ.at[k.z], v_send.at[3], v_recv.at[3], k.z_peer(step))

    hops = [vector_hop(n, peer) for n, peer in enumerate((k.c_peer, k.y_peer, k.x_peer))]

    def hop_in(n):
        hops[n].wait_recv()
        VA[n + 1] = VA[n] + VR[n]

    weight_grad(X, DQKV, 0, 0, 1)
    hops[0].start()
    weight_grad(X, DQKV, 0, 1, 2)
    grads.start(0)
    hop_in(0)
    hops[1].start()
    weight_grad(X, DQKV, 0, 2, 3)
    grads.start(1)
    grads.forward(6)
    r3 = reduce(3)
    r3.across(input_block(theirs, 1 - k.c))
    r3.theirs(input_block(theirs, k.c))
    hop_in(1)
    hops[2].start()
    grads.start(2)
    grads.forward(7)
    r3.partner(input_block(mine, 1 - k.c))
    r3.mine(input_block(mine, k.c))
    for p in (8, 9, 10):
        grads.finish(p)
    grads.forward(3)
    grads.forward(0)
    grads.forward(1)
    hop_in(2)
    VZ[k.z] = VA[3]

    def send_last(step, carry):
        vector_last(step).start()
        return carry

    lax.fori_loop(1, outer, send_last, 0)
    grads.forward(2)
    r3.wait()

    def last(r):
        gin_ref[r, :] = GS[r, :] + r3.total(r)

    norm_loop(last)
    for p in (11, 4, 5, 6, 7, 3, 0, 1):
        grads.finish(p)
    vz_all = VZ.at[pl.ds(0, outer - 1)]
    every = remote(vz_all, vz_all, v_send.at[3], v_recv.at[3], k.x_peer)
    every.wait_recv()

    def add(i, total):
        return total + VZ[i]

    gvec_ref[...] = lax.fori_loop(1, outer, add, VZ[0])
    grads.finish(2)

    weights.drain(pieces)
    grads.drain(pieces)
    for s in (s0, s1, s2, s3):
        s.drain()
    r3.drain()
    for hop in hops:
        hop.wait_send()
    every.wait_send()


def layer(outer, arrays):
    inputs, query_weight, up_weight = arrays[0], arrays[2], arrays[6]
    rows, model = inputs.shape
    shard_rows, width = query_weight.shape
    inner = up_weight.shape[1]
    heads = width // HEAD_DIM
    columns_all = 4 * width + 2 * inner
    pieces = columns_all // width
    seq = 2 * rows
    vmem = pl.BlockSpec(memory_space=pltpu.VMEM)
    anywhere = pl.BlockSpec(memory_space=pl.ANY)
    full = (outer, 2, shard_rows, columns_all)
    dma = pltpu.SemaphoreType.DMA
    outs = (
        jax.ShapeDtypeStruct((rows, model), BF16),
        jax.ShapeDtypeStruct((rows, model), F32),
        jax.ShapeDtypeStruct((shard_rows, width), F32),
        jax.ShapeDtypeStruct((shard_rows, width), F32),
        jax.ShapeDtypeStruct((shard_rows, width), F32),
        jax.ShapeDtypeStruct((width, shard_rows), F32),
        jax.ShapeDtypeStruct((shard_rows, inner), F32),
        jax.ShapeDtypeStruct((inner, shard_rows), F32),
        jax.ShapeDtypeStruct((VECTORS, model), F32),
    )
    return pl.pallas_call(
        functools.partial(body, outer),
        out_shape=outs,
        in_specs=[anywhere] * len(arrays),
        out_specs=(vmem,) * len(outs),
        scratch_shapes=[
            pltpu.VMEM(full, BF16),
            pltpu.VMEM(full, BF16),
            pltpu.VMEM((outer, shard_rows, columns_all), BF16),
            pltpu.VMEM((outer - 1, shard_rows, columns_all), BF16),
            pltpu.VMEM((4, rows, model), BF16),
            pltpu.VMEM((4, rows, model), BF16),
            pltpu.VMEM((4, rows, model), BF16),
            pltpu.VMEM((4, rows, model), BF16),
            pltpu.VMEM((2, seq, width), BF16),
            pltpu.VMEM((2, seq, width), BF16),
            pltpu.VMEM((2, seq, width), BF16),
            pltpu.VMEM((2, seq, width), BF16),
            pltpu.VMEM((seq, width), BF16),
            pltpu.VMEM((2, seq, 3 * width), BF16),
            pltpu.VMEM((2, heads, seq, seq), BF16),
            pltpu.VMEM((2, seq, inner), F32),
            pltpu.VMEM((2, seq, inner), BF16),
            pltpu.VMEM((2, seq, inner), BF16),
            pltpu.VMEM((rows, model), F32),
            pltpu.VMEM((rows, model), F32),
            pltpu.VMEM((rows, model), F32),
            pltpu.VMEM((rows, 128), F32),
            pltpu.VMEM((rows, model), F32),
            pltpu.VMEM((8, 8, model), F32),
            pltpu.VMEM((3, seq, width), F32),
            pltpu.VMEM((3, rows, model), BF16),
            pltpu.VMEM((3, rows, model), BF16),
            pltpu.VMEM((4, VECTORS, model), F32),
            pltpu.VMEM((3, VECTORS, model), F32),
            pltpu.VMEM((outer, VECTORS, model), F32),
            pltpu.VMEM((rows, model), BF16),
            pltpu.VMEM((width, shard_rows), BF16),
            pltpu.VMEM((inner, shard_rows), BF16),
            pltpu.VMEM((9, 4 * inner), F32),
            dma((2, pieces)),
            dma((2, pieces)),
            dma((2, pieces)),
            dma((2, pieces)),
            dma((4, 3)),
            dma((4, 3)),
            dma((4, 3)),
            dma((4, 3)),
            dma((4,)),
            dma((4,)),
            dma((len(arrays),)),
        ],
        compiler_params=pltpu.CompilerParams(
            collective_id=0, has_side_effects=True, vmem_limit_bytes=67043328
        ),
        name="layer",
    )(*arrays)


def write_body(count, *refs):
    ins, outs, sem = refs[:9], refs[9 : 9 + count], refs[-1]
    vec = ins[8]
    pairs = list(zip(ins[:8], outs[:8]))
    single = [(0, 8), (1, 9), (2, 10), (7, 12), (8, 13), (9, 14), (10, 15), (11, 16), (12, 17)]
    pairs += [(vec.at[pl.ds(row, 1), :], outs[place]) for row, place in single]
    model = vec.shape[1]
    parts = outs[11].shape[1] // model
    for n in range(parts):
        pairs.append((vec.at[pl.ds(3 + n, 1), :], outs[11].at[:, pl.ds(n * model, model)]))
    copies = [pltpu.make_async_copy(src, dst, sem.at[n]) for n, (src, dst) in enumerate(pairs)]
    for copy in copies:
        copy.start()
    for copy in copies:
        copy.wait()


def write(values, up_length):
    model = values[8].shape[1]
    line = jax.ShapeDtypeStruct((1, model), F32)
    outs = [jax.ShapeDtypeStruct(v.shape, v.dtype) for v in values[:8]] + [line] * 10
    outs[11] = jax.ShapeDtypeStruct((1, up_length), F32)
    copies = 17 + up_length // model
    return pl.pallas_call(
        functools.partial(write_body, len(outs)),
        out_shape=tuple(outs),
        in_specs=[pl.BlockSpec(memory_space=pltpu.VMEM)] * len(values),
        out_specs=(pl.BlockSpec(memory_space=pl.ANY),) * len(outs),
        scratch_shapes=[pltpu.SemaphoreType.DMA((copies,))],
        name="write",
    )(*values)


def shards(*arrays):
    inputs = arrays[0]
    outer = lax.axis_size("dp") // 2
    arrays = arrays[:8] + tuple(v.reshape(1, -1) for v in arrays[8:])
    up_length = arrays[11].shape[1]
    values = write(layer(outer, arrays), up_length)
    token_total = inputs.shape[0] * lax.axis_size("dp") * lax.axis_size("tensor")
    loss = jnp.sum(values[17]) * (0.5 / token_total)
    output, grad_inputs, gq, gk, gv, go, gu, gd = values[:8]
    return (output, loss, grad_inputs, gq, gk, gv, go, gu, gd) + tuple(
        v.reshape(-1) for v in values[8:17]
    )


def solution(mesh):
    tokens = P(("dp", "tensor"), None)
    across, down = P("dp", "tensor"), P("tensor", "dp")
    in_specs = (tokens, tokens, across, across, across, down, across, down) + (P(),) * 9
    out_specs = (tokens, P(), tokens, across, across, across, down, across, down) + (P(),) * 9
    return jax.shard_map(shards, mesh=mesh, in_specs=in_specs, out_specs=out_specs, check_vma=False)
```

```python
import functools
import math

import jax
import jax.numpy as jnp
from jax import lax
from jax.experimental import pallas as pl
from jax.experimental.pallas import tpu as pltpu
from jax.sharding import PartitionSpec as P

HEAD_DIM = 64
SEQ = 512
EPSILON = 1e-05
MESH = pl.DeviceIdType.MESH
F32 = jnp.float32
BF16 = jnp.bfloat16
NN = ((1,), (0,))
NT = ((1,), (1,))
TN = ((0,), (0,))
CHUNK = 32
WINDOW = 3
ROOT_TWO = math.sqrt(2.0)
ROOT_TWO_PI = math.sqrt(2.0 * math.pi)
VECTORS = 16


def dot(left, right, dims):
    return lax.dot_general(left, right, (dims, ((), ())), preferred_element_type=F32)


def remote(src, dst, send, recv, peer):
    return pltpu.make_async_remote_copy(
        src_ref=src, dst_ref=dst, send_sem=send, recv_sem=recv, device_id=peer, device_id_type=MESH
    )


class Place:
    def __init__(self, outer):
        self.outer = outer
        self.dp = lax.axis_index("dp")
        self.t = lax.axis_index("tensor")
        self.z, self.x = self.dp // 2, self.dp % 2
        self.y, self.c = self.t // 2, self.t % 2
        self.x_peer = (self.z * 2 + 1 - self.x, self.t)
        self.y_peer = (self.dp, (1 - self.y) * 2 + self.c)
        self.c_peer = (self.dp, self.y * 2 + 1 - self.c)
        self.diag = (1 - self.y) * 2 + 1 - self.c
        self.diag_peer = (self.dp, self.diag)

    def z_peer(self, step):
        return (lax.rem(self.z + step, self.outer) * 2 + self.x, self.t)

    def greet(self):
        barrier = pltpu.get_barrier_semaphore()

        def one(step, carry):
            pl.semaphore_signal(barrier, inc=1, device_id=self.z_peer(step), device_id_type=MESH)
            return carry

        lax.fori_loop(1, self.outer, one, 0)
        for peer in (self.x_peer, self.y_peer, self.diag_peer, self.c_peer):
            pl.semaphore_signal(barrier, inc=1, device_id=peer, device_id_type=MESH)

    def enter(self):
        pl.semaphore_wait(pltpu.get_barrier_semaphore(), self.outer + 3)


def columns(piece, width):
    start = piece * width
    if not isinstance(start, int):
        start = pl.multiple_of(start, width)
    return pl.ds(start, width)


class Weights:
    def __init__(self, k, full, send, recv, width, pieces):
        self.k, self.full, self.send, self.recv, self.width = k, full, send, recv, width
        self.pieces = pieces

    def first(self, p, step):
        block = self.full.at[self.k.z, self.k.x, :, columns(p, self.width)]
        return remote(block, block, self.send.at[0, p], self.recv.at[0, p], self.k.z_peer(step))

    def all_first(self, p):
        block = self.full.at[pl.ds(0, self.k.outer - 1), 0, :, columns(p, self.width)]
        return remote(block, block, self.send.at[0, p], self.recv.at[0, p], self.k.x_peer)

    def second(self, p):
        block = self.full.at[:, self.k.x, :, columns(p, self.width)]
        return remote(block, block, self.send.at[1, p], self.recv.at[1, p], self.k.x_peer)

    def start(self, p):
        def one(step, carry):
            self.first(p, step).start()
            return carry

        lax.fori_loop(1, self.k.outer, one, 0)

    def forward(self, p):
        self.all_first(p).wait_recv()
        self.second(p).start()
        if p + WINDOW < self.pieces:
            self.start(p + WINDOW)

    def arrive(self, p):
        self.second(p).wait_recv()

    def drain(self, pieces):
        def piece(p, carry):
            self.all_first(p).wait_send()
            self.second(p).wait_send()
            return carry

        lax.fori_loop(0, pieces, piece, 0)


class Gradients:
    def __init__(self, k, part, near, far, out, send, recv, width):
        self.k, self.part, self.near, self.far, self.out = k, part, near, far, out
        self.send, self.recv, self.width = send, recv, width

    def one(self, p):
        k, cols = self.k, columns(p, self.width)
        return remote(
            self.part.at[:, 1 - k.x, :, cols],
            self.near.at[:, :, cols],
            self.send.at[0, p],
            self.recv.at[0, p],
            k.x_peer,
        )

    def two(self, p, step):
        k, cols = self.k, columns(p, self.width)
        return remote(
            self.part.at[lax.rem(k.z + step, k.outer), k.x, :, cols],
            self.far.at[step - 1, :, cols],
            self.send.at[1, p],
            self.recv.at[1, p],
            k.z_peer(step),
        )

    def all_two(self, p):
        block = self.far.at[:, :, columns(p, self.width)]
        return remote(block, block, self.send.at[1, p], self.recv.at[1, p], self.k.x_peer)

    def start(self, p):
        self.one(p).start()

    def forward(self, p):
        k, cols = self.k, columns(p, self.width)
        self.one(p).wait_recv()
        here = self.part[:, k.x, :, cols].astype(F32)
        self.part[:, k.x, :, cols] = (here + self.near[:, :, cols].astype(F32)).astype(BF16)

        def send(step, carry):
            self.two(p, step).start()
            return carry

        lax.fori_loop(1, k.outer, send, 0)

    def finish(self, p):
        k, cols = self.k, columns(p, self.width)
        self.all_two(p).wait_recv()

        def add(i, total):
            return total + self.far[i, :, cols].astype(F32)

        total = self.part[k.z, k.x, :, cols].astype(F32)
        total = lax.fori_loop(0, k.outer - 1, add, total)
        self.out(p, total)

    def drain(self, pieces):
        def piece(p, carry):
            self.one(p).wait_send()
            self.all_two(p).wait_send()
            return carry

        lax.fori_loop(0, pieces, piece, 0)


class Spread:
    def __init__(self, k, blocks, send, recv, phase):
        self.k, self.blocks, self.send, self.recv, self.phase = k, blocks, send, recv, phase

    def copy(self, number, block, peer):
        ref = self.blocks.at[block]
        return remote(
            ref, ref, self.send.at[self.phase, number], self.recv.at[self.phase, number], peer
        )

    def near(self):
        return self.copy(0, self.k.t, self.k.c_peer)

    def far(self):
        return self.copy(1, self.k.t, self.k.diag_peer)

    def relay(self):
        return self.copy(2, self.k.diag, self.k.c_peer)

    def start(self):
        self.far().start()
        self.near().start()

    def own(self):
        self.near().wait_recv()

    def pass_on(self):
        self.far().wait_recv()
        self.relay().start()

    def other(self):
        self.relay().wait_recv()

    def drain(self):
        self.near().wait_send()
        self.far().wait_send()
        self.relay().wait_send()


class SpreadColumns(Spread):
    def __init__(self, k, blocks, send, recv, phase, chunks, far_sems):
        super().__init__(k, blocks, send, recv, phase)
        self.chunks = chunks
        self.far_send, self.far_recv, self.relay_send, self.relay_recv = far_sems

    def cols(self, chunk):
        width = self.blocks.shape[2] // self.chunks
        return pl.ds(pl.multiple_of(chunk * width, width), width)

    def far_part(self, n, chunk):
        ref = self.blocks.at[self.k.t, :, self.cols(chunk)]
        return remote(ref, ref, self.far_send.at[n], self.far_recv.at[n], self.k.diag_peer)

    def relay_part(self, n, chunk):
        ref = self.blocks.at[self.k.diag, :, self.cols(chunk)]
        return remote(ref, ref, self.relay_send.at[n], self.relay_recv.at[n], self.k.c_peer)

    def start_columns(self, order):
        self.near().start()
        for n, chunk in enumerate(order):
            self.far_part(n, chunk).start()

    def pass_part(self, n, chunk):
        self.far_part(n, chunk).wait_recv()
        self.relay_part(n, chunk).start()

    def other_part(self, n, chunk):
        self.relay_part(n, chunk).wait_recv()

    def drain_columns(self, order):
        self.near().wait_send()
        for n, chunk in enumerate(order):
            self.far_part(n, chunk).wait_send()
            self.relay_part(n, chunk).wait_send()


class Reduce:
    def __init__(self, k, out, inbox, keep, send, recv, phase):
        self.k, self.out, self.inbox, self.keep = k, out, inbox, keep
        self.send, self.recv, self.phase = send, recv, phase

    def copy(self, number, phase=None):
        peer = self.k.y_peer if number == 2 else self.k.c_peer
        phase = self.phase if phase is None else phase
        return remote(
            self.out.at[number],
            self.inbox.at[number],
            self.send.at[phase, number],
            self.recv.at[phase, number],
            peer,
        )

    phase_free = True

    def free(self, number):
        if self.phase > 0 and self.phase_free:
            self.copy(number, self.phase - 1).wait_send()

    def across(self, value):
        self.free(0)
        self.out[0] = value.astype(BF16)
        self.copy(0).start()

    def theirs(self, value):
        self.free(2)
        self.copy(0).wait_recv()
        self.out[2] = (value + self.inbox[0].astype(F32)).astype(BF16)
        self.copy(2).start()

    def partner(self, value):
        self.free(1)
        self.out[1] = value.astype(BF16)
        self.copy(1).start()

    def mine(self, value):
        self.keep[...] = value

    def wait(self):
        self.copy(1).wait_recv()
        self.copy(2).wait_recv()

    def total(self, rows):
        return self.keep[rows, :] + (
            self.inbox[1, rows, :].astype(F32) + self.inbox[2, rows, :].astype(F32)
        )

    def drain(self):
        for number in range(3):
            self.copy(number).wait_send()


class ReduceColumns(Reduce):
    def __init__(self, k, out, inbox, keep, send, recv, phase, chunks, sems):
        super().__init__(k, out, inbox, keep, send, recv, phase)
        self.chunks, self.part_send, self.part_recv = chunks, sems[0], sems[1]

    def cols(self, chunk):
        width = self.keep.shape[1] // self.chunks
        return pl.ds(pl.multiple_of(chunk * width, width), width)

    def part(self, number, n, chunk):
        cols = self.cols(chunk)
        return remote(
            self.out.at[number, :, cols],
            self.inbox.at[number, :, cols],
            self.part_send.at[number, n],
            self.part_recv.at[number, n],
            self.k.y_peer if number == 2 else self.k.c_peer,
        )

    def step(self, n, chunk, block):
        cols = self.cols(chunk)
        if n == 0:
            for number in range(3):
                self.free(number)
        self.out[0, :, cols] = block("across").astype(BF16)
        self.part(0, n, chunk).start()
        self.out[1, :, cols] = block("partner").astype(BF16)
        self.part(1, n, chunk).start()
        value = block("theirs")
        self.part(0, n, chunk).wait_recv()
        self.out[2, :, cols] = (value + self.inbox[0, :, cols].astype(F32)).astype(BF16)
        self.part(2, n, chunk).start()
        self.keep[:, cols] = block("mine")

    def wait_columns(self, order):
        for n, chunk in enumerate(order):
            self.part(1, n, chunk).wait_recv()
            self.part(2, n, chunk).wait_recv()

    def drain_columns(self, order):
        for n, chunk in enumerate(order):
            for number in range(3):
                self.part(number, n, chunk).wait_send()


class DownWeights:
    HALVES = 2

    def __init__(self, k, full, start, size, sems):
        self.k, self.full, self.start_at, self.half = k, full, start, size // self.HALVES
        self.z_send, self.z_recv, self.x_send, self.x_recv = sems

    def shard(self, step, x, half):
        z = lax.rem(self.k.z - step + self.k.outer, self.k.outer)
        return self.full.at[z, x, :, pl.ds(self.start_at + half * self.half, self.half)]

    def first(self, step, half):
        block = self.shard(0, self.k.x, half)
        sems = (self.z_send.at[step, half], self.z_recv.at[step, half])
        return remote(block, block, *sems, self.k.z_peer(step))

    def arrived(self, step, half):
        block = self.shard(step, self.k.x, half)
        sems = (self.z_send.at[step, half], self.z_recv.at[step, half])
        return remote(block, block, *sems, self.k.z_peer(step))

    def second(self, step, half, x):
        block = self.shard(step, x, half)
        sems = (self.x_send.at[step, half], self.x_recv.at[step, half])
        return remote(block, block, *sems, self.k.x_peer)

    def start(self, step):
        for half in range(self.HALVES):
            self.first(step, half).start()

    def forward(self, step):
        for half in range(self.HALVES):
            if step > 0:
                self.arrived(step, half).wait_recv()
            self.second(step, half, self.k.x).start()

    def arrive(self, step):
        for half in range(self.HALVES):
            self.second(step, half, 1 - self.k.x).wait_recv()

    def drain(self):
        for step in range(self.k.outer):
            for half in range(self.HALVES):
                if step > 0:
                    self.first(step, half).wait_send()
                self.second(step, half, self.k.x).wait_send()


class DownGradient:
    def __init__(self, k, part, near, far, start, size, sems):
        self.k, self.part, self.near, self.far = k, part, near, far
        self.cols = pl.ds(start, size)
        self.x_send, self.x_recv, self.z_send, self.z_recv = sems

    def one(self, step):
        k = self.k
        z = lax.rem(k.z + step, k.outer)
        return remote(
            self.part.at[z, 1 - k.x, :, self.cols],
            self.near.at[z, :, self.cols],
            self.x_send.at[step],
            self.x_recv.at[step],
            k.x_peer,
        )

    def two(self, step):
        k = self.k
        return remote(
            self.part.at[lax.rem(k.z + step, k.outer), k.x, :, self.cols],
            self.far.at[step - 1, :, self.cols],
            self.z_send.at[step],
            self.z_recv.at[step],
            k.z_peer(step),
        )

    def start(self, step):
        self.one(step).start()

    def forward(self, step):
        k = self.k
        z = lax.rem(k.z + step, k.outer)
        self.one(step).wait_recv()
        here = self.part[z, k.x, :, self.cols].astype(F32)
        self.part[z, k.x, :, self.cols] = (
            here + self.near[z, :, self.cols].astype(F32)
        ).astype(BF16)
        if step > 0:
            self.two(step).start()

    def finish(self, out):
        k = self.k
        total = self.part[k.z, k.x, :, self.cols].astype(F32)
        for step in range(1, k.outer):
            self.two(step).wait_recv()
            total = total + self.far[step - 1, :, self.cols].astype(F32)
        out[...] = total.T

    def drain(self):
        for step in range(self.k.outer):
            self.one(step).wait_send()
            if step > 0:
                self.two(step).wait_send()


def fold(values):
    rows, width = values.shape
    return jnp.sum(values.reshape(rows // 8, 8, width), axis=0)


def mean(values):
    return jnp.sum(values, axis=-1, keepdims=True) * (1.0 / values.shape[-1])


def body(
    outer,
    x_in,
    teacher_in,
    qw_in,
    kw_in,
    vw_in,
    ow_in,
    uw_in,
    dw_in,
    qb_in,
    vb_in,
    ob_in,
    ub_in,
    db_in,
    g1_in,
    b1_in,
    g2_in,
    b2_in,
    out_ref,
    gin_ref,
    gq_ref,
    gk_ref,
    gv_ref,
    go_ref,
    gu_ref,
    gd_ref,
    gvec_ref,
    W,
    G,
    near,
    far,
    X,
    H,
    MX,
    GF,
    Q,
    K,
    V,
    C,
    GC,
    DQKV,
    PT,
    SL,
    ACT,
    GU,
    OWN,
    HID,
    N1,
    R1,
    GS,
    SUMS,
    ACC,
    OUTBOX,
    INBOX,
    VA,
    VR,
    VZ,
    TEACH,
    OT,
    DT,
    VEC,
    w_send,
    w_recv,
    g_send,
    g_recv,
    s_send,
    s_recv,
    r_send,
    r_recv,
    v_send,
    v_recv,
    load_sem,
    dw_sems,
    dg_sems,
    rc_sems,
    sc_sems,
):
    k = Place(outer)
    rows, model = x_in.shape
    width = Q.shape[2]
    inner = ACT.shape[2]
    heads = width // HEAD_DIM
    steps = inner // width
    up_piece = 4
    down_piece = 4 + steps
    pieces = 4 + 2 * steps
    scale = 1.0 / math.sqrt(HEAD_DIM)
    mine, theirs = k.y, 1 - k.y

    own = W.at[k.z, k.x]
    loads = []

    def load(src, dst):
        copy = pltpu.make_async_copy(src, dst, load_sem.at[len(loads)])
        copy.start()
        loads.append(copy)

    load(x_in, X.at[k.t])
    load(qw_in, own.at[:, columns(0, width)])
    load(kw_in, own.at[:, columns(1, width)])
    load(vw_in, own.at[:, columns(2, width)])
    load(ow_in, OT)
    load(uw_in, own.at[:, pl.ds(4 * width, inner)])
    load(dw_in, DT)
    load(teacher_in, TEACH)
    for row, ref in enumerate((qb_in, vb_in, ob_in, db_in, g1_in, b1_in, g2_in, b2_in)):
        load(ref, VEC.at[pl.ds(row, 1), pl.ds(0, model)])
    load(ub_in, VEC.at[pl.ds(8, 1), :])
    k.greet()


    def keep(p, total):
        if p < 3:
            (gq_ref, gk_ref, gv_ref)[p][...] = total
        elif p == 3:
            go_ref[...] = total.T
        elif p < down_piece:
            gu_ref[:, (p - up_piece) * width : (p - up_piece + 1) * width] = total
        else:
            gd_ref[(p - down_piece) * width : (p - down_piece + 1) * width, :] = total.T

    grads = Gradients(k, G, near, far, keep, g_send, g_recv, width)
    stepped = outer == 4 and (model // outer) % 128 == 0
    simple = down_piece if stepped else pieces
    weights = Weights(k, W, w_send, w_recv, width, simple)
    if stepped:
        down_w = DownWeights(k, W, down_piece * width, inner, dw_sems)
        down_g = DownGradient(k, G, near, far, down_piece * width, inner, dg_sems)
    w_order = (0, 1, 3, 2)
    w_chunks = [lax.rem(k.z - step + outer, outer) for step in w_order]
    g_order = (2, 1, 3, 0)
    g_chunks = [lax.rem(k.z + step, outer) for step in g_order]

    def spread(blocks, phase):
        return Spread(k, blocks, s_send, s_recv, phase)

    def reduce(phase):
        return Reduce(k, OUTBOX, INBOX, OWN, r_send, r_recv, phase)

    def matrix(start, size):
        return W[:, :, :, pl.ds(start, size)].reshape(model, size)

    def vector(row):
        return VEC[row : row + 1, 0:model]

    def pair(blocks, seq):
        return blocks[pl.ds(2 * seq, 2)].reshape(2 * rows, model)

    def part_rows(core):
        return pl.ds(pl.multiple_of(core * rows, rows), rows)

    def norm_loop(step):
        def one(i, carry):
            step(pl.ds(pl.multiple_of(i * CHUNK, CHUNK), CHUNK))
            return carry

        lax.fori_loop(0, rows // CHUNK, one, 0)

    SUMS[...] = jnp.zeros_like(SUMS)
    VA[0] = jnp.zeros_like(VA[0])
    for copy in loads:
        copy.wait()
    own[:, columns(3, width)] = OT[...].T
    own[:, pl.ds(4 * width + inner, inner)] = DT[...].T
    s0 = spread(X, 0)
    k.enter()
    s0.start()
    for p in range(WINDOW):
        weights.start(p)

    def project(p, held):
        weights.arrive(p)
        for seq in range(2):
            tokens = X[2 * seq : 2 * seq + 2].reshape(2 * rows, model)
            product = dot(tokens, matrix(p * width, width), NN)
            if p != 1:
                here = pl.ds(pl.multiple_of(k.t * width, width), width)
                product = product + VEC[p // 2 : p // 2 + 1, here]
            held[seq] = product.astype(BF16)

    def head_mask(h):
        lane = lax.broadcasted_iota(jnp.int32, (1, width), 1)
        inside = (lane >= h * HEAD_DIM) & (lane < (h + 1) * HEAD_DIM)
        return jnp.where(inside, 1.0, 0.0).astype(BF16)

    def attend(seq):
        ACC[0] = jnp.zeros_like(ACC[0])

        def head(h, carry):
            mask = head_mask(h)
            scores = dot(K[seq], Q[seq] * mask, NT) * scale
            raised = jnp.exp(scores - jnp.max(scores, axis=0, keepdims=True))
            probs = (raised * (1.0 / jnp.sum(raised, axis=0, keepdims=True))).astype(BF16)
            PT[seq, h] = probs
            ACC[0] += dot(probs, V[seq] * mask, TN)
            return carry

        lax.fori_loop(0, heads, head, 0)
        C[seq] = ACC[0].astype(BF16)

    def out_block(seq, core):
        return dot(C[seq, part_rows(core), :], matrix(3 * width, width), NT)

    weights.forward(0)
    weights.forward(1)
    s0.pass_on()
    s0.own()
    s0.other()
    project(0, Q)
    weights.forward(2)
    project(1, K)
    weights.forward(3)
    project(2, V)
    r0 = reduce(0)
    attend(theirs)
    weights.forward(4)
    weights.arrive(3)
    r0.across(out_block(theirs, 1 - k.c))
    r0.theirs(out_block(theirs, k.c))
    attend(mine)
    weights.forward(5)
    if stepped:
        down_w.start(1)
    r0.partner(out_block(mine, 1 - k.c))
    r0.mine(out_block(mine, k.c))
    weights.forward(6)
    if stepped:
        down_w.start(3)
        down_w.start(2)
    r0.wait()

    def first_norm(r):
        first = X[k.t, r, :].astype(F32) + r0.total(r) + vector(2)
        center = first - mean(first)
        scaling = lax.rsqrt(mean(center * center) + EPSILON)
        normed = center * scaling
        hidden = normed * vector(4) + vector(5)
        N1[r, :] = normed
        R1[r, :] = jnp.broadcast_to(scaling, (CHUNK, R1.shape[1]))
        HID[r, :] = hidden
        H[k.t, r, :] = hidden.astype(BF16)

    norm_loop(first_norm)
    s1 = spread(H, 1)
    s1.start()
    weights.forward(7)
    if stepped:
        down_w.forward(0)
    else:
        weights.forward(8)
    s1.own()
    for p in range(up_piece, down_piece):
        weights.arrive(p)

    def up(seq):
        def part(n, carry):
            cols = pl.ds(pl.multiple_of(n * width, width), width)
            wide = pl.ds(pl.multiple_of((up_piece + n) * width, width), width)
            upper = dot(pair(H, seq), W[:, :, :, wide].reshape(model, width), NN)
            upper = upper + VEC[8:9, pl.ds(pl.multiple_of(k.t * inner + n * width, width), width)]
            erf_part = 1.0 + lax.erf(upper * (1.0 / ROOT_TWO))
            ACT[seq, :, cols] = (0.5 * upper * erf_part).astype(BF16)
            SL[seq, :, cols] = 0.5 * erf_part + upper * jnp.exp(-0.5 * upper * upper) * (
                1.0 / ROOT_TWO_PI
            )
            return carry

        lax.fori_loop(0, steps, part, 0)

    def down_block(seq, core):
        return dot(ACT[seq, part_rows(core), :], matrix(down_piece * width, inner), NT)

    if stepped:
        up(mine)
        down_w.forward(1)
        down_w.forward(3)
        s1.pass_on()
        s1.other()
        up(theirs)
        r1 = ReduceColumns(k, OUTBOX, INBOX, OWN, r_send, r_recv, 1, outer, rc_sems)
        places = {
            "across": (theirs, 1 - k.c),
            "theirs": (theirs, k.c),
            "partner": (mine, 1 - k.c),
            "mine": (mine, k.c),
        }

        def down_chunk(n):
            shard = W[w_chunks[n], :, :, pl.ds(down_piece * width, inner)]
            shard = shard.reshape(model // outer, inner)

            def block(name):
                seq, core = places[name]
                return dot(ACT[seq, part_rows(core), :], shard, NT)

            r1.step(n, w_chunks[n], block)

        down_w.arrive(0)
        down_chunk(0)
        down_w.forward(2)
        down_w.arrive(1)
        down_chunk(1)
        down_w.arrive(3)
        down_chunk(2)
        down_w.arrive(2)
        down_chunk(3)
        r1.wait_columns(w_chunks)
    else:
        up(mine)
        weights.forward(9)
        s1.pass_on()
        s1.other()
        up(theirs)
        weights.forward(10)
        weights.forward(11)
        for p in range(down_piece, pieces):
            weights.arrive(p)
        r1 = reduce(1)
        r1.across(down_block(theirs, 1 - k.c))
        r1.theirs(down_block(theirs, k.c))
        r1.partner(down_block(mine, 1 - k.c))
        r1.mine(down_block(mine, k.c))
        r1.wait()

    def norm_back(d, gain, normed, scaling):
        e = d * gain
        return scaling * (e - mean(e) - normed * mean(e * normed))

    def second_norm(r):
        second = HID[r, :] + r1.total(r) + vector(3)
        center = second - mean(second)
        scaling = lax.rsqrt(mean(center * center) + EPSILON)
        normed = center * scaling
        result = normed * vector(6) + vector(7)
        out_ref[r, :] = result.astype(BF16)
        diff = result - TEACH[r, :].astype(F32)
        grad = norm_back(diff, vector(6), normed, scaling)
        GS[r, :] = grad
        MX[k.t, r, :] = grad.astype(BF16)
        SUMS[0] += fold(grad)
        SUMS[1] += fold(diff * normed)
        SUMS[2] += fold(diff)
        SUMS[3] += fold(diff * diff)

    norm_loop(second_norm)
    if stepped:
        s2 = SpreadColumns(k, MX, s_send, s_recv, 2, outer, sc_sems)
        s2.start_columns(g_chunks)
    else:
        s2 = spread(MX, 2)
        s2.start()
    s2.own()

    def back_up(seq):
        def part(n, carry):
            cols = pl.ds(pl.multiple_of(n * width, width), width)
            wide = pl.ds(pl.multiple_of((down_piece + n) * width, width), width)
            grad = dot(pair(MX, seq), W[:, :, :, wide].reshape(model, width), NN)
            grad = (grad * SL[seq, :, cols]).astype(BF16)
            GU[seq, :, cols] = grad
            SUMS[7, :, cols] += fold(grad.astype(F32))
            return carry

        lax.fori_loop(0, steps, part, 0)

    def hidden_block(seq, core):
        return dot(GU[seq, part_rows(core), :], matrix(up_piece * width, inner), NT)

    def weight_grad(left, right, first, begin, end):
        def piece(n, carry):
            cols = pl.ds(pl.multiple_of(n * width, width), width)
            tokens = 4 * rows
            grad = dot(
                left[...].reshape(tokens, model), right[:, :, cols].reshape(tokens, width), TN
            )
            wide = pl.ds(pl.multiple_of((first + n) * width, width), width)
            G[:, :, :, wide] = grad.astype(BF16).reshape(outer, 2, model // (2 * outer), width)

            @pl.when(n > begin)
            def _():
                grads.start(first + n - 1)

            return carry

        lax.fori_loop(begin, end, piece, 0)

    r2 = reduce(2)
    if stepped:
        r1.drain_columns(w_chunks)
        r2.phase_free = False
    back_up(mine)
    r2.partner(hidden_block(mine, 1 - k.c))
    r2.mine(hidden_block(mine, k.c))
    if stepped:

        def down_grad_chunk(n):
            tokens, size = 4 * rows, model // outer
            cols = pl.ds(pl.multiple_of(g_chunks[n] * size, size), size)
            grad = dot(
                MX[:, :, cols].reshape(tokens, size), ACT[...].reshape(tokens, inner), TN
            )
            G[g_chunks[n], :, :, pl.ds(down_piece * width, inner)] = grad.astype(BF16).reshape(
                2, size // 2, inner
            )

        for n in range(outer):
            s2.pass_part(n, g_chunks[n])
            s2.other_part(n, g_chunks[n])
            down_grad_chunk(n)
            down_g.start(g_order[n])
        back_up(theirs)
        r2.across(hidden_block(theirs, 1 - k.c))
        down_g.forward(g_order[0])
        r2.theirs(hidden_block(theirs, k.c))
        down_g.forward(g_order[1])
        weight_grad(H, GU, up_piece, 0, steps)
        grads.start(up_piece + steps - 1)
        down_g.forward(g_order[2])
        down_g.forward(g_order[3])
    else:
        s2.pass_on()
        s2.other()
        weight_grad(MX, ACT, down_piece, 0, 2)
        back_up(theirs)
        grads.start(down_piece + 1)
        r2.across(hidden_block(theirs, 1 - k.c))
        r2.theirs(hidden_block(theirs, k.c))
        weight_grad(MX, ACT, down_piece, 2, steps)
        grads.forward(8)
        grads.start(down_piece + steps - 1)
        weight_grad(H, GU, up_piece, 0, steps)
        grads.start(up_piece + steps - 1)
        grads.forward(9)
        grads.forward(10)
    r2.wait()

    def first_back(r):
        grad_hidden = GS[r, :] + r2.total(r)
        normed = N1[r, :]
        grad = norm_back(grad_hidden, vector(4), normed, R1[r, :][:, :1])
        GS[r, :] = grad
        GF[k.t, r, :] = grad.astype(BF16)
        SUMS[4] += fold(grad)
        SUMS[5] += fold(grad_hidden * normed)
        SUMS[6] += fold(grad_hidden)

    norm_loop(first_back)
    s3 = spread(GF, 3)
    s3.start()
    s3.own()

    def attend_back(seq):
        GC[...] = dot(pair(GF, seq), matrix(3 * width, width), NN).astype(BF16)
        ACC[...] = jnp.zeros_like(ACC)

        def head(h, carry):
            mask = head_mask(h)
            context = GC[...] * mask
            low = PT[seq, h]
            ACC[2] += dot(low, context, NN)
            probs = low.astype(F32)
            grad = dot(V[seq], context, NT)
            across = jnp.sum(probs * grad, axis=0, keepdims=True)
            grad = (probs * (grad - across)).astype(BF16)
            ACC[1] += dot(grad, Q[seq] * mask, NN)
            ACC[0] += dot(grad, K[seq] * mask, TN)
            return carry

        lax.fori_loop(0, heads, head, 0)
        for n in range(3):
            grad = ACC[n] if n == 2 else ACC[n] * scale
            DQKV[seq, :, n * width : (n + 1) * width] = grad.astype(BF16)

    def input_block(seq, core):
        return dot(DQKV[seq, part_rows(core), :], matrix(0, 3 * width), NT)

    if stepped:
        grads.forward(4)
    attend_back(mine)
    grads.forward(5 if stepped else 11)
    s3.pass_on()
    grads.forward(6 if stepped else 4)
    s3.other()
    weight_grad(GF, C, 3, 0, 1)
    if not stepped:
        grads.forward(5)
    attend_back(theirs)
    grads.start(3)
    if stepped:
        grads.forward(7)

    here = pl.ds(pl.multiple_of(k.t * width, width), width)
    for row, n in ((0, 0), (1, 2)):
        grad = DQKV[:, :, n * width : (n + 1) * width].reshape(4 * rows, width).astype(F32)
        VA[0, row : row + 1, here] = jnp.sum(grad, axis=0, keepdims=True)
    VA[0, pl.ds(3 + k.t, 1), :] = jnp.sum(SUMS[7], axis=0, keepdims=True)
    for row, n in ((7, 0), (10, 1), (11, 2), (12, 3), (2, 4), (8, 5), (9, 6)):
        VA[0, row : row + 1, :] = jnp.sum(SUMS[n], axis=0, keepdims=True)

    def vector_hop(n, peer):
        return remote(VA.at[n], VR.at[n], v_send.at[n], v_recv.at[n], peer)

    def vector_last(step):
        return remote(VA.at[3], VZ.at[k.z], v_send.at[3], v_recv.at[3], k.z_peer(step))

    hops = [vector_hop(n, peer) for n, peer in enumerate((k.c_peer, k.y_peer, k.x_peer))]

    def hop_in(n):
        hops[n].wait_recv()
        VA[n + 1] = VA[n] + VR[n]

    weight_grad(X, DQKV, 0, 0, 1)
    hops[0].start()
    weight_grad(X, DQKV, 0, 1, 2)
    grads.start(0)
    hop_in(0)
    hops[1].start()
    weight_grad(X, DQKV, 0, 2, 3)
    grads.start(1)
    if not stepped:
        grads.forward(6)
    r3 = reduce(3)
    r3.across(input_block(theirs, 1 - k.c))
    r3.theirs(input_block(theirs, k.c))
    hop_in(1)
    hops[2].start()
    grads.start(2)
    if not stepped:
        grads.forward(7)
    r3.partner(input_block(mine, 1 - k.c))
    r3.mine(input_block(mine, k.c))
    if not stepped:
        for p in (8, 9, 10):
            grads.finish(p)
    grads.forward(3)
    grads.forward(0)
    grads.forward(1)
    hop_in(2)
    VZ[k.z] = VA[3]

    def send_last(step, carry):
        vector_last(step).start()
        return carry

    lax.fori_loop(1, outer, send_last, 0)
    grads.forward(2)
    r3.wait()

    def last(r):
        gin_ref[r, :] = GS[r, :] + r3.total(r)

    norm_loop(last)
    if stepped:
        down_g.finish(gd_ref)
    else:
        grads.finish(11)
    for p in (4, 5, 6, 7, 3, 0, 1):
        grads.finish(p)
    vz_all = VZ.at[pl.ds(0, outer - 1)]
    every = remote(vz_all, vz_all, v_send.at[3], v_recv.at[3], k.x_peer)
    every.wait_recv()

    def add(i, total):
        return total + VZ[i]

    gvec_ref[...] = lax.fori_loop(1, outer, add, VZ[0])
    grads.finish(2)

    weights.drain(simple)
    grads.drain(simple)
    if stepped:
        down_w.drain()
        down_g.drain()
        s2.drain_columns(g_chunks)
    for s in (s0, s1, s3) if stepped else (s0, s1, s2, s3):
        s.drain()
    r3.drain()
    for hop in hops:
        hop.wait_send()
    every.wait_send()


def layer(outer, arrays):
    inputs, query_weight, up_weight = arrays[0], arrays[2], arrays[6]
    rows, model = inputs.shape
    shard_rows, width = query_weight.shape
    inner = up_weight.shape[1]
    heads = width // HEAD_DIM
    columns_all = 4 * width + 2 * inner
    pieces = columns_all // width
    seq = 2 * rows
    vmem = pl.BlockSpec(memory_space=pltpu.VMEM)
    anywhere = pl.BlockSpec(memory_space=pl.ANY)
    full = (outer, 2, shard_rows, columns_all)
    dma = pltpu.SemaphoreType.DMA
    outs = (
        jax.ShapeDtypeStruct((rows, model), BF16),
        jax.ShapeDtypeStruct((rows, model), F32),
        jax.ShapeDtypeStruct((shard_rows, width), F32),
        jax.ShapeDtypeStruct((shard_rows, width), F32),
        jax.ShapeDtypeStruct((shard_rows, width), F32),
        jax.ShapeDtypeStruct((width, shard_rows), F32),
        jax.ShapeDtypeStruct((shard_rows, inner), F32),
        jax.ShapeDtypeStruct((inner, shard_rows), F32),
        jax.ShapeDtypeStruct((VECTORS, model), F32),
    )
    return pl.pallas_call(
        functools.partial(body, outer),
        out_shape=outs,
        in_specs=[anywhere] * len(arrays),
        out_specs=(vmem,) * len(outs),
        scratch_shapes=[
            pltpu.VMEM(full, BF16),
            pltpu.VMEM(full, BF16),
            pltpu.VMEM((outer, shard_rows, columns_all), BF16),
            pltpu.VMEM((outer - 1, shard_rows, columns_all), BF16),
            pltpu.VMEM((4, rows, model), BF16),
            pltpu.VMEM((4, rows, model), BF16),
            pltpu.VMEM((4, rows, model), BF16),
            pltpu.VMEM((4, rows, model), BF16),
            pltpu.VMEM((2, seq, width), BF16),
            pltpu.VMEM((2, seq, width), BF16),
            pltpu.VMEM((2, seq, width), BF16),
            pltpu.VMEM((2, seq, width), BF16),
            pltpu.VMEM((seq, width), BF16),
            pltpu.VMEM((2, seq, 3 * width), BF16),
            pltpu.VMEM((2, heads, seq, seq), BF16),
            pltpu.VMEM((2, seq, inner), F32),
            pltpu.VMEM((2, seq, inner), BF16),
            pltpu.VMEM((2, seq, inner), BF16),
            pltpu.VMEM((rows, model), F32),
            pltpu.VMEM((rows, model), F32),
            pltpu.VMEM((rows, model), F32),
            pltpu.VMEM((rows, 128), F32),
            pltpu.VMEM((rows, model), F32),
            pltpu.VMEM((8, 8, model), F32),
            pltpu.VMEM((3, seq, width), F32),
            pltpu.VMEM((3, rows, model), BF16),
            pltpu.VMEM((3, rows, model), BF16),
            pltpu.VMEM((4, VECTORS, model), F32),
            pltpu.VMEM((3, VECTORS, model), F32),
            pltpu.VMEM((outer, VECTORS, model), F32),
            pltpu.VMEM((rows, model), BF16),
            pltpu.VMEM((width, shard_rows), BF16),
            pltpu.VMEM((inner, shard_rows), BF16),
            pltpu.VMEM((9, 4 * inner), F32),
            dma((2, pieces)),
            dma((2, pieces)),
            dma((2, pieces)),
            dma((2, pieces)),
            dma((4, 3)),
            dma((4, 3)),
            dma((4, 3)),
            dma((4, 3)),
            dma((4,)),
            dma((4,)),
            dma((len(arrays),)),
            (dma((outer, 2)),) * 4,
            (dma((outer,)),) * 4,
            (dma((3, outer)),) * 2,
            (dma((outer,)),) * 4,
        ],
        compiler_params=pltpu.CompilerParams(
            collective_id=0, has_side_effects=True, vmem_limit_bytes=67043328
        ),
        name="layer",
    )(*arrays)


def write_body(count, *refs):
    ins, outs, sem = refs[:9], refs[9 : 9 + count], refs[-1]
    vec = ins[8]
    pairs = list(zip(ins[:8], outs[:8]))
    single = [(0, 8), (1, 9), (2, 10), (7, 12), (8, 13), (9, 14), (10, 15), (11, 16), (12, 17)]
    pairs += [(vec.at[pl.ds(row, 1), :], outs[place]) for row, place in single]
    model = vec.shape[1]
    parts = outs[11].shape[1] // model
    for n in range(parts):
        pairs.append((vec.at[pl.ds(3 + n, 1), :], outs[11].at[:, pl.ds(n * model, model)]))
    copies = [pltpu.make_async_copy(src, dst, sem.at[n]) for n, (src, dst) in enumerate(pairs)]
    for copy in copies:
        copy.start()
    for copy in copies:
        copy.wait()


def write(values, up_length):
    model = values[8].shape[1]
    line = jax.ShapeDtypeStruct((1, model), F32)
    outs = [jax.ShapeDtypeStruct(v.shape, v.dtype) for v in values[:8]] + [line] * 10
    outs[11] = jax.ShapeDtypeStruct((1, up_length), F32)
    copies = 17 + up_length // model
    return pl.pallas_call(
        functools.partial(write_body, len(outs)),
        out_shape=tuple(outs),
        in_specs=[pl.BlockSpec(memory_space=pltpu.VMEM)] * len(values),
        out_specs=(pl.BlockSpec(memory_space=pl.ANY),) * len(outs),
        scratch_shapes=[pltpu.SemaphoreType.DMA((copies,))],
        name="write",
    )(*values)


def shards(*arrays):
    inputs = arrays[0]
    outer = lax.axis_size("dp") // 2
    arrays = arrays[:8] + tuple(v.reshape(1, -1) for v in arrays[8:])
    up_length = arrays[11].shape[1]
    values = write(layer(outer, arrays), up_length)
    token_total = inputs.shape[0] * lax.axis_size("dp") * lax.axis_size("tensor")
    loss = jnp.sum(values[17]) * (0.5 / token_total)
    output, grad_inputs, gq, gk, gv, go, gu, gd = values[:8]
    return (output, loss, grad_inputs, gq, gk, gv, go, gu, gd) + tuple(
        v.reshape(-1) for v in values[8:17]
    )


def solution(mesh):
    tokens = P(("dp", "tensor"), None)
    across, down = P("dp", "tensor"), P("tensor", "dp")
    in_specs = (tokens, tokens, across, across, across, down, across, down) + (P(),) * 9
    out_specs = (tokens, P(), tokens, across, across, across, down, across, down) + (P(),) * 9
    return jax.shard_map(shards, mesh=mesh, in_specs=in_specs, out_specs=out_specs, check_vma=False)
```

```python
import functools
import math

import jax
import jax.numpy as jnp
from jax import lax
from jax.experimental import pallas as pl
from jax.experimental.pallas import tpu as pltpu
from jax.sharding import PartitionSpec as P

HEAD_DIM = 64
SEQ = 512
EPSILON = 1e-05
MESH = pl.DeviceIdType.MESH
F32 = jnp.float32
BF16 = jnp.bfloat16
NN = ((1,), (0,))
NT = ((1,), (1,))
TN = ((0,), (0,))
CHUNK = 32
WINDOW = 3
ROOT_TWO = math.sqrt(2.0)
ROOT_TWO_PI = math.sqrt(2.0 * math.pi)
VECTORS = 16


def dot(left, right, dims):
    return lax.dot_general(left, right, (dims, ((), ())), preferred_element_type=F32)


def remote(src, dst, send, recv, peer):
    return pltpu.make_async_remote_copy(
        src_ref=src, dst_ref=dst, send_sem=send, recv_sem=recv, device_id=peer, device_id_type=MESH
    )


class Place:
    def __init__(self, outer):
        self.outer = outer
        self.dp = lax.axis_index("dp")
        self.t = lax.axis_index("tensor")
        self.z, self.x = self.dp // 2, self.dp % 2
        self.y, self.c = self.t // 2, self.t % 2
        self.x_peer = (self.z * 2 + 1 - self.x, self.t)
        self.y_peer = (self.dp, (1 - self.y) * 2 + self.c)
        self.c_peer = (self.dp, self.y * 2 + 1 - self.c)
        self.diag = (1 - self.y) * 2 + 1 - self.c
        self.diag_peer = (self.dp, self.diag)

    def z_peer(self, step):
        return (lax.rem(self.z + step, self.outer) * 2 + self.x, self.t)

    def greet(self):
        barrier = pltpu.get_barrier_semaphore()

        def one(step, carry):
            pl.semaphore_signal(barrier, inc=1, device_id=self.z_peer(step), device_id_type=MESH)
            return carry

        lax.fori_loop(1, self.outer, one, 0)
        for peer in (self.x_peer, self.y_peer, self.diag_peer, self.c_peer):
            pl.semaphore_signal(barrier, inc=1, device_id=peer, device_id_type=MESH)

    def enter(self):
        pl.semaphore_wait(pltpu.get_barrier_semaphore(), self.outer + 3)


def columns(piece, width):
    start = piece * width
    if not isinstance(start, int):
        start = pl.multiple_of(start, width)
    return pl.ds(start, width)


class Weights:
    def __init__(self, k, full, send, recv, width, pieces):
        self.k, self.full, self.send, self.recv, self.width = k, full, send, recv, width
        self.pieces = pieces

    def first(self, p, step):
        block = self.full.at[self.k.z, self.k.x, :, columns(p, self.width)]
        return remote(block, block, self.send.at[0, p], self.recv.at[0, p], self.k.z_peer(step))

    def all_first(self, p):
        block = self.full.at[pl.ds(0, self.k.outer - 1), 0, :, columns(p, self.width)]
        return remote(block, block, self.send.at[0, p], self.recv.at[0, p], self.k.x_peer)

    def second(self, p):
        block = self.full.at[:, self.k.x, :, columns(p, self.width)]
        return remote(block, block, self.send.at[1, p], self.recv.at[1, p], self.k.x_peer)

    def start(self, p):
        def one(step, carry):
            self.first(p, step).start()
            return carry

        lax.fori_loop(1, self.k.outer, one, 0)

    def forward(self, p):
        self.all_first(p).wait_recv()
        self.second(p).start()
        if p + WINDOW < self.pieces:
            self.start(p + WINDOW)

    def arrive(self, p):
        self.second(p).wait_recv()

    def drain(self, pieces):
        def piece(p, carry):
            self.all_first(p).wait_send()
            self.second(p).wait_send()
            return carry

        lax.fori_loop(0, pieces, piece, 0)


class Gradients:
    def __init__(self, k, part, near, far, out, send, recv, width):
        self.k, self.part, self.near, self.far, self.out = k, part, near, far, out
        self.send, self.recv, self.width = send, recv, width

    def one(self, p):
        k, cols = self.k, columns(p, self.width)
        return remote(
            self.part.at[:, 1 - k.x, :, cols],
            self.near.at[:, :, cols],
            self.send.at[0, p],
            self.recv.at[0, p],
            k.x_peer,
        )

    def two(self, p, step):
        k, cols = self.k, columns(p, self.width)
        return remote(
            self.part.at[lax.rem(k.z + step, k.outer), k.x, :, cols],
            self.far.at[step - 1, :, cols],
            self.send.at[1, p],
            self.recv.at[1, p],
            k.z_peer(step),
        )

    def all_two(self, p):
        block = self.far.at[:, :, columns(p, self.width)]
        return remote(block, block, self.send.at[1, p], self.recv.at[1, p], self.k.x_peer)

    def start(self, p):
        self.one(p).start()

    def forward(self, p):
        k, cols = self.k, columns(p, self.width)
        self.one(p).wait_recv()
        here = self.part[:, k.x, :, cols].astype(F32)
        self.part[:, k.x, :, cols] = (here + self.near[:, :, cols].astype(F32)).astype(BF16)

        def send(step, carry):
            self.two(p, step).start()
            return carry

        lax.fori_loop(1, k.outer, send, 0)

    def finish(self, p):
        k, cols = self.k, columns(p, self.width)
        self.all_two(p).wait_recv()

        def add(i, total):
            return total + self.far[i, :, cols].astype(F32)

        total = self.part[k.z, k.x, :, cols].astype(F32)
        total = lax.fori_loop(0, k.outer - 1, add, total)
        self.out(p, total)

    def drain(self, pieces):
        def piece(p, carry):
            self.one(p).wait_send()
            self.all_two(p).wait_send()
            return carry

        lax.fori_loop(0, pieces, piece, 0)


class Line:
    def __init__(self, k):
        self.k = k
        self.two = lax.rem(k.z + 2, 4)
        self.next = k.z + 1 - 2 * lax.rem(k.z, 2)
        self.third = 3 - k.z
        self.middle = (k.z == 1) | (k.z == 2)
        self.end = (k.z == 0) | (k.z == 3)

    def peer(self, z):
        return (z * 2 + self.k.x, self.k.t)


class LineWeights(Weights):
    def __init__(self, line, *rest):
        super().__init__(line.k, *rest)
        self.line = line

    def send_to(self, z, source, send, recv, p):
        block = self.full.at[source, self.k.x, :, columns(p, self.width)]
        return remote(
            block, block, self.send.at[send, p], self.recv.at[recv, p], self.line.peer(z)
        )

    def some(self, count, send, recv, p):
        block = self.full.at[pl.ds(0, count), 0, :, columns(p, self.width)]
        return remote(block, block, self.send.at[send, p], self.recv.at[recv, p], self.k.x_peer)

    def start(self, p):
        line = self.line
        self.send_to(line.two, self.k.z, 0, 0, p).start()
        self.send_to(line.next, self.k.z, 0, 0, p).start()

        @pl.when(line.middle)
        def _():
            self.send_to(line.third, self.k.z, 2, 2, p).start()

    def relay(self, p):
        line = self.line
        self.some(2, 0, 0, p).wait_recv()

        @pl.when(line.middle)
        def _():
            self.send_to(line.next, line.two, 3, 2, p).start()

        if p + WINDOW < self.pieces:
            self.start(p + WINDOW)

    def forward(self, p):
        self.some(1, 2, 2, p).wait_recv()
        self.second(p).start()

    def drain(self, pieces):
        def piece(p, carry):
            self.some(2, 0, 0, p).wait_send()
            self.second(p).wait_send()

            @pl.when(self.line.middle)
            def _():
                self.some(1, 2, 2, p).wait_send()
                self.some(1, 3, 2, p).wait_send()

            return carry

        lax.fori_loop(0, pieces, piece, 0)


class LineGradients(Gradients):
    def __init__(self, line, hop, *rest):
        super().__init__(line.k, *rest)
        self.line, self.hop = line, hop

    def to(self, z, dst, send, recv, p):
        cols = columns(p, self.width)
        return remote(
            self.part.at[z, self.k.x, :, cols],
            dst.at[:, cols],
            self.send.at[send, p],
            self.recv.at[recv, p],
            self.line.peer(z),
        )

    def to_hop(self, p):
        cols = columns(p, self.width)
        return remote(
            self.part.at[self.line.third, self.k.x, :, cols],
            self.hop.at[:, cols],
            self.send.at[2, p],
            self.recv.at[3, p],
            self.line.peer(self.line.next),
        )

    def forward(self, p):
        k, line, cols = self.k, self.line, columns(p, self.width)
        self.one(p).wait_recv()
        here = self.part[:, k.x, :, cols].astype(F32)
        self.part[:, k.x, :, cols] = (here + self.near[:, :, cols].astype(F32)).astype(BF16)

        @pl.when(line.end)
        def _():
            self.to_hop(p).start()
            self.to(line.two, self.far.at[0], 3, 1, p).start()

        @pl.when(line.middle)
        def _():
            self.to(line.third, self.far.at[2], 2, 2, p).start()

        self.to(line.next, self.far.at[1], 1, 1, p).start()

    def relay(self, p):
        line, cols = self.line, columns(p, self.width)

        @pl.when(line.middle)
        def _():
            self.to_hop(p).wait_recv()
            here = self.part[line.two, self.k.x, :, cols].astype(F32)
            here = here + self.hop[:, cols].astype(F32)
            self.part[line.two, self.k.x, :, cols] = here.astype(BF16)
            self.to(line.two, self.far.at[0], 3, 1, p).start()

    def finish(self, p):
        k, line, cols = self.k, self.line, columns(p, self.width)
        both = self.far.at[pl.ds(0, 2), :, cols]
        remote(both, both, self.send.at[1, p], self.recv.at[1, p], k.x_peer).wait_recv()

        @pl.when(line.middle)
        def _():
            self.to(line.third, self.far.at[2], 2, 2, p).wait_recv()

        total = self.part[k.z, k.x, :, cols].astype(F32)
        for n in range(3):
            total = total + self.far[n, :, cols].astype(F32)
        self.out(p, total)

    def drain(self, pieces):
        line = self.line

        def piece(p, carry):
            self.one(p).wait_send()
            for z, sem in ((line.next, 1), (line.third, 2), (line.two, 3)):
                self.to(z, self.far.at[0], sem, 1, p).wait_send()
            return carry

        lax.fori_loop(0, pieces, piece, 0)


class Spread:
    def __init__(self, k, blocks, send, recv, phase):
        self.k, self.blocks, self.send, self.recv, self.phase = k, blocks, send, recv, phase

    def copy(self, number, block, peer):
        ref = self.blocks.at[block]
        return remote(
            ref, ref, self.send.at[self.phase, number], self.recv.at[self.phase, number], peer
        )

    def near(self):
        return self.copy(0, self.k.t, self.k.c_peer)

    def far(self):
        return self.copy(1, self.k.t, self.k.diag_peer)

    def relay(self):
        return self.copy(2, self.k.diag, self.k.c_peer)

    def start(self):
        self.far().start()
        self.near().start()

    def own(self):
        self.near().wait_recv()

    def pass_on(self):
        self.far().wait_recv()
        self.relay().start()

    def other(self):
        self.relay().wait_recv()

    def drain(self):
        self.near().wait_send()
        self.far().wait_send()
        self.relay().wait_send()


class SpreadColumns(Spread):
    def __init__(self, k, blocks, send, recv, phase, chunks, far_sems):
        super().__init__(k, blocks, send, recv, phase)
        self.chunks = chunks
        self.far_send, self.far_recv, self.relay_send, self.relay_recv = far_sems

    def cols(self, chunk):
        width = self.blocks.shape[2] // self.chunks
        return pl.ds(pl.multiple_of(chunk * width, width), width)

    def far_part(self, n, chunk):
        ref = self.blocks.at[self.k.t, :, self.cols(chunk)]
        return remote(ref, ref, self.far_send.at[n], self.far_recv.at[n], self.k.diag_peer)

    def relay_part(self, n, chunk):
        ref = self.blocks.at[self.k.diag, :, self.cols(chunk)]
        return remote(ref, ref, self.relay_send.at[n], self.relay_recv.at[n], self.k.c_peer)

    def start_columns(self, order):
        self.near().start()
        for n, chunk in enumerate(order):
            self.far_part(n, chunk).start()

    def pass_part(self, n, chunk):
        self.far_part(n, chunk).wait_recv()
        self.relay_part(n, chunk).start()

    def other_part(self, n, chunk):
        self.relay_part(n, chunk).wait_recv()

    def drain_columns(self, order):
        self.near().wait_send()
        for n, chunk in enumerate(order):
            self.far_part(n, chunk).wait_send()
            self.relay_part(n, chunk).wait_send()


class Reduce:
    def __init__(self, k, out, inbox, keep, send, recv, phase):
        self.k, self.out, self.inbox, self.keep = k, out, inbox, keep
        self.send, self.recv, self.phase = send, recv, phase

    def copy(self, number, phase=None):
        peer = self.k.y_peer if number == 2 else self.k.c_peer
        phase = self.phase if phase is None else phase
        return remote(
            self.out.at[number],
            self.inbox.at[number],
            self.send.at[phase, number],
            self.recv.at[phase, number],
            peer,
        )

    phase_free = True

    def free(self, number):
        if self.phase > 0 and self.phase_free:
            self.copy(number, self.phase - 1).wait_send()

    def across(self, value):
        self.free(0)
        self.out[0] = value.astype(BF16)
        self.copy(0).start()

    def theirs(self, value):
        self.free(2)
        self.copy(0).wait_recv()
        self.out[2] = (value + self.inbox[0].astype(F32)).astype(BF16)
        self.copy(2).start()

    def partner(self, value):
        self.free(1)
        self.out[1] = value.astype(BF16)
        self.copy(1).start()

    def mine(self, value):
        self.keep[...] = value

    def wait(self):
        self.copy(1).wait_recv()
        self.copy(2).wait_recv()

    def total(self, rows):
        return self.keep[rows, :] + (
            self.inbox[1, rows, :].astype(F32) + self.inbox[2, rows, :].astype(F32)
        )

    def drain(self):
        for number in range(3):
            self.copy(number).wait_send()


class ReduceColumns(Reduce):
    def __init__(self, k, out, inbox, keep, send, recv, phase, chunks, sems):
        super().__init__(k, out, inbox, keep, send, recv, phase)
        self.chunks, self.part_send, self.part_recv = chunks, sems[0], sems[1]

    def cols(self, chunk):
        width = self.keep.shape[1] // self.chunks
        return pl.ds(pl.multiple_of(chunk * width, width), width)

    def part(self, number, n, chunk):
        cols = self.cols(chunk)
        return remote(
            self.out.at[number, :, cols],
            self.inbox.at[number, :, cols],
            self.part_send.at[number, n],
            self.part_recv.at[number, n],
            self.k.y_peer if number == 2 else self.k.c_peer,
        )

    def step(self, n, chunk, block):
        cols = self.cols(chunk)
        if n == 0:
            for number in range(3):
                self.free(number)
        self.out[0, :, cols] = block("across").astype(BF16)
        self.part(0, n, chunk).start()
        self.out[1, :, cols] = block("partner").astype(BF16)
        self.part(1, n, chunk).start()
        value = block("theirs")
        self.part(0, n, chunk).wait_recv()
        self.out[2, :, cols] = (value + self.inbox[0, :, cols].astype(F32)).astype(BF16)
        self.part(2, n, chunk).start()
        self.keep[:, cols] = block("mine")

    def wait_columns(self, order):
        for n, chunk in enumerate(order):
            self.part(1, n, chunk).wait_recv()
            self.part(2, n, chunk).wait_recv()

    def drain_columns(self, order):
        for n, chunk in enumerate(order):
            for number in range(3):
                self.part(number, n, chunk).wait_send()


class DownWeights:
    HALVES = 2

    def __init__(self, line, full, start, size, sems):
        self.line, self.k = line, line.k
        self.full, self.start_at, self.half = full, start, size // self.HALVES
        self.z_send, self.z_recv, self.x_send, self.x_recv = sems
        self.sources = (self.k.z, line.two, line.next, line.third)

    def shard(self, z, x, half):
        return self.full.at[z, x, :, pl.ds(self.start_at + half * self.half, self.half)]

    def along(self, z, source, send, recv, half):
        block = self.shard(source, self.k.x, half)
        sems = (self.z_send.at[send, half], self.z_recv.at[recv, half])
        return remote(block, block, *sems, self.line.peer(z))

    def across(self, step, half, x):
        block = self.shard(self.sources[step], x, half)
        sems = (self.x_send.at[step, half], self.x_recv.at[step, half])
        return remote(block, block, *sems, self.k.x_peer)

    def start(self, step):
        z = self.sources[step]
        for half in range(self.HALVES):
            if step < 3:
                self.along(z, self.k.z, step, step, half).start()
            else:

                @pl.when(self.line.middle)
                def _():
                    self.along(z, self.k.z, 3, 3, half).start()

    def forward(self, step):
        for half in range(self.HALVES):
            if step > 0:
                self.along(self.line.next, self.k.z, step, step, half).wait_recv()
            if step == 1:

                @pl.when(self.line.middle)
                def _():
                    self.along(self.line.next, self.line.two, 0, 3, half).start()

            self.across(step, half, self.k.x).start()

    def arrive(self, step):
        for half in range(self.HALVES):
            self.across(step, half, 1 - self.k.x).wait_recv()

    def drain(self):
        for half in range(self.HALVES):
            for step in range(4):
                self.across(step, half, self.k.x).wait_send()
            for step in (1, 2):
                self.along(self.line.next, self.k.z, step, step, half).wait_send()

            @pl.when(self.line.middle)
            def _():
                for sem in (3, 0):
                    self.along(self.line.next, self.k.z, sem, 3, half).wait_send()


class DownGradient:
    def __init__(self, line, part, near, far, hop, start, size, sems):
        self.line, self.k = line, line.k
        self.part, self.near, self.far, self.hop = part, near, far, hop
        self.cols = pl.ds(start, size)
        self.x_send, self.x_recv, self.z_send, self.z_recv = sems
        self.targets = (line.third, line.next, line.two, self.k.z)

    def one(self, step):
        z = self.targets[step]
        return remote(
            self.part.at[z, 1 - self.k.x, :, self.cols],
            self.near.at[z, :, self.cols],
            self.x_send.at[step],
            self.x_recv.at[step],
            self.k.x_peer,
        )

    def along(self, step, dst, recv, peer):
        return remote(
            self.part.at[self.targets[step], self.k.x, :, self.cols],
            dst.at[:, self.cols],
            self.z_send.at[step],
            self.z_recv.at[recv],
            self.line.peer(peer),
        )

    def start(self, step):
        self.one(step).start()

    def forward(self, step):
        k, line, z = self.k, self.line, self.targets[step]
        self.one(step).wait_recv()
        here = self.part[z, k.x, :, self.cols].astype(F32)
        here = here + self.near[z, :, self.cols].astype(F32)
        if step != 2:
            self.part[z, k.x, :, self.cols] = here.astype(BF16)
        if step == 0:

            @pl.when(line.end)
            def _():
                self.along(0, self.hop, 3, line.next).start()

            @pl.when(line.middle)
            def _():
                self.along(0, self.far.at[2], 0, line.third).start()

        if step == 1:
            self.along(1, self.far.at[1], 1, line.next).start()
        if step == 2:

            @pl.when(line.end)
            def _():
                self.part[z, k.x, :, self.cols] = here.astype(BF16)

            @pl.when(line.middle)
            def _():
                self.along(0, self.hop, 3, line.next).wait_recv()
                both = here + self.hop[:, self.cols].astype(F32)
                self.part[z, k.x, :, self.cols] = both.astype(BF16)

            self.along(2, self.far.at[0], 2, line.two).start()

    def finish(self, out):
        k = self.k

        @pl.when(self.line.middle)
        def _():
            self.along(0, self.far.at[2], 0, k.z).wait_recv()

        total = self.part[k.z, k.x, :, self.cols].astype(F32)
        for n in range(3):
            if n < 2:
                self.along(0, self.far.at[n], 2 - n, k.z).wait_recv()
            total = total + self.far[n, :, self.cols].astype(F32)
        out[...] = total.T

    def drain(self):
        for step in range(4):
            self.one(step).wait_send()
            if step < 3:
                self.along(step, self.far.at[0], 0, self.k.z).wait_send()


def fold(values):
    rows, width = values.shape
    return jnp.sum(values.reshape(rows // 8, 8, width), axis=0)


def mean(values):
    return jnp.sum(values, axis=-1, keepdims=True) * (1.0 / values.shape[-1])


def body(
    outer,
    x_in,
    teacher_in,
    qw_in,
    kw_in,
    vw_in,
    ow_in,
    uw_in,
    dw_in,
    qb_in,
    vb_in,
    ob_in,
    ub_in,
    db_in,
    g1_in,
    b1_in,
    g2_in,
    b2_in,
    out_ref,
    gin_ref,
    gq_ref,
    gk_ref,
    gv_ref,
    go_ref,
    gu_ref,
    gd_ref,
    gvec_ref,
    W,
    G,
    near,
    far,
    X,
    H,
    MX,
    GF,
    Q,
    K,
    V,
    C,
    GC,
    DQKV,
    PT,
    SL,
    ACT,
    GU,
    OWN,
    HID,
    N1,
    R1,
    GS,
    SUMS,
    ACC,
    OUTBOX,
    INBOX,
    VA,
    VR,
    VZ,
    TEACH,
    OT,
    DT,
    VEC,
    w_send,
    w_recv,
    g_send,
    g_recv,
    s_send,
    s_recv,
    r_send,
    r_recv,
    v_send,
    v_recv,
    load_sem,
    HOP,
    dw_sems,
    dg_sems,
    rc_sems,
    sc_sems,
):
    k = Place(outer)
    rows, model = x_in.shape
    width = Q.shape[2]
    inner = ACT.shape[2]
    heads = width // HEAD_DIM
    steps = inner // width
    up_piece = 4
    down_piece = 4 + steps
    pieces = 4 + 2 * steps
    scale = 1.0 / math.sqrt(HEAD_DIM)
    mine, theirs = k.y, 1 - k.y

    own = W.at[k.z, k.x]
    loads = []

    def load(src, dst):
        copy = pltpu.make_async_copy(src, dst, load_sem.at[len(loads)])
        copy.start()
        loads.append(copy)

    load(x_in, X.at[k.t])
    load(qw_in, own.at[:, columns(0, width)])
    load(kw_in, own.at[:, columns(1, width)])
    load(vw_in, own.at[:, columns(2, width)])
    load(ow_in, OT)
    load(uw_in, own.at[:, pl.ds(4 * width, inner)])
    load(dw_in, DT)
    load(teacher_in, TEACH)
    for row, ref in enumerate((qb_in, vb_in, ob_in, db_in, g1_in, b1_in, g2_in, b2_in)):
        load(ref, VEC.at[pl.ds(row, 1), pl.ds(0, model)])
    load(ub_in, VEC.at[pl.ds(8, 1), :])
    k.greet()


    def keep(p, total):
        if p < 3:
            (gq_ref, gk_ref, gv_ref)[p][...] = total
        elif p == 3:
            go_ref[...] = total.T
        elif p < down_piece:
            gu_ref[:, (p - up_piece) * width : (p - up_piece + 1) * width] = total
        else:
            gd_ref[(p - down_piece) * width : (p - down_piece + 1) * width, :] = total.T

    stepped = outer == 4 and (model // outer) % 128 == 0
    simple = down_piece if stepped else pieces
    if stepped:
        line = Line(k)
        weights = LineWeights(line, W, w_send, w_recv, width, simple)
        grads = LineGradients(line, HOP, G, near, far, keep, g_send, g_recv, width)
        down_w = DownWeights(line, W, down_piece * width, inner, dw_sems)
        down_g = DownGradient(line, G, near, far, HOP, down_piece * width, inner, dg_sems)
        w_chunks, g_chunks = down_w.sources, down_g.targets
    else:
        weights = Weights(k, W, w_send, w_recv, width, simple)
        grads = Gradients(k, G, near, far, keep, g_send, g_recv, width)

    def relay(p):
        if stepped and p < simple:
            weights.relay(p)

    def relay_back(p):
        if stepped:
            grads.relay(p)

    def spread(blocks, phase):
        return Spread(k, blocks, s_send, s_recv, phase)

    def reduce(phase):
        return Reduce(k, OUTBOX, INBOX, OWN, r_send, r_recv, phase)

    def matrix(start, size):
        return W[:, :, :, pl.ds(start, size)].reshape(model, size)

    def vector(row):
        return VEC[row : row + 1, 0:model]

    def pair(blocks, seq):
        return blocks[pl.ds(2 * seq, 2)].reshape(2 * rows, model)

    def part_rows(core):
        return pl.ds(pl.multiple_of(core * rows, rows), rows)

    def norm_loop(step):
        def one(i, carry):
            step(pl.ds(pl.multiple_of(i * CHUNK, CHUNK), CHUNK))
            return carry

        lax.fori_loop(0, rows // CHUNK, one, 0)

    SUMS[...] = jnp.zeros_like(SUMS)
    VA[0] = jnp.zeros_like(VA[0])
    if stepped:
        far[2] = jnp.zeros_like(far[2])
    for copy in loads:
        copy.wait()
    own[:, columns(3, width)] = OT[...].T
    own[:, pl.ds(4 * width + inner, inner)] = DT[...].T
    s0 = spread(X, 0)
    k.enter()
    s0.start()
    for p in range(WINDOW):
        weights.start(p)

    def project(p, held):
        weights.arrive(p)
        for seq in range(2):
            tokens = X[2 * seq : 2 * seq + 2].reshape(2 * rows, model)
            product = dot(tokens, matrix(p * width, width), NN)
            if p != 1:
                here = pl.ds(pl.multiple_of(k.t * width, width), width)
                product = product + VEC[p // 2 : p // 2 + 1, here]
            held[seq] = product.astype(BF16)

    def head_mask(h):
        lane = lax.broadcasted_iota(jnp.int32, (1, width), 1)
        inside = (lane >= h * HEAD_DIM) & (lane < (h + 1) * HEAD_DIM)
        return jnp.where(inside, 1.0, 0.0).astype(BF16)

    def attend(seq):
        ACC[0] = jnp.zeros_like(ACC[0])

        def head(h, carry):
            mask = head_mask(h)
            scores = dot(K[seq], Q[seq] * mask, NT) * scale
            raised = jnp.exp(scores - jnp.max(scores, axis=0, keepdims=True))
            probs = (raised * (1.0 / jnp.sum(raised, axis=0, keepdims=True))).astype(BF16)
            PT[seq, h] = probs
            ACC[0] += dot(probs, V[seq] * mask, TN)
            return carry

        lax.fori_loop(0, heads, head, 0)
        C[seq] = ACC[0].astype(BF16)

    def out_block(seq, core):
        return dot(C[seq, part_rows(core), :], matrix(3 * width, width), NT)

    relay(0)
    weights.forward(0)
    relay(1)
    relay(2)
    weights.forward(1)
    s0.pass_on()
    s0.own()
    s0.other()
    project(0, Q)
    relay(3)
    weights.forward(2)
    project(1, K)
    relay(4)
    weights.forward(3)
    project(2, V)
    r0 = reduce(0)
    attend(theirs)
    relay(5)
    weights.forward(4)
    weights.arrive(3)
    r0.across(out_block(theirs, 1 - k.c))
    r0.theirs(out_block(theirs, k.c))
    relay(6)
    attend(mine)
    weights.forward(5)
    relay(7)
    if stepped:
        down_w.start(1)
    r0.partner(out_block(mine, 1 - k.c))
    r0.mine(out_block(mine, k.c))
    weights.forward(6)
    if stepped:
        down_w.start(2)
        down_w.start(3)
    r0.wait()

    def first_norm(r):
        first = X[k.t, r, :].astype(F32) + r0.total(r) + vector(2)
        center = first - mean(first)
        scaling = lax.rsqrt(mean(center * center) + EPSILON)
        normed = center * scaling
        hidden = normed * vector(4) + vector(5)
        N1[r, :] = normed
        R1[r, :] = jnp.broadcast_to(scaling, (CHUNK, R1.shape[1]))
        HID[r, :] = hidden
        H[k.t, r, :] = hidden.astype(BF16)

    norm_loop(first_norm)
    s1 = spread(H, 1)
    s1.start()
    weights.forward(7)
    if stepped:
        down_w.forward(0)
    else:
        weights.forward(8)
    s1.own()
    for p in range(up_piece, down_piece):
        weights.arrive(p)

    def up(seq):
        def part(n, carry):
            cols = pl.ds(pl.multiple_of(n * width, width), width)
            wide = pl.ds(pl.multiple_of((up_piece + n) * width, width), width)
            upper = dot(pair(H, seq), W[:, :, :, wide].reshape(model, width), NN)
            upper = upper + VEC[8:9, pl.ds(pl.multiple_of(k.t * inner + n * width, width), width)]
            erf_part = 1.0 + lax.erf(upper * (1.0 / ROOT_TWO))
            ACT[seq, :, cols] = (0.5 * upper * erf_part).astype(BF16)
            SL[seq, :, cols] = 0.5 * erf_part + upper * jnp.exp(-0.5 * upper * upper) * (
                1.0 / ROOT_TWO_PI
            )
            return carry

        lax.fori_loop(0, steps, part, 0)

    def down_block(seq, core):
        return dot(ACT[seq, part_rows(core), :], matrix(down_piece * width, inner), NT)

    if stepped:
        up(mine)
        down_w.forward(1)
        down_w.forward(2)
        s1.pass_on()
        s1.other()
        up(theirs)
        r1 = ReduceColumns(k, OUTBOX, INBOX, OWN, r_send, r_recv, 1, outer, rc_sems)
        places = {
            "across": (theirs, 1 - k.c),
            "theirs": (theirs, k.c),
            "partner": (mine, 1 - k.c),
            "mine": (mine, k.c),
        }

        def down_chunk(n):
            shard = W[w_chunks[n], :, :, pl.ds(down_piece * width, inner)]
            shard = shard.reshape(model // outer, inner)

            def block(name):
                seq, core = places[name]
                return dot(ACT[seq, part_rows(core), :], shard, NT)

            r1.step(n, w_chunks[n], block)

        down_w.arrive(0)
        down_chunk(0)
        down_w.forward(3)
        for n in range(1, outer):
            down_w.arrive(n)
            down_chunk(n)
        r1.wait_columns(w_chunks)
    else:
        up(mine)
        weights.forward(9)
        s1.pass_on()
        s1.other()
        up(theirs)
        weights.forward(10)
        weights.forward(11)
        for p in range(down_piece, pieces):
            weights.arrive(p)
        r1 = reduce(1)
        r1.across(down_block(theirs, 1 - k.c))
        r1.theirs(down_block(theirs, k.c))
        r1.partner(down_block(mine, 1 - k.c))
        r1.mine(down_block(mine, k.c))
        r1.wait()

    def norm_back(d, gain, normed, scaling):
        e = d * gain
        return scaling * (e - mean(e) - normed * mean(e * normed))

    def second_norm(r):
        second = HID[r, :] + r1.total(r) + vector(3)
        center = second - mean(second)
        scaling = lax.rsqrt(mean(center * center) + EPSILON)
        normed = center * scaling
        result = normed * vector(6) + vector(7)
        out_ref[r, :] = result.astype(BF16)
        diff = result - TEACH[r, :].astype(F32)
        grad = norm_back(diff, vector(6), normed, scaling)
        GS[r, :] = grad
        MX[k.t, r, :] = grad.astype(BF16)
        SUMS[0] += fold(grad)
        SUMS[1] += fold(diff * normed)
        SUMS[2] += fold(diff)
        SUMS[3] += fold(diff * diff)

    norm_loop(second_norm)
    if stepped:
        s2 = SpreadColumns(k, MX, s_send, s_recv, 2, outer, sc_sems)
        s2.start_columns(g_chunks)
    else:
        s2 = spread(MX, 2)
        s2.start()
    s2.own()

    def back_up(seq):
        def part(n, carry):
            cols = pl.ds(pl.multiple_of(n * width, width), width)
            wide = pl.ds(pl.multiple_of((down_piece + n) * width, width), width)
            grad = dot(pair(MX, seq), W[:, :, :, wide].reshape(model, width), NN)
            grad = (grad * SL[seq, :, cols]).astype(BF16)
            GU[seq, :, cols] = grad
            SUMS[7, :, cols] += fold(grad.astype(F32))
            return carry

        lax.fori_loop(0, steps, part, 0)

    def hidden_block(seq, core):
        return dot(GU[seq, part_rows(core), :], matrix(up_piece * width, inner), NT)

    def weight_grad(left, right, first, begin, end):
        def piece(n, carry):
            cols = pl.ds(pl.multiple_of(n * width, width), width)
            tokens = 4 * rows
            grad = dot(
                left[...].reshape(tokens, model), right[:, :, cols].reshape(tokens, width), TN
            )
            wide = pl.ds(pl.multiple_of((first + n) * width, width), width)
            G[:, :, :, wide] = grad.astype(BF16).reshape(outer, 2, model // (2 * outer), width)

            @pl.when(n > begin)
            def _():
                grads.start(first + n - 1)

            return carry

        lax.fori_loop(begin, end, piece, 0)

    r2 = reduce(2)
    if stepped:
        r1.drain_columns(w_chunks)
        r2.phase_free = False
    back_up(mine)
    r2.partner(hidden_block(mine, 1 - k.c))
    r2.mine(hidden_block(mine, k.c))
    if stepped:

        def down_grad_chunk(n):
            tokens, size = 4 * rows, model // outer
            cols = pl.ds(pl.multiple_of(g_chunks[n] * size, size), size)
            grad = dot(
                MX[:, :, cols].reshape(tokens, size), ACT[...].reshape(tokens, inner), TN
            )
            G[g_chunks[n], :, :, pl.ds(down_piece * width, inner)] = grad.astype(BF16).reshape(
                2, size // 2, inner
            )

        for n in range(outer):
            s2.pass_part(n, g_chunks[n])
            s2.other_part(n, g_chunks[n])
            down_grad_chunk(n)
            down_g.start(n)
        back_up(theirs)
        r2.across(hidden_block(theirs, 1 - k.c))
        down_g.forward(0)
        r2.theirs(hidden_block(theirs, k.c))
        down_g.forward(1)
        weight_grad(H, GU, up_piece, 0, steps)
        grads.start(up_piece + steps - 1)
        down_g.forward(2)
        down_g.forward(3)
    else:
        s2.pass_on()
        s2.other()
        weight_grad(MX, ACT, down_piece, 0, 2)
        back_up(theirs)
        grads.start(down_piece + 1)
        r2.across(hidden_block(theirs, 1 - k.c))
        r2.theirs(hidden_block(theirs, k.c))
        weight_grad(MX, ACT, down_piece, 2, steps)
        grads.forward(8)
        grads.start(down_piece + steps - 1)
        weight_grad(H, GU, up_piece, 0, steps)
        grads.start(up_piece + steps - 1)
        grads.forward(9)
        grads.forward(10)
    r2.wait()

    def first_back(r):
        grad_hidden = GS[r, :] + r2.total(r)
        normed = N1[r, :]
        grad = norm_back(grad_hidden, vector(4), normed, R1[r, :][:, :1])
        GS[r, :] = grad
        GF[k.t, r, :] = grad.astype(BF16)
        SUMS[4] += fold(grad)
        SUMS[5] += fold(grad_hidden * normed)
        SUMS[6] += fold(grad_hidden)

    norm_loop(first_back)
    s3 = spread(GF, 3)
    s3.start()
    s3.own()

    def attend_back(seq):
        GC[...] = dot(pair(GF, seq), matrix(3 * width, width), NN).astype(BF16)
        ACC[...] = jnp.zeros_like(ACC)

        def head(h, carry):
            mask = head_mask(h)
            context = GC[...] * mask
            low = PT[seq, h]
            ACC[2] += dot(low, context, NN)
            probs = low.astype(F32)
            grad = dot(V[seq], context, NT)
            across = jnp.sum(probs * grad, axis=0, keepdims=True)
            grad = (probs * (grad - across)).astype(BF16)
            ACC[1] += dot(grad, Q[seq] * mask, NN)
            ACC[0] += dot(grad, K[seq] * mask, TN)
            return carry

        lax.fori_loop(0, heads, head, 0)
        for n in range(3):
            grad = ACC[n] if n == 2 else ACC[n] * scale
            DQKV[seq, :, n * width : (n + 1) * width] = grad.astype(BF16)

    def input_block(seq, core):
        return dot(DQKV[seq, part_rows(core), :], matrix(0, 3 * width), NT)

    if stepped:
        grads.forward(4)
    attend_back(mine)
    relay_back(4)
    grads.forward(5 if stepped else 11)
    s3.pass_on()
    relay_back(5)
    grads.forward(6 if stepped else 4)
    s3.other()
    weight_grad(GF, C, 3, 0, 1)
    if not stepped:
        grads.forward(5)
    attend_back(theirs)
    grads.start(3)
    relay_back(6)
    if stepped:
        grads.forward(7)

    here = pl.ds(pl.multiple_of(k.t * width, width), width)
    for row, n in ((0, 0), (1, 2)):
        grad = DQKV[:, :, n * width : (n + 1) * width].reshape(4 * rows, width).astype(F32)
        VA[0, row : row + 1, here] = jnp.sum(grad, axis=0, keepdims=True)
    VA[0, pl.ds(3 + k.t, 1), :] = jnp.sum(SUMS[7], axis=0, keepdims=True)
    for row, n in ((7, 0), (10, 1), (11, 2), (12, 3), (2, 4), (8, 5), (9, 6)):
        VA[0, row : row + 1, :] = jnp.sum(SUMS[n], axis=0, keepdims=True)

    def vector_hop(n, peer):
        return remote(VA.at[n], VR.at[n], v_send.at[n], v_recv.at[n], peer)

    def vector_last(step):
        return remote(VA.at[3], VZ.at[k.z], v_send.at[3], v_recv.at[3], k.z_peer(step))

    hops = [vector_hop(n, peer) for n, peer in enumerate((k.c_peer, k.y_peer, k.x_peer))]

    def hop_in(n):
        hops[n].wait_recv()
        VA[n + 1] = VA[n] + VR[n]

    weight_grad(X, DQKV, 0, 0, 1)
    hops[0].start()
    weight_grad(X, DQKV, 0, 1, 2)
    grads.start(0)
    hop_in(0)
    hops[1].start()
    weight_grad(X, DQKV, 0, 2, 3)
    grads.start(1)
    if not stepped:
        grads.forward(6)
    r3 = reduce(3)
    r3.across(input_block(theirs, 1 - k.c))
    r3.theirs(input_block(theirs, k.c))
    hop_in(1)
    hops[2].start()
    grads.start(2)
    if not stepped:
        grads.forward(7)
    r3.partner(input_block(mine, 1 - k.c))
    r3.mine(input_block(mine, k.c))
    if not stepped:
        for p in (8, 9, 10):
            grads.finish(p)
    relay_back(7)
    grads.forward(3)
    relay_back(3)
    grads.forward(0)
    relay_back(0)
    grads.forward(1)
    relay_back(1)
    hop_in(2)
    VZ[k.z] = VA[3]

    def send_last(step, carry):
        vector_last(step).start()
        return carry

    lax.fori_loop(1, outer, send_last, 0)
    grads.forward(2)
    relay_back(2)
    r3.wait()

    def last(r):
        gin_ref[r, :] = GS[r, :] + r3.total(r)

    norm_loop(last)
    if stepped:
        down_g.finish(gd_ref)
    else:
        grads.finish(11)
    for p in (4, 5, 6, 7, 3, 0, 1):
        grads.finish(p)
    vz_all = VZ.at[pl.ds(0, outer - 1)]
    every = remote(vz_all, vz_all, v_send.at[3], v_recv.at[3], k.x_peer)
    every.wait_recv()

    def add(i, total):
        return total + VZ[i]

    gvec_ref[...] = lax.fori_loop(1, outer, add, VZ[0])
    grads.finish(2)

    weights.drain(simple)
    grads.drain(simple)
    if stepped:
        down_w.drain()
        down_g.drain()
        s2.drain_columns(g_chunks)
    for s in (s0, s1, s3) if stepped else (s0, s1, s2, s3):
        s.drain()
    r3.drain()
    for hop in hops:
        hop.wait_send()
    every.wait_send()


def layer(outer, arrays):
    inputs, query_weight, up_weight = arrays[0], arrays[2], arrays[6]
    rows, model = inputs.shape
    shard_rows, width = query_weight.shape
    inner = up_weight.shape[1]
    heads = width // HEAD_DIM
    columns_all = 4 * width + 2 * inner
    pieces = columns_all // width
    seq = 2 * rows
    vmem = pl.BlockSpec(memory_space=pltpu.VMEM)
    anywhere = pl.BlockSpec(memory_space=pl.ANY)
    full = (outer, 2, shard_rows, columns_all)
    dma = pltpu.SemaphoreType.DMA
    outs = (
        jax.ShapeDtypeStruct((rows, model), BF16),
        jax.ShapeDtypeStruct((rows, model), F32),
        jax.ShapeDtypeStruct((shard_rows, width), F32),
        jax.ShapeDtypeStruct((shard_rows, width), F32),
        jax.ShapeDtypeStruct((shard_rows, width), F32),
        jax.ShapeDtypeStruct((width, shard_rows), F32),
        jax.ShapeDtypeStruct((shard_rows, inner), F32),
        jax.ShapeDtypeStruct((inner, shard_rows), F32),
        jax.ShapeDtypeStruct((VECTORS, model), F32),
    )
    return pl.pallas_call(
        functools.partial(body, outer),
        out_shape=outs,
        in_specs=[anywhere] * len(arrays),
        out_specs=(vmem,) * len(outs),
        scratch_shapes=[
            pltpu.VMEM(full, BF16),
            pltpu.VMEM(full, BF16),
            pltpu.VMEM((outer, shard_rows, columns_all), BF16),
            pltpu.VMEM((outer - 1, shard_rows, columns_all), BF16),
            pltpu.VMEM((4, rows, model), BF16),
            pltpu.VMEM((4, rows, model), BF16),
            pltpu.VMEM((4, rows, model), BF16),
            pltpu.VMEM((4, rows, model), BF16),
            pltpu.VMEM((2, seq, width), BF16),
            pltpu.VMEM((2, seq, width), BF16),
            pltpu.VMEM((2, seq, width), BF16),
            pltpu.VMEM((2, seq, width), BF16),
            pltpu.VMEM((seq, width), BF16),
            pltpu.VMEM((2, seq, 3 * width), BF16),
            pltpu.VMEM((2, heads, seq, seq), BF16),
            pltpu.VMEM((2, seq, inner), F32),
            pltpu.VMEM((2, seq, inner), BF16),
            pltpu.VMEM((2, seq, inner), BF16),
            pltpu.VMEM((rows, model), F32),
            pltpu.VMEM((rows, model), F32),
            pltpu.VMEM((rows, model), F32),
            pltpu.VMEM((rows, 128), F32),
            pltpu.VMEM((rows, model), F32),
            pltpu.VMEM((8, 8, model), F32),
            pltpu.VMEM((3, seq, width), F32),
            pltpu.VMEM((3, rows, model), BF16),
            pltpu.VMEM((3, rows, model), BF16),
            pltpu.VMEM((4, VECTORS, model), F32),
            pltpu.VMEM((3, VECTORS, model), F32),
            pltpu.VMEM((outer, VECTORS, model), F32),
            pltpu.VMEM((rows, model), BF16),
            pltpu.VMEM((width, shard_rows), BF16),
            pltpu.VMEM((inner, shard_rows), BF16),
            pltpu.VMEM((9, 4 * inner), F32),
            dma((4, pieces)),
            dma((4, pieces)),
            dma((4, pieces)),
            dma((4, pieces)),
            dma((4, 3)),
            dma((4, 3)),
            dma((4, 3)),
            dma((4, 3)),
            dma((4,)),
            dma((4,)),
            dma((len(arrays),)),
            pltpu.VMEM((shard_rows, columns_all), BF16),
            (dma((outer, 2)),) * 4,
            (dma((outer,)),) * 4,
            (dma((3, outer)),) * 2,
            (dma((outer,)),) * 4,
        ],
        compiler_params=pltpu.CompilerParams(
            collective_id=0, has_side_effects=True, vmem_limit_bytes=67043328
        ),
        name="layer",
    )(*arrays)


def write_body(count, *refs):
    ins, outs, sem = refs[:9], refs[9 : 9 + count], refs[-1]
    vec = ins[8]
    pairs = list(zip(ins[:8], outs[:8]))
    single = [(0, 8), (1, 9), (2, 10), (7, 12), (8, 13), (9, 14), (10, 15), (11, 16), (12, 17)]
    pairs += [(vec.at[pl.ds(row, 1), :], outs[place]) for row, place in single]
    model = vec.shape[1]
    parts = outs[11].shape[1] // model
    for n in range(parts):
        pairs.append((vec.at[pl.ds(3 + n, 1), :], outs[11].at[:, pl.ds(n * model, model)]))
    copies = [pltpu.make_async_copy(src, dst, sem.at[n]) for n, (src, dst) in enumerate(pairs)]
    for copy in copies:
        copy.start()
    for copy in copies:
        copy.wait()


def write(values, up_length):
    model = values[8].shape[1]
    line = jax.ShapeDtypeStruct((1, model), F32)
    outs = [jax.ShapeDtypeStruct(v.shape, v.dtype) for v in values[:8]] + [line] * 10
    outs[11] = jax.ShapeDtypeStruct((1, up_length), F32)
    copies = 17 + up_length // model
    return pl.pallas_call(
        functools.partial(write_body, len(outs)),
        out_shape=tuple(outs),
        in_specs=[pl.BlockSpec(memory_space=pltpu.VMEM)] * len(values),
        out_specs=(pl.BlockSpec(memory_space=pl.ANY),) * len(outs),
        scratch_shapes=[pltpu.SemaphoreType.DMA((copies,))],
        name="write",
    )(*values)


def shards(*arrays):
    inputs = arrays[0]
    outer = lax.axis_size("dp") // 2
    arrays = arrays[:8] + tuple(v.reshape(1, -1) for v in arrays[8:])
    up_length = arrays[11].shape[1]
    values = write(layer(outer, arrays), up_length)
    token_total = inputs.shape[0] * lax.axis_size("dp") * lax.axis_size("tensor")
    loss = jnp.sum(values[17]) * (0.5 / token_total)
    output, grad_inputs, gq, gk, gv, go, gu, gd = values[:8]
    return (output, loss, grad_inputs, gq, gk, gv, go, gu, gd) + tuple(
        v.reshape(-1) for v in values[8:17]
    )


def solution(mesh):
    tokens = P(("dp", "tensor"), None)
    across, down = P("dp", "tensor"), P("tensor", "dp")
    in_specs = (tokens, tokens, across, across, across, down, across, down) + (P(),) * 9
    out_specs = (tokens, P(), tokens, across, across, across, down, across, down) + (P(),) * 9
    return jax.shard_map(shards, mesh=mesh, in_specs=in_specs, out_specs=out_specs, check_vma=False)
```

```python
import functools
import math

import jax
import jax.numpy as jnp
from jax import lax
from jax.experimental import pallas as pl
from jax.experimental.pallas import tpu as pltpu
from jax.sharding import PartitionSpec as P

HEAD_DIM = 64
SEQ = 512
EPSILON = 1e-05
MESH = pl.DeviceIdType.MESH
F32 = jnp.float32
BF16 = jnp.bfloat16
NN = ((1,), (0,))
NT = ((1,), (1,))
TN = ((0,), (0,))
CHUNK = 32
WINDOW = 3
CROSSED = (3, 7)
CROSSED_BACK = (2, 7)
ROOT_TWO = math.sqrt(2.0)
ROOT_TWO_PI = math.sqrt(2.0 * math.pi)
VECTORS = 16


def dot(left, right, dims):
    return lax.dot_general(left, right, (dims, ((), ())), preferred_element_type=F32)


def remote(src, dst, send, recv, peer):
    return pltpu.make_async_remote_copy(
        src_ref=src, dst_ref=dst, send_sem=send, recv_sem=recv, device_id=peer, device_id_type=MESH
    )


class Place:
    def __init__(self, outer):
        self.outer = outer
        self.dp = lax.axis_index("dp")
        self.t = lax.axis_index("tensor")
        self.z, self.x = self.dp // 2, self.dp % 2
        self.y, self.c = self.t // 2, self.t % 2
        self.x_peer = (self.z * 2 + 1 - self.x, self.t)
        self.y_peer = (self.dp, (1 - self.y) * 2 + self.c)
        self.c_peer = (self.dp, self.y * 2 + 1 - self.c)
        self.diag = (1 - self.y) * 2 + 1 - self.c
        self.diag_peer = (self.dp, self.diag)

    def z_peer(self, step):
        return (lax.rem(self.z + step, self.outer) * 2 + self.x, self.t)

    def greet(self):
        barrier = pltpu.get_barrier_semaphore()

        def one(step, carry):
            pl.semaphore_signal(barrier, inc=1, device_id=self.z_peer(step), device_id_type=MESH)
            return carry

        lax.fori_loop(1, self.outer, one, 0)
        for peer in (self.x_peer, self.y_peer, self.diag_peer, self.c_peer):
            pl.semaphore_signal(barrier, inc=1, device_id=peer, device_id_type=MESH)

    def enter(self):
        pl.semaphore_wait(pltpu.get_barrier_semaphore(), self.outer + 3)


def columns(piece, width):
    start = piece * width
    if not isinstance(start, int):
        start = pl.multiple_of(start, width)
    return pl.ds(start, width)


class Weights:
    def __init__(self, k, full, send, recv, width, pieces):
        self.k, self.full, self.send, self.recv, self.width = k, full, send, recv, width
        self.pieces = pieces

    def first(self, p, step):
        block = self.full.at[self.k.z, self.k.x, :, columns(p, self.width)]
        return remote(block, block, self.send.at[0, p], self.recv.at[0, p], self.k.z_peer(step))

    def all_first(self, p):
        block = self.full.at[pl.ds(0, self.k.outer - 1), 0, :, columns(p, self.width)]
        return remote(block, block, self.send.at[0, p], self.recv.at[0, p], self.k.x_peer)

    def second(self, p):
        block = self.full.at[:, self.k.x, :, columns(p, self.width)]
        return remote(block, block, self.send.at[1, p], self.recv.at[1, p], self.k.x_peer)

    def start(self, p):
        def one(step, carry):
            self.first(p, step).start()
            return carry

        lax.fori_loop(1, self.k.outer, one, 0)

    def forward(self, p):
        self.all_first(p).wait_recv()
        self.second(p).start()
        if p + WINDOW < self.pieces:
            self.start(p + WINDOW)

    def arrive(self, p):
        self.second(p).wait_recv()

    def drain(self, pieces):
        def piece(p, carry):
            self.all_first(p).wait_send()
            self.second(p).wait_send()
            return carry

        lax.fori_loop(0, pieces, piece, 0)


class Gradients:
    def __init__(self, k, part, near, far, out, send, recv, width):
        self.k, self.part, self.near, self.far, self.out = k, part, near, far, out
        self.send, self.recv, self.width = send, recv, width

    def one(self, p):
        k, cols = self.k, columns(p, self.width)
        return remote(
            self.part.at[:, 1 - k.x, :, cols],
            self.near.at[:, :, cols],
            self.send.at[0, p],
            self.recv.at[0, p],
            k.x_peer,
        )

    def two(self, p, step):
        k, cols = self.k, columns(p, self.width)
        return remote(
            self.part.at[lax.rem(k.z + step, k.outer), k.x, :, cols],
            self.far.at[step - 1, :, cols],
            self.send.at[1, p],
            self.recv.at[1, p],
            k.z_peer(step),
        )

    def all_two(self, p):
        block = self.far.at[:, :, columns(p, self.width)]
        return remote(block, block, self.send.at[1, p], self.recv.at[1, p], self.k.x_peer)

    def start(self, p):
        self.one(p).start()

    def forward(self, p):
        k, cols = self.k, columns(p, self.width)
        self.one(p).wait_recv()
        here = self.part[:, k.x, :, cols].astype(F32)
        self.part[:, k.x, :, cols] = (here + self.near[:, :, cols].astype(F32)).astype(BF16)

        def send(step, carry):
            self.two(p, step).start()
            return carry

        lax.fori_loop(1, k.outer, send, 0)

    def finish(self, p):
        k, cols = self.k, columns(p, self.width)
        self.all_two(p).wait_recv()

        def add(i, total):
            return total + self.far[i, :, cols].astype(F32)

        total = self.part[k.z, k.x, :, cols].astype(F32)
        total = lax.fori_loop(0, k.outer - 1, add, total)
        self.out(p, total)

    def drain(self, pieces):
        def piece(p, carry):
            self.one(p).wait_send()
            self.all_two(p).wait_send()
            return carry

        lax.fori_loop(0, pieces, piece, 0)


class Line:
    def __init__(self, k):
        self.k = k
        self.two = lax.rem(k.z + 2, 4)
        self.next = k.z + 1 - 2 * lax.rem(k.z, 2)
        self.third = 3 - k.z
        self.middle = (k.z == 1) | (k.z == 2)
        self.end = (k.z == 0) | (k.z == 3)

    def peer(self, z):
        return (z * 2 + self.k.x, self.k.t)


class LineWeights(Weights):
    def __init__(self, line, *rest):
        super().__init__(line.k, *rest)
        self.line = line

    def shards(self, z, p):
        return self.full.at[z, slice(None) if p in CROSSED else self.k.x, :, columns(p, self.width)]

    def send_to(self, z, source, send, recv, p):
        block = self.shards(source, p)
        return remote(
            block, block, self.send.at[send, p], self.recv.at[recv, p], self.line.peer(z)
        )

    def some(self, count, send, recv, p):
        block = self.shards(pl.ds(0, count), p)
        return remote(block, block, self.send.at[send, p], self.recv.at[recv, p], self.k.x_peer)

    def crossing(self, p):
        block = self.full.at[self.k.z, self.k.x, :, columns(p, self.width)]
        return remote(block, block, self.send.at[1, p], self.recv.at[1, p], self.k.x_peer)

    def cross(self):
        for p in CROSSED:
            self.crossing(p).start()

    def start(self, p):
        line = self.line
        if p in CROSSED:
            self.crossing(p).wait_recv()
        self.send_to(line.two, self.k.z, 0, 0, p).start()
        self.send_to(line.next, self.k.z, 0, 0, p).start()

        @pl.when(line.middle)
        def _():
            self.send_to(line.third, self.k.z, 2, 2, p).start()

    def relay(self, p):
        line = self.line
        self.some(2, 0, 0, p).wait_recv()

        @pl.when(line.middle)
        def _():
            self.send_to(line.next, line.two, 3, 2, p).start()

        if p + WINDOW < self.pieces:
            self.start(p + WINDOW)

    def forward(self, p):
        if p not in CROSSED:
            self.some(1, 2, 2, p).wait_recv()
            self.second(p).start()

    def arrive(self, p):
        if p in CROSSED:
            self.some(1, 2, 2, p).wait_recv()
        else:
            self.second(p).wait_recv()

    def drain(self, pieces):
        for p in range(pieces):
            self.some(2, 0, 0, p).wait_send()
            (self.crossing(p) if p in CROSSED else self.second(p)).wait_send()

        @pl.when(self.line.middle)
        def _():
            for p in range(pieces):
                self.some(1, 2, 2, p).wait_send()
                self.some(1, 3, 2, p).wait_send()


class CrossedGradient:
    def __init__(self, line, part, far, hop, last, out, send, recv, width, p, place):
        self.line, self.k, self.part, self.out, self.p = line, line.k, part, out, p
        self.far, self.hop, self.last = far.at[place], hop.at[place], last.at[place]
        self.cols = columns(p, width)
        self.send, self.recv = send, recv

    def along(self, z, dst, send, recv, peer):
        return remote(
            self.part.at[z, :, :, self.cols],
            dst,
            self.send.at[send, self.p],
            self.recv.at[recv, self.p],
            self.line.peer(peer),
        )

    def to(self, z, slot, send, recv):
        return self.along(z, self.far.at[slot], send, recv, z)

    def to_hop(self):
        return self.along(self.line.third, self.hop, 2, 3, self.line.next)

    def over(self):
        return remote(
            self.part.at[self.k.z, 1 - self.k.x, :, self.cols],
            self.last,
            self.send.at[0, self.p],
            self.recv.at[0, self.p],
            self.k.x_peer,
        )

    def start(self):
        line = self.line

        @pl.when(line.end)
        def _():
            self.to_hop().start()
            self.to(line.two, 0, 3, 1).start()

        @pl.when(line.middle)
        def _():
            self.to(line.third, 2, 2, 2).start()

        self.to(line.next, 1, 1, 1).start()

    def relay(self):
        line = self.line

        @pl.when(line.middle)
        def _():
            self.to_hop().wait_recv()
            here = self.part[line.two, :, :, self.cols].astype(F32) + self.hop[...].astype(F32)
            self.part[line.two, :, :, self.cols] = here.astype(BF16)
            self.to(line.two, 0, 3, 1).start()

    def total(self, x):
        total = self.part[self.k.z, x, :, self.cols].astype(F32)
        for n in range(3):
            total = total + self.far[n, x].astype(F32)
        return total

    def forward(self):
        line = self.line
        both = self.far.at[pl.ds(0, 2)]
        remote(both, both, self.send.at[1, self.p], self.recv.at[1, self.p], self.k.x_peer).wait_recv()

        @pl.when(line.middle)
        def _():
            self.to(line.third, 2, 2, 2).wait_recv()

        x = 1 - self.k.x
        self.part[self.k.z, x, :, self.cols] = self.total(x).astype(BF16)
        self.over().start()

    def finish(self):
        self.over().wait_recv()
        self.out(self.p, self.total(self.k.x) + self.last[...].astype(F32))

    def drain(self):
        line = self.line
        self.over().wait_send()
        for z, sem in ((line.next, 1), (line.third, 2), (line.two, 3)):
            self.to(z, 0, sem, 1).wait_send()


class LineGradients(Gradients):
    def __init__(self, line, hop, *rest):
        super().__init__(line.k, *rest)
        self.line, self.hop = line, hop

    def to(self, z, dst, send, recv, p):
        cols = columns(p, self.width)
        return remote(
            self.part.at[z, self.k.x, :, cols],
            dst.at[:, cols],
            self.send.at[send, p],
            self.recv.at[recv, p],
            self.line.peer(z),
        )

    def to_hop(self, p):
        cols = columns(p, self.width)
        return remote(
            self.part.at[self.line.third, self.k.x, :, cols],
            self.hop.at[:, cols],
            self.send.at[2, p],
            self.recv.at[3, p],
            self.line.peer(self.line.next),
        )

    def forward(self, p):
        k, line, cols = self.k, self.line, columns(p, self.width)
        self.one(p).wait_recv()
        here = self.part[:, k.x, :, cols].astype(F32)
        self.part[:, k.x, :, cols] = (here + self.near[:, :, cols].astype(F32)).astype(BF16)

        @pl.when(line.end)
        def _():
            self.to_hop(p).start()
            self.to(line.two, self.far.at[0], 3, 1, p).start()

        @pl.when(line.middle)
        def _():
            self.to(line.third, self.far.at[2], 2, 2, p).start()

        self.to(line.next, self.far.at[1], 1, 1, p).start()

    def relay(self, p):
        line, cols = self.line, columns(p, self.width)

        @pl.when(line.middle)
        def _():
            self.to_hop(p).wait_recv()
            here = self.part[line.two, self.k.x, :, cols].astype(F32)
            here = here + self.hop[:, cols].astype(F32)
            self.part[line.two, self.k.x, :, cols] = here.astype(BF16)
            self.to(line.two, self.far.at[0], 3, 1, p).start()

    def finish(self, p):
        k, line, cols = self.k, self.line, columns(p, self.width)
        both = self.far.at[pl.ds(0, 2), :, cols]
        remote(both, both, self.send.at[1, p], self.recv.at[1, p], k.x_peer).wait_recv()

        @pl.when(line.middle)
        def _():
            self.to(line.third, self.far.at[2], 2, 2, p).wait_recv()

        total = self.part[k.z, k.x, :, cols].astype(F32)
        for n in range(3):
            total = total + self.far[n, :, cols].astype(F32)
        self.out(p, total)

    def drain(self, pieces):
        line = self.line
        for p in range(pieces):
            if p in CROSSED_BACK:
                continue
            self.one(p).wait_send()
            for z, sem in ((line.next, 1), (line.third, 2), (line.two, 3)):
                self.to(z, self.far.at[0], sem, 1, p).wait_send()


class Spread:
    def __init__(self, k, blocks, send, recv, phase):
        self.k, self.blocks, self.send, self.recv, self.phase = k, blocks, send, recv, phase

    def copy(self, number, block, peer):
        ref = self.blocks.at[block]
        return remote(
            ref, ref, self.send.at[self.phase, number], self.recv.at[self.phase, number], peer
        )

    def near(self):
        return self.copy(0, self.k.t, self.k.c_peer)

    def far(self):
        return self.copy(1, self.k.t, self.k.diag_peer)

    def relay(self):
        return self.copy(2, self.k.diag, self.k.c_peer)

    def start(self):
        self.far().start()
        self.near().start()

    def own(self):
        self.near().wait_recv()

    def pass_on(self):
        self.far().wait_recv()
        self.relay().start()

    def other(self):
        self.relay().wait_recv()

    def drain(self):
        self.near().wait_send()
        self.far().wait_send()
        self.relay().wait_send()


class SpreadColumns(Spread):
    def __init__(self, k, blocks, send, recv, phase, chunks, far_sems):
        super().__init__(k, blocks, send, recv, phase)
        self.chunks = chunks
        self.far_send, self.far_recv, self.relay_send, self.relay_recv = far_sems

    def cols(self, chunk):
        width = self.blocks.shape[2] // self.chunks
        return pl.ds(pl.multiple_of(chunk * width, width), width)

    def far_part(self, n, chunk):
        ref = self.blocks.at[self.k.t, :, self.cols(chunk)]
        return remote(ref, ref, self.far_send.at[n], self.far_recv.at[n], self.k.diag_peer)

    def relay_part(self, n, chunk):
        ref = self.blocks.at[self.k.diag, :, self.cols(chunk)]
        return remote(ref, ref, self.relay_send.at[n], self.relay_recv.at[n], self.k.c_peer)

    def start_columns(self, order):
        self.near().start()
        for n, chunk in enumerate(order):
            self.far_part(n, chunk).start()

    def pass_part(self, n, chunk):
        self.far_part(n, chunk).wait_recv()
        self.relay_part(n, chunk).start()

    def other_part(self, n, chunk):
        self.relay_part(n, chunk).wait_recv()

    def drain_columns(self, order):
        self.near().wait_send()
        for n, chunk in enumerate(order):
            self.far_part(n, chunk).wait_send()
            self.relay_part(n, chunk).wait_send()


class Reduce:
    def __init__(self, k, out, inbox, keep, send, recv, phase):
        self.k, self.out, self.inbox, self.keep = k, out, inbox, keep
        self.send, self.recv, self.phase = send, recv, phase

    def copy(self, number, phase=None):
        peer = self.k.y_peer if number == 2 else self.k.c_peer
        phase = self.phase if phase is None else phase
        return remote(
            self.out.at[number],
            self.inbox.at[number],
            self.send.at[phase, number],
            self.recv.at[phase, number],
            peer,
        )

    phase_free = True

    def free(self, number):
        if self.phase > 0 and self.phase_free:
            self.copy(number, self.phase - 1).wait_send()

    def across(self, value):
        self.free(0)
        self.out[0] = value.astype(BF16)
        self.copy(0).start()

    def theirs(self, value):
        self.free(2)
        self.copy(0).wait_recv()
        self.out[2] = (value + self.inbox[0].astype(F32)).astype(BF16)
        self.copy(2).start()

    def partner(self, value):
        self.free(1)
        self.out[1] = value.astype(BF16)
        self.copy(1).start()

    def mine(self, value):
        self.keep[...] = value

    def wait(self):
        self.copy(1).wait_recv()
        self.copy(2).wait_recv()

    def total(self, rows):
        return self.keep[rows, :] + (
            self.inbox[1, rows, :].astype(F32) + self.inbox[2, rows, :].astype(F32)
        )

    def drain(self):
        for number in range(3):
            self.copy(number).wait_send()


class ReduceColumns(Reduce):
    def __init__(self, k, out, inbox, keep, send, recv, phase, chunks, sems):
        super().__init__(k, out, inbox, keep, send, recv, phase)
        self.chunks, self.part_send, self.part_recv = chunks, sems[0], sems[1]

    def cols(self, chunk):
        width = self.keep.shape[1] // self.chunks
        return pl.ds(pl.multiple_of(chunk * width, width), width)

    def part(self, number, n, chunk):
        cols = self.cols(chunk)
        return remote(
            self.out.at[number, :, cols],
            self.inbox.at[number, :, cols],
            self.part_send.at[number, n],
            self.part_recv.at[number, n],
            self.k.y_peer if number == 2 else self.k.c_peer,
        )

    def step(self, n, chunk, block):
        cols = self.cols(chunk)
        if n == 0:
            for number in range(3):
                self.free(number)
        self.out[0, :, cols] = block("across").astype(BF16)
        self.part(0, n, chunk).start()
        self.out[1, :, cols] = block("partner").astype(BF16)
        self.part(1, n, chunk).start()
        value = block("theirs")
        self.part(0, n, chunk).wait_recv()
        self.out[2, :, cols] = (value + self.inbox[0, :, cols].astype(F32)).astype(BF16)
        self.part(2, n, chunk).start()
        self.keep[:, cols] = block("mine")

    def wait_columns(self, order):
        for n, chunk in enumerate(order):
            self.part(1, n, chunk).wait_recv()
            self.part(2, n, chunk).wait_recv()

    def drain_columns(self, order):
        for n, chunk in enumerate(order):
            for number in range(3):
                self.part(number, n, chunk).wait_send()


class DownWeights:
    HALVES = 2

    def __init__(self, line, full, start, size, sems):
        self.line, self.k = line, line.k
        self.full, self.start_at, self.half = full, start, size // self.HALVES
        self.z_send, self.z_recv, self.x_send, self.x_recv = sems
        self.sources = (self.k.z, line.two, line.next, line.third)

    def shard(self, z, x, half):
        return self.full.at[z, x, :, pl.ds(self.start_at + half * self.half, self.half)]

    def along(self, z, source, send, recv, half):
        block = self.shard(source, self.k.x, half)
        sems = (self.z_send.at[send, half], self.z_recv.at[recv, half])
        return remote(block, block, *sems, self.line.peer(z))

    def across(self, step, half, x):
        block = self.shard(self.sources[step], x, half)
        sems = (self.x_send.at[step, half], self.x_recv.at[step, half])
        return remote(block, block, *sems, self.k.x_peer)

    def start(self, step):
        z = self.sources[step]
        for half in range(self.HALVES):
            if step < 3:
                self.along(z, self.k.z, step, step, half).start()
            else:

                @pl.when(self.line.middle)
                def _():
                    self.along(z, self.k.z, 3, 3, half).start()

    def forward(self, step):
        for half in range(self.HALVES):
            if step > 0:
                self.along(self.line.next, self.k.z, step, step, half).wait_recv()
            if step == 1:

                @pl.when(self.line.middle)
                def _():
                    self.along(self.line.next, self.line.two, 0, 3, half).start()

            self.across(step, half, self.k.x).start()

    def arrive(self, step):
        for half in range(self.HALVES):
            self.across(step, half, 1 - self.k.x).wait_recv()

    def drain(self):
        for half in range(self.HALVES):
            for step in range(4):
                self.across(step, half, self.k.x).wait_send()
            for step in (1, 2):
                self.along(self.line.next, self.k.z, step, step, half).wait_send()

            @pl.when(self.line.middle)
            def _():
                for sem in (3, 0):
                    self.along(self.line.next, self.k.z, sem, 3, half).wait_send()


class DownGradient:
    def __init__(self, line, part, near, far, hop, start, size, sems):
        self.line, self.k = line, line.k
        self.part, self.near, self.far, self.hop = part, near, far, hop
        self.cols = pl.ds(start, size)
        self.x_send, self.x_recv, self.z_send, self.z_recv = sems
        self.targets = (line.third, line.next, line.two, self.k.z)

    def one(self, step):
        z = self.targets[step]
        return remote(
            self.part.at[z, 1 - self.k.x, :, self.cols],
            self.near.at[z, :, self.cols],
            self.x_send.at[step],
            self.x_recv.at[step],
            self.k.x_peer,
        )

    def along(self, step, dst, recv, peer):
        return remote(
            self.part.at[self.targets[step], self.k.x, :, self.cols],
            dst.at[:, self.cols],
            self.z_send.at[step],
            self.z_recv.at[recv],
            self.line.peer(peer),
        )

    def start(self, step):
        self.one(step).start()

    def forward(self, step):
        k, line, z = self.k, self.line, self.targets[step]
        self.one(step).wait_recv()
        here = self.part[z, k.x, :, self.cols].astype(F32)
        here = here + self.near[z, :, self.cols].astype(F32)
        if step != 2:
            self.part[z, k.x, :, self.cols] = here.astype(BF16)
        if step == 0:

            @pl.when(line.end)
            def _():
                self.along(0, self.hop, 3, line.next).start()

            @pl.when(line.middle)
            def _():
                self.along(0, self.far.at[2], 0, line.third).start()

        if step == 1:
            self.along(1, self.far.at[1], 1, line.next).start()
        if step == 2:

            @pl.when(line.end)
            def _():
                self.part[z, k.x, :, self.cols] = here.astype(BF16)

            @pl.when(line.middle)
            def _():
                self.along(0, self.hop, 3, line.next).wait_recv()
                both = here + self.hop[:, self.cols].astype(F32)
                self.part[z, k.x, :, self.cols] = both.astype(BF16)

            self.along(2, self.far.at[0], 2, line.two).start()

    def finish(self, out):
        k = self.k

        @pl.when(self.line.middle)
        def _():
            self.along(0, self.far.at[2], 0, k.z).wait_recv()

        total = self.part[k.z, k.x, :, self.cols].astype(F32)
        for n in range(3):
            if n < 2:
                self.along(0, self.far.at[n], 2 - n, k.z).wait_recv()
            total = total + self.far[n, :, self.cols].astype(F32)
        out[...] = total.T

    def drain(self):
        for step in range(4):
            self.one(step).wait_send()
            if step < 3:
                self.along(step, self.far.at[0], 0, self.k.z).wait_send()


def fold(values):
    rows, width = values.shape
    return jnp.sum(values.reshape(rows // 8, 8, width), axis=0)


def mean(values):
    return jnp.sum(values, axis=-1, keepdims=True) * (1.0 / values.shape[-1])


def body(
    outer,
    x_in,
    teacher_in,
    qw_in,
    kw_in,
    vw_in,
    ow_in,
    uw_in,
    dw_in,
    qb_in,
    vb_in,
    ob_in,
    ub_in,
    db_in,
    g1_in,
    b1_in,
    g2_in,
    b2_in,
    out_ref,
    gin_ref,
    gq_ref,
    gk_ref,
    gv_ref,
    go_ref,
    gu_ref,
    gd_ref,
    gvec_ref,
    W,
    G,
    near,
    far,
    X,
    H,
    MX,
    GF,
    Q,
    K,
    V,
    C,
    GC,
    DQKV,
    PT,
    SL,
    ACT,
    GU,
    OWN,
    HID,
    N1,
    R1,
    GS,
    SUMS,
    ACC,
    OUTBOX,
    INBOX,
    VA,
    VR,
    VZ,
    TEACH,
    OT,
    DT,
    VEC,
    w_send,
    w_recv,
    g_send,
    g_recv,
    s_send,
    s_recv,
    r_send,
    r_recv,
    v_send,
    v_recv,
    load_sem,
    HOP,
    CFAR,
    CHOP,
    CLAST,
    dw_sems,
    dg_sems,
    rc_sems,
    sc_sems,
):
    k = Place(outer)
    rows, model = x_in.shape
    width = Q.shape[2]
    inner = ACT.shape[2]
    heads = width // HEAD_DIM
    steps = inner // width
    up_piece = 4
    down_piece = 4 + steps
    pieces = 4 + 2 * steps
    scale = 1.0 / math.sqrt(HEAD_DIM)
    mine, theirs = k.y, 1 - k.y

    own = W.at[k.z, k.x]
    loads = []

    def load(src, dst):
        copy = pltpu.make_async_copy(src, dst, load_sem.at[len(loads)])
        copy.start()
        loads.append(copy)

    load(x_in, X.at[k.t])
    load(qw_in, own.at[:, columns(0, width)])
    load(kw_in, own.at[:, columns(1, width)])
    load(vw_in, own.at[:, columns(2, width)])
    load(ow_in, OT)
    load(uw_in, own.at[:, pl.ds(4 * width, inner)])
    load(dw_in, DT)
    load(teacher_in, TEACH)
    for row, ref in enumerate((qb_in, vb_in, ob_in, db_in, g1_in, b1_in, g2_in, b2_in)):
        load(ref, VEC.at[pl.ds(row, 1), pl.ds(0, model)])
    load(ub_in, VEC.at[pl.ds(8, 1), :])
    k.greet()


    def keep(p, total):
        if p < 3:
            (gq_ref, gk_ref, gv_ref)[p][...] = total
        elif p == 3:
            go_ref[...] = total.T
        elif p < down_piece:
            gu_ref[:, (p - up_piece) * width : (p - up_piece + 1) * width] = total
        else:
            gd_ref[(p - down_piece) * width : (p - down_piece + 1) * width, :] = total.T

    stepped = outer == 4 and (model // outer) % 128 == 0
    simple = down_piece if stepped else pieces
    if stepped:
        line = Line(k)
        weights = LineWeights(line, W, w_send, w_recv, width, simple)
        grads = LineGradients(line, HOP, G, near, far, keep, g_send, g_recv, width)
        crossed = {
            p: CrossedGradient(
                line, G, CFAR, CHOP, CLAST, keep, g_send, g_recv, width, p, place
            )
            for place, p in enumerate(CROSSED_BACK)
        }
        down_w = DownWeights(line, W, down_piece * width, inner, dw_sems)
        down_g = DownGradient(line, G, near, far, HOP, down_piece * width, inner, dg_sems)
        w_chunks, g_chunks = down_w.sources, down_g.targets
    else:
        weights = Weights(k, W, w_send, w_recv, width, simple)
        grads = Gradients(k, G, near, far, keep, g_send, g_recv, width)

    def relay(p):
        if stepped and p < simple:
            weights.relay(p)

    def relay_back(p):
        if stepped:
            grads.relay(p)

    def spread(blocks, phase):
        return Spread(k, blocks, s_send, s_recv, phase)

    def reduce(phase):
        return Reduce(k, OUTBOX, INBOX, OWN, r_send, r_recv, phase)

    def matrix(start, size):
        return W[:, :, :, pl.ds(start, size)].reshape(model, size)

    def vector(row):
        return VEC[row : row + 1, 0:model]

    def pair(blocks, seq):
        return blocks[pl.ds(2 * seq, 2)].reshape(2 * rows, model)

    def part_rows(core):
        return pl.ds(pl.multiple_of(core * rows, rows), rows)

    def norm_loop(step):
        def one(i, carry):
            step(pl.ds(pl.multiple_of(i * CHUNK, CHUNK), CHUNK))
            return carry

        lax.fori_loop(0, rows // CHUNK, one, 0)

    SUMS[...] = jnp.zeros_like(SUMS)
    VA[0] = jnp.zeros_like(VA[0])
    if stepped:
        far[2] = jnp.zeros_like(far[2])
        for place in range(len(CROSSED_BACK)):
            CFAR[place, 2] = jnp.zeros_like(CFAR[place, 2])
    for copy in loads:
        copy.wait()
    own[:, columns(3, width)] = OT[...].T
    own[:, pl.ds(4 * width + inner, inner)] = DT[...].T
    s0 = spread(X, 0)
    k.enter()
    if stepped:
        weights.cross()
    s0.start()
    for p in range(WINDOW):
        weights.start(p)

    def project(p, held):
        weights.arrive(p)
        for seq in range(2):
            tokens = X[2 * seq : 2 * seq + 2].reshape(2 * rows, model)
            product = dot(tokens, matrix(p * width, width), NN)
            if p != 1:
                here = pl.ds(pl.multiple_of(k.t * width, width), width)
                product = product + VEC[p // 2 : p // 2 + 1, here]
            held[seq] = product.astype(BF16)

    def head_mask(h):
        lane = lax.broadcasted_iota(jnp.int32, (1, width), 1)
        inside = (lane >= h * HEAD_DIM) & (lane < (h + 1) * HEAD_DIM)
        return jnp.where(inside, 1.0, 0.0).astype(BF16)

    def attend(seq, between=lambda: None):
        ACC[0] = jnp.zeros_like(ACC[0])

        def head(h, carry):
            mask = head_mask(h)
            scores = dot(K[seq], Q[seq] * mask, NT) * scale
            raised = jnp.exp(scores - jnp.max(scores, axis=0, keepdims=True))
            probs = (raised * (1.0 / jnp.sum(raised, axis=0, keepdims=True))).astype(BF16)
            PT[seq, h] = probs
            ACC[0] += dot(probs, V[seq] * mask, TN)
            return carry

        lax.fori_loop(0, heads // 2, head, 0)
        between()
        lax.fori_loop(heads // 2, heads, head, 0)
        C[seq] = ACC[0].astype(BF16)

    def out_block(seq, core):
        return dot(C[seq, part_rows(core), :], matrix(3 * width, width), NT)

    relay(0)
    weights.forward(0)
    relay(1)
    weights.forward(1)
    relay(2)
    s0.pass_on()
    s0.own()
    s0.other()
    project(0, Q)
    weights.forward(2)
    project(1, K)
    relay(3)
    if not stepped:
        weights.forward(3)
    project(2, V)
    r0 = reduce(0)
    attend(theirs, lambda: relay(4))
    weights.forward(4)
    weights.arrive(3)
    r0.across(out_block(theirs, 1 - k.c))
    r0.theirs(out_block(theirs, k.c))
    relay(5)
    attend(mine, lambda: weights.forward(5))
    relay(6)
    r0.partner(out_block(mine, 1 - k.c))
    r0.mine(out_block(mine, k.c))
    weights.forward(6)
    relay(7)
    if stepped:
        down_w.forward(0)
        down_w.start(1)
        down_w.start(2)
        down_w.start(3)
    r0.wait()

    def first_norm(r):
        first = X[k.t, r, :].astype(F32) + r0.total(r) + vector(2)
        center = first - mean(first)
        scaling = lax.rsqrt(mean(center * center) + EPSILON)
        normed = center * scaling
        hidden = normed * vector(4) + vector(5)
        N1[r, :] = normed
        R1[r, :] = jnp.broadcast_to(scaling, (CHUNK, R1.shape[1]))
        HID[r, :] = hidden
        H[k.t, r, :] = hidden.astype(BF16)

    norm_loop(first_norm)
    s1 = spread(H, 1)
    s1.start()
    weights.forward(7)
    if not stepped:
        weights.forward(8)
    s1.own()
    for p in range(up_piece, down_piece):
        weights.arrive(p)

    def up(seq):
        def part(n, carry):
            cols = pl.ds(pl.multiple_of(n * width, width), width)
            wide = pl.ds(pl.multiple_of((up_piece + n) * width, width), width)
            upper = dot(pair(H, seq), W[:, :, :, wide].reshape(model, width), NN)
            upper = upper + VEC[8:9, pl.ds(pl.multiple_of(k.t * inner + n * width, width), width)]
            erf_part = 1.0 + lax.erf(upper * (1.0 / ROOT_TWO))
            ACT[seq, :, cols] = (0.5 * upper * erf_part).astype(BF16)
            SL[seq, :, cols] = 0.5 * erf_part + upper * jnp.exp(-0.5 * upper * upper) * (
                1.0 / ROOT_TWO_PI
            )
            return carry

        lax.fori_loop(0, steps, part, 0)

    def down_block(seq, core):
        return dot(ACT[seq, part_rows(core), :], matrix(down_piece * width, inner), NT)

    if stepped:
        up(mine)
        down_w.forward(1)
        s1.pass_on()
        down_w.forward(2)
        s1.other()
        up(theirs)
        r1 = ReduceColumns(k, OUTBOX, INBOX, OWN, r_send, r_recv, 1, outer, rc_sems)
        places = {
            "across": (theirs, 1 - k.c),
            "theirs": (theirs, k.c),
            "partner": (mine, 1 - k.c),
            "mine": (mine, k.c),
        }

        def down_chunk(n):
            shard = W[w_chunks[n], :, :, pl.ds(down_piece * width, inner)]
            shard = shard.reshape(model // outer, inner)

            def block(name):
                seq, core = places[name]
                return dot(ACT[seq, part_rows(core), :], shard, NT)

            r1.step(n, w_chunks[n], block)

        down_w.arrive(0)
        down_chunk(0)
        down_w.forward(3)
        for n in range(1, outer):
            down_w.arrive(n)
            down_chunk(n)
        r1.wait_columns(w_chunks)
    else:
        up(mine)
        weights.forward(9)
        s1.pass_on()
        s1.other()
        up(theirs)
        weights.forward(10)
        weights.forward(11)
        for p in range(down_piece, pieces):
            weights.arrive(p)
        r1 = reduce(1)
        r1.across(down_block(theirs, 1 - k.c))
        r1.theirs(down_block(theirs, k.c))
        r1.partner(down_block(mine, 1 - k.c))
        r1.mine(down_block(mine, k.c))
        r1.wait()

    def norm_back(d, gain, normed, scaling):
        e = d * gain
        return scaling * (e - mean(e) - normed * mean(e * normed))

    def second_norm(r):
        second = HID[r, :] + r1.total(r) + vector(3)
        center = second - mean(second)
        scaling = lax.rsqrt(mean(center * center) + EPSILON)
        normed = center * scaling
        result = normed * vector(6) + vector(7)
        out_ref[r, :] = result.astype(BF16)
        diff = result - TEACH[r, :].astype(F32)
        grad = norm_back(diff, vector(6), normed, scaling)
        GS[r, :] = grad
        MX[k.t, r, :] = grad.astype(BF16)
        SUMS[0] += fold(grad)
        SUMS[1] += fold(diff * normed)
        SUMS[2] += fold(diff)
        SUMS[3] += fold(diff * diff)

    norm_loop(second_norm)
    if stepped:
        s2 = SpreadColumns(k, MX, s_send, s_recv, 2, outer, sc_sems)
        s2.start_columns(g_chunks)
    else:
        s2 = spread(MX, 2)
        s2.start()
    s2.own()

    def back_up(seq):
        def part(n, carry):
            cols = pl.ds(pl.multiple_of(n * width, width), width)
            wide = pl.ds(pl.multiple_of((down_piece + n) * width, width), width)
            grad = dot(pair(MX, seq), W[:, :, :, wide].reshape(model, width), NN)
            grad = (grad * SL[seq, :, cols]).astype(BF16)
            GU[seq, :, cols] = grad
            SUMS[7, :, cols] += fold(grad.astype(F32))
            return carry

        lax.fori_loop(0, steps, part, 0)

    def hidden_block(seq, core):
        return dot(GU[seq, part_rows(core), :], matrix(up_piece * width, inner), NT)

    def weight_grad(left, right, first, begin, end):
        def piece(n, carry):
            cols = pl.ds(pl.multiple_of(n * width, width), width)
            tokens = 4 * rows
            grad = dot(
                left[...].reshape(tokens, model), right[:, :, cols].reshape(tokens, width), TN
            )
            wide = pl.ds(pl.multiple_of((first + n) * width, width), width)
            G[:, :, :, wide] = grad.astype(BF16).reshape(outer, 2, model // (2 * outer), width)

            @pl.when(n > begin)
            def _():
                grads.start(first + n - 1)

            return carry

        lax.fori_loop(begin, end, piece, 0)

    r2 = reduce(2)
    if stepped:
        r1.drain_columns(w_chunks)
        r2.phase_free = False
    back_up(mine)
    r2.partner(hidden_block(mine, 1 - k.c))
    r2.mine(hidden_block(mine, k.c))
    if stepped:

        def down_grad_chunk(n):
            tokens, size = 4 * rows, model // outer
            cols = pl.ds(pl.multiple_of(g_chunks[n] * size, size), size)
            grad = dot(
                MX[:, :, cols].reshape(tokens, size), ACT[...].reshape(tokens, inner), TN
            )
            G[g_chunks[n], :, :, pl.ds(down_piece * width, inner)] = grad.astype(BF16).reshape(
                2, size // 2, inner
            )

        for n in range(outer):
            s2.pass_part(n, g_chunks[n])
            s2.other_part(n, g_chunks[n])
            down_grad_chunk(n)
            down_g.start(n)
        back_up(theirs)
        r2.across(hidden_block(theirs, 1 - k.c))
        down_g.forward(0)
        r2.theirs(hidden_block(theirs, k.c))
        down_g.forward(1)
        weight_grad(H, GU, up_piece, steps - 1, steps)
        crossed[7].start()
        weight_grad(H, GU, up_piece, 0, steps - 1)
        grads.start(up_piece + steps - 2)
        down_g.forward(2)
        down_g.forward(3)
    else:
        s2.pass_on()
        s2.other()
        weight_grad(MX, ACT, down_piece, 0, 2)
        back_up(theirs)
        grads.start(down_piece + 1)
        r2.across(hidden_block(theirs, 1 - k.c))
        r2.theirs(hidden_block(theirs, k.c))
        weight_grad(MX, ACT, down_piece, 2, steps)
        grads.forward(8)
        grads.start(down_piece + steps - 1)
        weight_grad(H, GU, up_piece, 0, steps)
        grads.start(up_piece + steps - 1)
        grads.forward(9)
        grads.forward(10)
    r2.wait()

    def first_back(r):
        grad_hidden = GS[r, :] + r2.total(r)
        normed = N1[r, :]
        grad = norm_back(grad_hidden, vector(4), normed, R1[r, :][:, :1])
        GS[r, :] = grad
        GF[k.t, r, :] = grad.astype(BF16)
        SUMS[4] += fold(grad)
        SUMS[5] += fold(grad_hidden * normed)
        SUMS[6] += fold(grad_hidden)

    norm_loop(first_back)
    s3 = spread(GF, 3)
    s3.start()
    s3.own()

    def attend_back(seq, between=lambda: None):
        GC[...] = dot(pair(GF, seq), matrix(3 * width, width), NN).astype(BF16)
        ACC[...] = jnp.zeros_like(ACC)

        def head(h, carry):
            mask = head_mask(h)
            context = GC[...] * mask
            low = PT[seq, h]
            ACC[2] += dot(low, context, NN)
            probs = low.astype(F32)
            grad = dot(V[seq], context, NT)
            across = jnp.sum(probs * grad, axis=0, keepdims=True)
            grad = (probs * (grad - across)).astype(BF16)
            ACC[1] += dot(grad, Q[seq] * mask, NN)
            ACC[0] += dot(grad, K[seq] * mask, TN)
            return carry

        lax.fori_loop(0, heads // 2, head, 0)
        between()
        lax.fori_loop(heads // 2, heads, head, 0)
        for n in range(3):
            grad = ACC[n] if n == 2 else ACC[n] * scale
            DQKV[seq, :, n * width : (n + 1) * width] = grad.astype(BF16)

    def input_block(seq, core):
        return dot(DQKV[seq, part_rows(core), :], matrix(0, 3 * width), NT)

    if stepped:
        crossed[7].relay()
        grads.forward(4)
        attend_back(mine)
        grads.forward(5)
        relay_back(4)
        s3.pass_on()
        crossed[7].forward()
        s3.other()
        weight_grad(GF, C, 3, 0, 1)
        grads.forward(6)
        grads.start(3)
        relay_back(5)
        attend_back(theirs)
        relay_back(6)
    else:
        attend_back(mine)
        grads.forward(11)
        s3.pass_on()
        grads.forward(4)
        s3.other()
        weight_grad(GF, C, 3, 0, 1)
        grads.forward(5)
        attend_back(theirs)
        grads.start(3)

    here = pl.ds(pl.multiple_of(k.t * width, width), width)
    for row, n in ((0, 0), (1, 2)):
        grad = DQKV[:, :, n * width : (n + 1) * width].reshape(4 * rows, width).astype(F32)
        VA[0, row : row + 1, here] = jnp.sum(grad, axis=0, keepdims=True)
    VA[0, pl.ds(3 + k.t, 1), :] = jnp.sum(SUMS[7], axis=0, keepdims=True)
    for row, n in ((7, 0), (10, 1), (11, 2), (12, 3), (2, 4), (8, 5), (9, 6)):
        VA[0, row : row + 1, :] = jnp.sum(SUMS[n], axis=0, keepdims=True)

    def vector_hop(n, peer):
        return remote(VA.at[n], VR.at[n], v_send.at[n], v_recv.at[n], peer)

    def vector_last(step):
        return remote(VA.at[3], VZ.at[k.z], v_send.at[3], v_recv.at[3], k.z_peer(step))

    hops = [vector_hop(n, peer) for n, peer in enumerate((k.c_peer, k.y_peer, k.x_peer))]

    def hop_in(n):
        hops[n].wait_recv()
        VA[n + 1] = VA[n] + VR[n]

    if stepped:
        weight_grad(X, DQKV, 0, 2, 3)
        hops[0].start()
        crossed[2].start()
        weight_grad(X, DQKV, 0, 0, 1)
        hop_in(0)
        hops[1].start()
        grads.start(0)
        weight_grad(X, DQKV, 0, 1, 2)
        grads.forward(3)
        grads.start(1)
    else:
        weight_grad(X, DQKV, 0, 0, 1)
        hops[0].start()
        weight_grad(X, DQKV, 0, 1, 2)
        grads.start(0)
        hop_in(0)
        hops[1].start()
        weight_grad(X, DQKV, 0, 2, 3)
        grads.start(1)
        grads.forward(6)
    r3 = reduce(3)
    r3.across(input_block(theirs, 1 - k.c))
    if stepped:
        crossed[2].relay()
    r3.theirs(input_block(theirs, k.c))
    hop_in(1)
    hops[2].start()
    if stepped:
        grads.forward(0)
        relay_back(3)
    else:
        grads.start(2)
        grads.forward(7)
    r3.partner(input_block(mine, 1 - k.c))
    r3.mine(input_block(mine, k.c))

    def send_last(step, carry):
        vector_last(step).start()
        return carry

    def vectors_along():
        hop_in(2)
        VZ[k.z] = VA[3]
        lax.fori_loop(1, outer, send_last, 0)

    if stepped:
        crossed[2].forward()
        relay_back(0)
        grads.forward(1)
        vectors_along()
        relay_back(1)
    else:
        for p in (8, 9, 10):
            grads.finish(p)
        grads.forward(3)
        grads.forward(0)
        grads.forward(1)
        vectors_along()
        grads.forward(2)
    r3.wait()

    def last(r):
        gin_ref[r, :] = GS[r, :] + r3.total(r)

    norm_loop(last)
    vz_all = VZ.at[pl.ds(0, outer - 1)]
    every = remote(vz_all, vz_all, v_send.at[3], v_recv.at[3], k.x_peer)

    def add(i, total):
        return total + VZ[i]

    def vectors_out():
        every.wait_recv()
        gvec_ref[...] = lax.fori_loop(1, outer, add, VZ[0])

    if stepped:
        down_g.finish(gd_ref)
        for p in (4, 5, 6):
            grads.finish(p)
        crossed[7].finish()
        for p in (3, 0):
            grads.finish(p)
        crossed[2].finish()
        vectors_out()
        grads.finish(1)
    else:
        for p in (11, 4, 5, 6, 7, 3, 0, 1):
            grads.finish(p)
        vectors_out()
        grads.finish(2)

    weights.drain(simple)
    grads.drain(simple)
    if stepped:
        down_w.drain()
        down_g.drain()
        for gradient in crossed.values():
            gradient.drain()
        s2.drain_columns(g_chunks)
    for s in (s0, s1, s3) if stepped else (s0, s1, s2, s3):
        s.drain()
    r3.drain()
    for hop in hops:
        hop.wait_send()
    every.wait_send()


def layer(outer, arrays):
    inputs, query_weight, up_weight = arrays[0], arrays[2], arrays[6]
    rows, model = inputs.shape
    shard_rows, width = query_weight.shape
    inner = up_weight.shape[1]
    heads = width // HEAD_DIM
    columns_all = 4 * width + 2 * inner
    pieces = columns_all // width
    seq = 2 * rows
    vmem = pl.BlockSpec(memory_space=pltpu.VMEM)
    anywhere = pl.BlockSpec(memory_space=pl.ANY)
    full = (outer, 2, shard_rows, columns_all)
    dma = pltpu.SemaphoreType.DMA
    outs = (
        jax.ShapeDtypeStruct((rows, model), BF16),
        jax.ShapeDtypeStruct((rows, model), F32),
        jax.ShapeDtypeStruct((shard_rows, width), F32),
        jax.ShapeDtypeStruct((shard_rows, width), F32),
        jax.ShapeDtypeStruct((shard_rows, width), F32),
        jax.ShapeDtypeStruct((width, shard_rows), F32),
        jax.ShapeDtypeStruct((shard_rows, inner), F32),
        jax.ShapeDtypeStruct((inner, shard_rows), F32),
        jax.ShapeDtypeStruct((VECTORS, model), F32),
    )
    return pl.pallas_call(
        functools.partial(body, outer),
        out_shape=outs,
        in_specs=[anywhere] * len(arrays),
        out_specs=(vmem,) * len(outs),
        scratch_shapes=[
            pltpu.VMEM(full, BF16),
            pltpu.VMEM(full, BF16),
            pltpu.VMEM((outer, shard_rows, columns_all), BF16),
            pltpu.VMEM((outer - 1, shard_rows, columns_all), BF16),
            pltpu.VMEM((4, rows, model), BF16),
            pltpu.VMEM((4, rows, model), BF16),
            pltpu.VMEM((4, rows, model), BF16),
            pltpu.VMEM((4, rows, model), BF16),
            pltpu.VMEM((2, seq, width), BF16),
            pltpu.VMEM((2, seq, width), BF16),
            pltpu.VMEM((2, seq, width), BF16),
            pltpu.VMEM((2, seq, width), BF16),
            pltpu.VMEM((seq, width), BF16),
            pltpu.VMEM((2, seq, 3 * width), BF16),
            pltpu.VMEM((2, heads, seq, seq), BF16),
            pltpu.VMEM((2, seq, inner), F32),
            pltpu.VMEM((2, seq, inner), BF16),
            pltpu.VMEM((2, seq, inner), BF16),
            pltpu.VMEM((rows, model), F32),
            pltpu.VMEM((rows, model), F32),
            pltpu.VMEM((rows, model), F32),
            pltpu.VMEM((rows, 128), F32),
            pltpu.VMEM((rows, model), F32),
            pltpu.VMEM((8, 8, model), F32),
            pltpu.VMEM((3, seq, width), F32),
            pltpu.VMEM((3, rows, model), BF16),
            pltpu.VMEM((3, rows, model), BF16),
            pltpu.VMEM((4, VECTORS, model), F32),
            pltpu.VMEM((3, VECTORS, model), F32),
            pltpu.VMEM((outer, VECTORS, model), F32),
            pltpu.VMEM((rows, model), BF16),
            pltpu.VMEM((width, shard_rows), BF16),
            pltpu.VMEM((inner, shard_rows), BF16),
            pltpu.VMEM((9, 4 * inner), F32),
            dma((4, pieces)),
            dma((4, pieces)),
            dma((4, pieces)),
            dma((4, pieces)),
            dma((4, 3)),
            dma((4, 3)),
            dma((4, 3)),
            dma((4, 3)),
            dma((4,)),
            dma((4,)),
            dma((len(arrays),)),
            pltpu.VMEM((shard_rows, columns_all), BF16),
            pltpu.VMEM((len(CROSSED_BACK), 3, 2, shard_rows, width), BF16),
            pltpu.VMEM((len(CROSSED_BACK), 2, shard_rows, width), BF16),
            pltpu.VMEM((len(CROSSED_BACK), shard_rows, width), BF16),
            (dma((outer, 2)),) * 4,
            (dma((outer,)),) * 4,
            (dma((3, outer)),) * 2,
            (dma((outer,)),) * 4,
        ],
        compiler_params=pltpu.CompilerParams(
            collective_id=0, has_side_effects=True, vmem_limit_bytes=67043328
        ),
        name="layer",
    )(*arrays)


def write_body(count, *refs):
    ins, outs, sem = refs[:9], refs[9 : 9 + count], refs[-1]
    vec = ins[8]
    pairs = list(zip(ins[:8], outs[:8]))
    single = [(0, 8), (1, 9), (2, 10), (7, 12), (8, 13), (9, 14), (10, 15), (11, 16), (12, 17)]
    pairs += [(vec.at[pl.ds(row, 1), :], outs[place]) for row, place in single]
    model = vec.shape[1]
    parts = outs[11].shape[1] // model
    for n in range(parts):
        pairs.append((vec.at[pl.ds(3 + n, 1), :], outs[11].at[:, pl.ds(n * model, model)]))
    copies = [pltpu.make_async_copy(src, dst, sem.at[n]) for n, (src, dst) in enumerate(pairs)]
    for copy in copies:
        copy.start()
    for copy in copies:
        copy.wait()


def write(values, up_length):
    model = values[8].shape[1]
    line = jax.ShapeDtypeStruct((1, model), F32)
    outs = [jax.ShapeDtypeStruct(v.shape, v.dtype) for v in values[:8]] + [line] * 10
    outs[11] = jax.ShapeDtypeStruct((1, up_length), F32)
    copies = 17 + up_length // model
    return pl.pallas_call(
        functools.partial(write_body, len(outs)),
        out_shape=tuple(outs),
        in_specs=[pl.BlockSpec(memory_space=pltpu.VMEM)] * len(values),
        out_specs=(pl.BlockSpec(memory_space=pl.ANY),) * len(outs),
        scratch_shapes=[pltpu.SemaphoreType.DMA((copies,))],
        name="write",
    )(*values)


def shards(*arrays):
    inputs = arrays[0]
    outer = lax.axis_size("dp") // 2
    arrays = arrays[:8] + tuple(v.reshape(1, -1) for v in arrays[8:])
    up_length = arrays[11].shape[1]
    values = write(layer(outer, arrays), up_length)
    token_total = inputs.shape[0] * lax.axis_size("dp") * lax.axis_size("tensor")
    loss = jnp.sum(values[17]) * (0.5 / token_total)
    output, grad_inputs, gq, gk, gv, go, gu, gd = values[:8]
    return (output, loss, grad_inputs, gq, gk, gv, go, gu, gd) + tuple(
        v.reshape(-1) for v in values[8:17]
    )


def solution(mesh):
    tokens = P(("dp", "tensor"), None)
    across, down = P("dp", "tensor"), P("tensor", "dp")
    in_specs = (tokens, tokens, across, across, across, down, across, down) + (P(),) * 9
    out_specs = (tokens, P(), tokens, across, across, across, down, across, down) + (P(),) * 9
    return jax.shard_map(shards, mesh=mesh, in_specs=in_specs, out_specs=out_specs, check_vma=False)
```

```python
import functools
import math

import jax
import jax.numpy as jnp
from jax import lax
from jax.experimental import pallas as pl
from jax.experimental.pallas import tpu as pltpu
from jax.sharding import PartitionSpec as P

HEAD_DIM = 64
SEQ = 512
EPSILON = 1e-05
MESH = pl.DeviceIdType.MESH
F32 = jnp.float32
BF16 = jnp.bfloat16
NN = ((1,), (0,))
NT = ((1,), (1,))
TN = ((0,), (0,))
CHUNK = 128
WINDOW = 2
CROSSED = (3, 7)
CROSSED_BACK = (2, 7)
ROOT_TWO = math.sqrt(2.0)
ROOT_TWO_PI = math.sqrt(2.0 * math.pi)
VECTORS = 16


def dot(left, right, dims):
    return lax.dot_general(left, right, (dims, ((), ())), preferred_element_type=F32)


def remote(src, dst, send, recv, peer):
    return pltpu.make_async_remote_copy(
        src_ref=src, dst_ref=dst, send_sem=send, recv_sem=recv, device_id=peer, device_id_type=MESH
    )


class Place:
    def __init__(self, outer):
        self.outer = outer
        self.dp = lax.axis_index("dp")
        self.t = lax.axis_index("tensor")
        self.z, self.x = self.dp // 2, self.dp % 2
        self.y, self.c = self.t // 2, self.t % 2
        self.x_peer = (self.z * 2 + 1 - self.x, self.t)
        self.y_peer = (self.dp, (1 - self.y) * 2 + self.c)
        self.c_peer = (self.dp, self.y * 2 + 1 - self.c)
        self.diag = (1 - self.y) * 2 + 1 - self.c
        self.diag_peer = (self.dp, self.diag)

    def z_peer(self, step):
        return (lax.rem(self.z + step, self.outer) * 2 + self.x, self.t)

    def greet(self):
        barrier = pltpu.get_barrier_semaphore()

        def one(step, carry):
            pl.semaphore_signal(barrier, inc=1, device_id=self.z_peer(step), device_id_type=MESH)
            return carry

        lax.fori_loop(1, self.outer, one, 0)
        for peer in (self.x_peer, self.y_peer, self.diag_peer, self.c_peer):
            pl.semaphore_signal(barrier, inc=1, device_id=peer, device_id_type=MESH)

    def enter(self):
        pl.semaphore_wait(pltpu.get_barrier_semaphore(), self.outer + 3)


def columns(piece, width):
    start = piece * width
    if not isinstance(start, int):
        start = pl.multiple_of(start, width)
    return pl.ds(start, width)


class Weights:
    def __init__(self, k, full, send, recv, width, pieces):
        self.k, self.full, self.send, self.recv, self.width = k, full, send, recv, width
        self.pieces = pieces

    def first(self, p, step):
        block = self.full.at[self.k.z, self.k.x, :, columns(p, self.width)]
        return remote(block, block, self.send.at[0, p], self.recv.at[0, p], self.k.z_peer(step))

    def all_first(self, p):
        block = self.full.at[pl.ds(0, self.k.outer - 1), 0, :, columns(p, self.width)]
        return remote(block, block, self.send.at[0, p], self.recv.at[0, p], self.k.x_peer)

    def second(self, p):
        block = self.full.at[:, self.k.x, :, columns(p, self.width)]
        return remote(block, block, self.send.at[1, p], self.recv.at[1, p], self.k.x_peer)

    def start(self, p):
        def one(step, carry):
            self.first(p, step).start()
            return carry

        lax.fori_loop(1, self.k.outer, one, 0)

    def forward(self, p):
        self.all_first(p).wait_recv()
        self.second(p).start()
        if p + WINDOW < self.pieces:
            self.start(p + WINDOW)

    def arrive(self, p):
        self.second(p).wait_recv()

    def drain(self, pieces):
        def piece(p, carry):
            self.all_first(p).wait_send()
            self.second(p).wait_send()
            return carry

        lax.fori_loop(0, pieces, piece, 0)


class Gradients:
    def __init__(self, k, part, near, far, out, send, recv, width):
        self.k, self.part, self.near, self.far, self.out = k, part, near, far, out
        self.send, self.recv, self.width = send, recv, width

    def one(self, p):
        k, cols = self.k, columns(p, self.width)
        return remote(
            self.part.at[:, 1 - k.x, :, cols],
            self.near.at[:, :, cols],
            self.send.at[0, p],
            self.recv.at[0, p],
            k.x_peer,
        )

    def two(self, p, step):
        k, cols = self.k, columns(p, self.width)
        return remote(
            self.part.at[lax.rem(k.z + step, k.outer), k.x, :, cols],
            self.far.at[step - 1, :, cols],
            self.send.at[1, p],
            self.recv.at[1, p],
            k.z_peer(step),
        )

    def all_two(self, p):
        block = self.far.at[:, :, columns(p, self.width)]
        return remote(block, block, self.send.at[1, p], self.recv.at[1, p], self.k.x_peer)

    def start(self, p):
        self.one(p).start()

    def forward(self, p):
        k, cols = self.k, columns(p, self.width)
        self.one(p).wait_recv()
        here = self.part[:, k.x, :, cols].astype(F32)
        self.part[:, k.x, :, cols] = (here + self.near[:, :, cols].astype(F32)).astype(BF16)

        def send(step, carry):
            self.two(p, step).start()
            return carry

        lax.fori_loop(1, k.outer, send, 0)

    def finish(self, p):
        k, cols = self.k, columns(p, self.width)
        self.all_two(p).wait_recv()

        def add(i, total):
            return total + self.far[i, :, cols].astype(F32)

        total = self.part[k.z, k.x, :, cols].astype(F32)
        total = lax.fori_loop(0, k.outer - 1, add, total)
        self.out(p, total)

    def drain(self, pieces):
        def piece(p, carry):
            self.one(p).wait_send()
            self.all_two(p).wait_send()
            return carry

        lax.fori_loop(0, pieces, piece, 0)


class Line:
    def __init__(self, k):
        self.k = k
        self.two = lax.rem(k.z + 2, 4)
        self.next = k.z + 1 - 2 * lax.rem(k.z, 2)
        self.third = 3 - k.z
        self.middle = (k.z == 1) | (k.z == 2)
        self.end = (k.z == 0) | (k.z == 3)

    def peer(self, z):
        return (z * 2 + self.k.x, self.k.t)


class LineWeights(Weights):
    def __init__(self, line, *rest):
        super().__init__(line.k, *rest)
        self.line = line

    def shards(self, z, p):
        return self.full.at[z, slice(None) if p in CROSSED else self.k.x, :, columns(p, self.width)]

    def send_to(self, z, source, send, recv, p):
        block = self.shards(source, p)
        return remote(
            block, block, self.send.at[send, p], self.recv.at[recv, p], self.line.peer(z)
        )

    def some(self, count, send, recv, p):
        block = self.shards(pl.ds(0, count), p)
        return remote(block, block, self.send.at[send, p], self.recv.at[recv, p], self.k.x_peer)

    def crossing(self, p):
        block = self.full.at[self.k.z, self.k.x, :, columns(p, self.width)]
        return remote(block, block, self.send.at[1, p], self.recv.at[1, p], self.k.x_peer)

    def cross(self):
        for p in CROSSED:
            self.crossing(p).start()

    def over(self, z, p):
        block = self.full.at[z, self.k.x, :, columns(p, self.width)]
        return remote(block, block, self.send.at[1, p], self.recv.at[1, p], self.k.x_peer)

    def start(self, p):
        line = self.line
        if p in CROSSED:
            self.crossing(p).wait_recv()
        else:
            self.over(self.k.z, p).start()
        self.send_to(line.two, self.k.z, 0, 0, p).start()
        self.send_to(line.next, self.k.z, 0, 0, p).start()

        @pl.when(line.middle)
        def _():
            self.send_to(line.third, self.k.z, 2, 2, p).start()

    def relay(self, p):
        line = self.line
        self.some(2, 0, 0, p).wait_recv()

        @pl.when(line.middle)
        def _():
            self.send_to(line.next, line.two, 3, 2, p).start()

        if p not in CROSSED:
            self.over(line.two, p).start()
            self.over(line.next, p).start()
        if p + WINDOW < self.pieces:
            self.start(p + WINDOW)

    def forward(self, p):
        if p not in CROSSED:
            self.some(1, 2, 2, p).wait_recv()
            self.over(self.line.third, p).start()

    def arrive(self, p):
        if p in CROSSED:
            self.some(1, 2, 2, p).wait_recv()
        else:
            self.second(p).wait_recv()

    def drain(self, pieces):
        for p in range(pieces):
            self.some(2, 0, 0, p).wait_send()
            (self.crossing(p) if p in CROSSED else self.second(p)).wait_send()

        @pl.when(self.line.middle)
        def _():
            for p in range(pieces):
                self.some(1, 2, 2, p).wait_send()
                self.some(1, 3, 2, p).wait_send()


class CrossedGradient:
    def __init__(self, line, part, far, hop, last, out, send, recv, width, p, place):
        self.line, self.k, self.part, self.out, self.p = line, line.k, part, out, p
        self.far, self.hop, self.last = far.at[place], hop.at[place], last.at[place]
        self.cols = columns(p, width)
        self.send, self.recv = send, recv

    def along(self, z, dst, send, recv, peer):
        return remote(
            self.part.at[z, :, :, self.cols],
            dst,
            self.send.at[send, self.p],
            self.recv.at[recv, self.p],
            self.line.peer(peer),
        )

    def to(self, z, slot, send, recv):
        return self.along(z, self.far.at[slot], send, recv, z)

    def to_hop(self):
        return self.along(self.line.third, self.hop, 2, 3, self.line.next)

    def over(self):
        return remote(
            self.part.at[self.k.z, 1 - self.k.x, :, self.cols],
            self.last,
            self.send.at[0, self.p],
            self.recv.at[0, self.p],
            self.k.x_peer,
        )

    def start(self):
        line = self.line

        @pl.when(line.end)
        def _():
            self.to_hop().start()
            self.to(line.two, 0, 3, 1).start()

        @pl.when(line.middle)
        def _():
            self.to(line.third, 2, 2, 2).start()

        self.to(line.next, 1, 1, 1).start()

    def relay(self):
        line = self.line

        @pl.when(line.middle)
        def _():
            self.to_hop().wait_recv()
            here = self.part[line.two, :, :, self.cols].astype(F32) + self.hop[...].astype(F32)
            self.part[line.two, :, :, self.cols] = here.astype(BF16)
            self.to(line.two, 0, 3, 1).start()

    def total(self, x):
        total = self.part[self.k.z, x, :, self.cols].astype(F32)
        for n in range(3):
            total = total + self.far[n, x].astype(F32)
        return total

    def forward(self):
        line = self.line
        both = self.far.at[pl.ds(0, 2)]
        remote(both, both, self.send.at[1, self.p], self.recv.at[1, self.p], self.k.x_peer).wait_recv()

        @pl.when(line.middle)
        def _():
            self.to(line.third, 2, 2, 2).wait_recv()

        x = 1 - self.k.x
        self.part[self.k.z, x, :, self.cols] = self.total(x).astype(BF16)
        self.over().start()

    def finish(self):
        self.over().wait_recv()
        self.out(self.p, self.total(self.k.x) + self.last[...].astype(F32))

    def drain(self):
        line = self.line
        self.over().wait_send()
        for z, sem in ((line.next, 1), (line.third, 2), (line.two, 3)):
            self.to(z, 0, sem, 1).wait_send()


class LineGradients(Gradients):
    def __init__(self, line, hop, x_send, x_recv, *rest):
        super().__init__(line.k, *rest)
        self.line, self.hop, self.x_send, self.x_recv = line, hop, x_send, x_recv
        self.targets = (line.third, line.two, line.next, line.k.z)

    def over(self, p, n):
        k, z, cols = self.k, self.targets[n], columns(p, self.width)
        return remote(
            self.part.at[z, 1 - k.x, :, cols],
            self.near.at[z, :, cols],
            self.x_send.at[n, p],
            self.x_recv.at[n, p],
            k.x_peer,
        )

    def start(self, p):
        for n in range(4):
            self.over(p, n).start()

    def to(self, z, dst, send, recv, p):
        cols = columns(p, self.width)
        return remote(
            self.part.at[z, self.k.x, :, cols],
            dst.at[:, cols],
            self.send.at[send, p],
            self.recv.at[recv, p],
            self.line.peer(z),
        )

    def to_hop(self, p):
        cols = columns(p, self.width)
        return remote(
            self.part.at[self.line.third, self.k.x, :, cols],
            self.hop.at[:, cols],
            self.send.at[2, p],
            self.recv.at[3, p],
            self.line.peer(self.line.next),
        )

    def forward(self, p):
        k, line, cols = self.k, self.line, columns(p, self.width)
        for n in range(4):
            z = self.targets[n]
            self.over(p, n).wait_recv()
            here = self.part[z, k.x, :, cols].astype(F32)
            self.part[z, k.x, :, cols] = (here + self.near[z, :, cols].astype(F32)).astype(BF16)
            if n == 0:

                @pl.when(line.end)
                def _():
                    self.to_hop(p).start()

                @pl.when(line.middle)
                def _():
                    self.to(line.third, self.far.at[2], 2, 2, p).start()

            elif n == 1:

                @pl.when(line.end)
                def _():
                    self.to(line.two, self.far.at[0], 3, 1, p).start()

            elif n == 2:
                self.to(line.next, self.far.at[1], 1, 1, p).start()

    def relay(self, p):
        line, cols = self.line, columns(p, self.width)

        @pl.when(line.middle)
        def _():
            self.to_hop(p).wait_recv()
            here = self.part[line.two, self.k.x, :, cols].astype(F32)
            here = here + self.hop[:, cols].astype(F32)
            self.part[line.two, self.k.x, :, cols] = here.astype(BF16)
            self.to(line.two, self.far.at[0], 3, 1, p).start()

    def finish(self, p):
        k, line, cols = self.k, self.line, columns(p, self.width)
        both = self.far.at[pl.ds(0, 2), :, cols]
        remote(both, both, self.send.at[1, p], self.recv.at[1, p], k.x_peer).wait_recv()

        @pl.when(line.middle)
        def _():
            self.to(line.third, self.far.at[2], 2, 2, p).wait_recv()

        total = self.part[k.z, k.x, :, cols].astype(F32)
        for n in range(3):
            total = total + self.far[n, :, cols].astype(F32)
        self.out(p, total)

    def drain(self, pieces):
        line = self.line
        for p in range(pieces):
            if p in CROSSED_BACK:
                continue
            for n in range(4):
                self.over(p, n).wait_send()
            for z, sem in ((line.next, 1), (line.third, 2), (line.two, 3)):
                self.to(z, self.far.at[0], sem, 1, p).wait_send()


class Spread:
    def __init__(self, k, blocks, send, recv, phase):
        self.k, self.blocks, self.send, self.recv, self.phase = k, blocks, send, recv, phase

    def copy(self, number, block, peer):
        ref = self.blocks.at[block]
        return remote(
            ref, ref, self.send.at[self.phase, number], self.recv.at[self.phase, number], peer
        )

    def near(self):
        return self.copy(0, self.k.t, self.k.c_peer)

    def far(self):
        return self.copy(1, self.k.t, self.k.diag_peer)

    def relay(self):
        return self.copy(2, self.k.diag, self.k.c_peer)

    def start(self):
        self.far().start()
        self.near().start()

    def own(self):
        self.near().wait_recv()

    def pass_on(self):
        self.far().wait_recv()
        self.relay().start()

    def other(self):
        self.relay().wait_recv()

    def drain(self):
        self.near().wait_send()
        self.far().wait_send()
        self.relay().wait_send()


class SpreadColumns(Spread):
    def __init__(self, k, blocks, send, recv, phase, chunks, far_sems):
        super().__init__(k, blocks, send, recv, phase)
        self.chunks = chunks
        self.far_send, self.far_recv, self.relay_send, self.relay_recv = far_sems

    def cols(self, chunk):
        width = self.blocks.shape[2] // self.chunks
        return pl.ds(pl.multiple_of(chunk * width, width), width)

    def far_part(self, n, chunk):
        ref = self.blocks.at[self.k.t, :, self.cols(chunk)]
        return remote(ref, ref, self.far_send.at[n], self.far_recv.at[n], self.k.diag_peer)

    def relay_part(self, n, chunk):
        ref = self.blocks.at[self.k.diag, :, self.cols(chunk)]
        return remote(ref, ref, self.relay_send.at[n], self.relay_recv.at[n], self.k.c_peer)

    def start_columns(self, order):
        self.near().start()
        for n, chunk in enumerate(order):
            self.far_part(n, chunk).start()

    def pass_part(self, n, chunk):
        self.far_part(n, chunk).wait_recv()
        self.relay_part(n, chunk).start()

    def other_part(self, n, chunk):
        self.relay_part(n, chunk).wait_recv()

    def drain_columns(self, order):
        self.near().wait_send()
        for n, chunk in enumerate(order):
            self.far_part(n, chunk).wait_send()
            self.relay_part(n, chunk).wait_send()


class Reduce:
    def __init__(self, k, out, inbox, keep, send, recv, phase):
        self.k, self.out, self.inbox, self.keep = k, out, inbox, keep
        self.send, self.recv, self.phase = send, recv, phase

    def copy(self, number, phase=None):
        peer = self.k.y_peer if number == 2 else self.k.c_peer
        phase = self.phase if phase is None else phase
        return remote(
            self.out.at[number],
            self.inbox.at[number],
            self.send.at[phase, number],
            self.recv.at[phase, number],
            peer,
        )

    phase_free = True

    def free(self, number):
        if self.phase > 0 and self.phase_free:
            self.copy(number, self.phase - 1).wait_send()

    def across(self, value):
        self.free(0)
        self.out[0] = value.astype(BF16)
        self.copy(0).start()

    def theirs(self, value):
        self.free(2)
        self.copy(0).wait_recv()
        self.out[2] = (value + self.inbox[0].astype(F32)).astype(BF16)
        self.copy(2).start()

    def partner(self, value):
        self.free(1)
        self.out[1] = value.astype(BF16)
        self.copy(1).start()

    def mine(self, value):
        self.keep[...] = value

    def wait(self):
        self.copy(1).wait_recv()
        self.copy(2).wait_recv()

    def total(self, rows):
        return self.keep[rows, :] + (
            self.inbox[1, rows, :].astype(F32) + self.inbox[2, rows, :].astype(F32)
        )

    def drain(self):
        for number in range(3):
            self.copy(number).wait_send()


class ReduceColumns(Reduce):
    def __init__(self, k, out, inbox, keep, send, recv, phase, chunks, sems):
        super().__init__(k, out, inbox, keep, send, recv, phase)
        self.chunks, self.part_send, self.part_recv = chunks, sems[0], sems[1]

    def cols(self, chunk):
        width = self.keep.shape[1] // self.chunks
        return pl.ds(pl.multiple_of(chunk * width, width), width)

    def part(self, number, n, chunk):
        cols = self.cols(chunk)
        return remote(
            self.out.at[number, :, cols],
            self.inbox.at[number, :, cols],
            self.part_send.at[number, n],
            self.part_recv.at[number, n],
            self.k.y_peer if number == 2 else self.k.c_peer,
        )

    def step(self, n, chunk, block):
        cols = self.cols(chunk)
        if n == 0:
            for number in range(3):
                self.free(number)
        self.out[0, :, cols] = block("across").astype(BF16)
        self.part(0, n, chunk).start()
        self.out[1, :, cols] = block("partner").astype(BF16)
        self.part(1, n, chunk).start()
        value = block("theirs")
        self.part(0, n, chunk).wait_recv()
        self.out[2, :, cols] = (value + self.inbox[0, :, cols].astype(F32)).astype(BF16)
        self.part(2, n, chunk).start()
        self.keep[:, cols] = block("mine")

    def wait_columns(self, order):
        for n, chunk in enumerate(order):
            self.part(1, n, chunk).wait_recv()
            self.part(2, n, chunk).wait_recv()

    def drain_columns(self, order):
        for n, chunk in enumerate(order):
            for number in range(3):
                self.part(number, n, chunk).wait_send()


EARLY_ROWS = {2: (0, 0), 7: (0, 1), 8: (0, 2), 9: (0, 3), 10: (2, 0), 11: (2, 1), 12: (2, 2)}
EARLY_ROWS.update({3 + n: (1, n) for n in range(4)})


class Early:
    def __init__(self, k, sums, inbox, cross, along, total, sems):
        self.k, self.sums, self.inbox, self.cross = k, sums, inbox, cross
        self.along, self.total, (self.send, self.recv) = along, total, sems

    def copy(self, n, src, dst, peer):
        return remote(src, dst, self.send.at[n], self.recv.at[n], peer)

    def hop(self, n):
        peer = self.k.c_peer if n == 0 else self.k.y_peer
        rows = pl.ds(0, 4)
        return self.copy(n, self.sums.at[n, :, rows], self.inbox.at[n, :, rows], peer)

    def over(self):
        rows = pl.ds(0, 4)
        return self.copy(
            2, self.sums.at[2, self.k.t, rows], self.cross.at[0, rows], self.k.x_peer
        )

    def last(self, step):
        rows = pl.ds(0, 4)
        return self.copy(
            3, self.cross.at[1, rows], self.along.at[self.k.z, rows], self.k.z_peer(step)
        )

    def every(self):
        block = self.along.at[pl.ds(0, self.k.outer - 1), pl.ds(0, 4)]
        return self.copy(3, block, block, self.k.x_peer)

    def share(self, n):
        k = self.k
        block = self.total.at[k.t, pl.ds(0, 4)]
        return self.copy(4 + n, block, block, (k.c_peer, k.y_peer, k.diag_peer)[n])

    def add(self, n):
        self.hop(n).wait_recv()
        self.sums[n + 1, :, 0:4, :] = self.sums[n, :, 0:4, :] + self.inbox[n, :, 0:4, :]

    def add_over(self):
        k = self.k
        self.over().wait_recv()
        total = self.sums[2, k.t, 0:4, :] + self.cross[0, 0:4, :]
        self.cross[1, 0:4, :] = total
        self.along[k.z, 0:4, :] = total

        def send(step, carry):
            self.last(step).start()
            return carry

        lax.fori_loop(1, k.outer, send, 0)

    def add_along(self):
        self.every().wait_recv()

        def add(i, total):
            return total + self.along[i, 0:4, :]

        first = self.along[0, 0:4, :]
        self.total[self.k.t, 0:4, :] = lax.fori_loop(1, self.k.outer, add, first)
        for n in range(3):
            self.share(n).start()

    def finish(self):
        for n in range(3):
            self.share(n).wait_recv()

    def drain(self):
        self.hop(0).wait_send()
        self.hop(1).wait_send()
        self.over().wait_send()
        self.every().wait_send()
        for n in range(3):
            self.share(n).wait_send()


class DownWeights:
    HALVES = 2

    def __init__(self, line, full, start, size, sems):
        self.line, self.k = line, line.k
        self.full, self.start_at, self.half = full, start, size // self.HALVES
        self.z_send, self.z_recv, self.x_send, self.x_recv = sems
        self.sources = (self.k.z, line.two, line.next, line.third)

    def shard(self, z, x, half):
        return self.full.at[z, x, :, pl.ds(self.start_at + half * self.half, self.half)]

    def along(self, z, source, send, recv, half):
        block = self.shard(source, self.k.x, half)
        sems = (self.z_send.at[send, half], self.z_recv.at[recv, half])
        return remote(block, block, *sems, self.line.peer(z))

    def across(self, step, half, x):
        block = self.shard(self.sources[step], x, half)
        sems = (self.x_send.at[step, half], self.x_recv.at[step, half])
        return remote(block, block, *sems, self.k.x_peer)

    def start(self, step):
        z = self.sources[step]
        for half in range(self.HALVES):
            if step < 3:
                self.along(z, self.k.z, step, step, half).start()
            else:

                @pl.when(self.line.middle)
                def _():
                    self.along(z, self.k.z, 3, 3, half).start()

    def forward(self, step):
        for half in range(self.HALVES):
            if step > 0:
                self.along(self.line.next, self.k.z, step, step, half).wait_recv()
            if step == 1:

                @pl.when(self.line.middle)
                def _():
                    self.along(self.line.next, self.line.two, 0, 3, half).start()

            self.across(step, half, self.k.x).start()

    def arrive(self, step):
        for half in range(self.HALVES):
            self.across(step, half, 1 - self.k.x).wait_recv()

    def drain(self):
        for half in range(self.HALVES):
            for step in range(4):
                self.across(step, half, self.k.x).wait_send()
            for step in (1, 2):
                self.along(self.line.next, self.k.z, step, step, half).wait_send()

            @pl.when(self.line.middle)
            def _():
                for sem in (3, 0):
                    self.along(self.line.next, self.k.z, sem, 3, half).wait_send()


class DownGradient:
    def __init__(self, line, part, near, far, hop, start, size, sems):
        self.line, self.k = line, line.k
        self.part, self.near, self.far, self.hop = part, near, far, hop
        self.cols = pl.ds(start, size)
        self.x_send, self.x_recv, self.z_send, self.z_recv = sems
        self.targets = (line.third, line.next, line.two, self.k.z)

    def one(self, step):
        z = self.targets[step]
        return remote(
            self.part.at[z, 1 - self.k.x, :, self.cols],
            self.near.at[z, :, self.cols],
            self.x_send.at[step],
            self.x_recv.at[step],
            self.k.x_peer,
        )

    def along(self, step, dst, recv, peer):
        return remote(
            self.part.at[self.targets[step], self.k.x, :, self.cols],
            dst.at[:, self.cols],
            self.z_send.at[step],
            self.z_recv.at[recv],
            self.line.peer(peer),
        )

    def start(self, step):
        self.one(step).start()

    def forward(self, step):
        k, line, z = self.k, self.line, self.targets[step]
        self.one(step).wait_recv()
        here = self.part[z, k.x, :, self.cols].astype(F32)
        here = here + self.near[z, :, self.cols].astype(F32)
        if step != 2:
            self.part[z, k.x, :, self.cols] = here.astype(BF16)
        if step == 0:

            @pl.when(line.end)
            def _():
                self.along(0, self.hop, 3, line.next).start()

            @pl.when(line.middle)
            def _():
                self.along(0, self.far.at[2], 0, line.third).start()

        if step == 1:
            self.along(1, self.far.at[1], 1, line.next).start()
        if step == 2:

            @pl.when(line.end)
            def _():
                self.part[z, k.x, :, self.cols] = here.astype(BF16)

            @pl.when(line.middle)
            def _():
                self.along(0, self.hop, 3, line.next).wait_recv()
                both = here + self.hop[:, self.cols].astype(F32)
                self.part[z, k.x, :, self.cols] = both.astype(BF16)

            self.along(2, self.far.at[0], 2, line.two).start()

    def finish(self, out):
        k = self.k

        @pl.when(self.line.middle)
        def _():
            self.along(0, self.far.at[2], 0, k.z).wait_recv()

        total = self.part[k.z, k.x, :, self.cols].astype(F32)
        for n in range(3):
            if n < 2:
                self.along(0, self.far.at[n], 2 - n, k.z).wait_recv()
            total = total + self.far[n, :, self.cols].astype(F32)
        out[...] = total.T

    def drain(self):
        for step in range(4):
            self.one(step).wait_send()
            if step < 3:
                self.along(step, self.far.at[0], 0, self.k.z).wait_send()


def fold(values):
    rows, width = values.shape
    return jnp.sum(values.reshape(rows // 8, 8, width), axis=0)


def mean(values):
    return jnp.sum(values, axis=-1, keepdims=True) * (1.0 / values.shape[-1])


def body(
    outer,
    x_in,
    teacher_in,
    qw_in,
    kw_in,
    vw_in,
    ow_in,
    uw_in,
    dw_in,
    qb_in,
    vb_in,
    ob_in,
    ub_in,
    db_in,
    g1_in,
    b1_in,
    g2_in,
    b2_in,
    out_ref,
    gin_ref,
    gq_ref,
    gk_ref,
    gv_ref,
    go_ref,
    gu_ref,
    gd_ref,
    gvec_ref,
    W,
    G,
    near,
    far,
    X,
    H,
    MX,
    GF,
    Q,
    K,
    V,
    C,
    GC,
    DQKV,
    PT,
    SL,
    ACT,
    GU,
    OWN,
    HID,
    N1,
    R1,
    GS,
    SUMS,
    ACC,
    OUTBOX,
    INBOX,
    VA,
    VR,
    VZ,
    EA,
    EC,
    EX,
    EZ,
    ET,
    TEACH,
    OT,
    DT,
    VEC,
    w_send,
    w_recv,
    g_send,
    g_recv,
    s_send,
    s_recv,
    r_send,
    r_recv,
    v_send,
    v_recv,
    load_sem,
    HOP,
    CFAR,
    CHOP,
    CLAST,
    gx_send,
    gx_recv,
    early_sems,
    dw_sems,
    dg_sems,
    rc_sems,
    sc_sems,
):
    k = Place(outer)
    rows, model = x_in.shape
    width = Q.shape[2]
    inner = ACT.shape[2]
    heads = width // HEAD_DIM
    steps = inner // width
    up_piece = 4
    down_piece = 4 + steps
    pieces = 4 + 2 * steps
    scale = 1.0 / math.sqrt(HEAD_DIM)
    mine, theirs = k.y, 1 - k.y

    own = W.at[k.z, k.x]
    loads = []

    def load(src, dst):
        copy = pltpu.make_async_copy(src, dst, load_sem.at[len(loads)])
        copy.start()
        loads.append(copy)

    load(x_in, X.at[k.t])
    load(qw_in, own.at[:, columns(0, width)])
    load(kw_in, own.at[:, columns(1, width)])
    load(vw_in, own.at[:, columns(2, width)])
    load(ow_in, OT)
    load(uw_in, own.at[:, pl.ds(4 * width, inner)])
    load(dw_in, DT)
    load(teacher_in, TEACH)
    for row, ref in enumerate((qb_in, vb_in, ob_in, db_in, g1_in, b1_in, g2_in, b2_in)):
        load(ref, VEC.at[pl.ds(row, 1), pl.ds(0, model)])
    load(ub_in, VEC.at[pl.ds(8, 1), :])
    k.greet()


    def keep(p, total):
        if p < 3:
            (gq_ref, gk_ref, gv_ref)[p][...] = total
        elif p == 3:
            go_ref[...] = total.T
        elif p < down_piece:
            gu_ref[:, (p - up_piece) * width : (p - up_piece + 1) * width] = total
        else:
            gd_ref[(p - down_piece) * width : (p - down_piece + 1) * width, :] = total.T

    stepped = outer == 4 and (model // outer) % 128 == 0
    simple = down_piece if stepped else pieces
    if stepped:
        line = Line(k)
        weights = LineWeights(line, W, w_send, w_recv, width, simple)
        grads = LineGradients(line, HOP, gx_send, gx_recv, G, near, far, keep, g_send, g_recv, width)
        crossed = {
            p: CrossedGradient(
                line, G, CFAR, CHOP, CLAST, keep, g_send, g_recv, width, p, place
            )
            for place, p in enumerate(CROSSED_BACK)
        }
        down_w = DownWeights(line, W, down_piece * width, inner, dw_sems)
        down_g = DownGradient(line, G, near, far, HOP, down_piece * width, inner, dg_sems)
        w_chunks, g_chunks = down_w.sources, down_g.targets
    else:
        weights = Weights(k, W, w_send, w_recv, width, simple)
        grads = Gradients(k, G, near, far, keep, g_send, g_recv, width)

    def relay(p):
        if stepped and p < simple:
            weights.relay(p)

    def relay_back(p):
        if stepped:
            grads.relay(p)

    def spread(blocks, phase):
        return Spread(k, blocks, s_send, s_recv, phase)

    def reduce(phase):
        return Reduce(k, OUTBOX, INBOX, OWN, r_send, r_recv, phase)

    def matrix(start, size):
        return W[:, :, :, pl.ds(start, size)].reshape(model, size)

    def vector(row):
        return VEC[row : row + 1, 0:model]

    def pair(blocks, seq):
        return blocks[pl.ds(2 * seq, 2)].reshape(2 * rows, model)

    def part_rows(core):
        return pl.ds(pl.multiple_of(core * rows, rows), rows)

    def norm_loop(step):
        def one(i, carry):
            step(pl.ds(pl.multiple_of(i * CHUNK, CHUNK), CHUNK))
            return carry

        lax.fori_loop(0, rows // CHUNK, one, 0)

    SUMS[...] = jnp.zeros_like(SUMS)
    VA[0] = jnp.zeros_like(VA[0])
    EA[0] = jnp.zeros_like(EA[0])
    if stepped:
        far[2] = jnp.zeros_like(far[2])
        for place in range(len(CROSSED_BACK)):
            CFAR[place, 2] = jnp.zeros_like(CFAR[place, 2])
    for copy in loads[:4]:
        copy.wait()
    s0 = spread(X, 0)
    k.enter()
    for p in range(WINDOW):
        weights.start(p)
    s0.start()
    for copy in loads[4:]:
        copy.wait()
    own[:, columns(3, width)] = OT[...].T
    own[:, pl.ds(4 * width + inner, inner)] = DT[...].T
    if stepped:
        weights.cross()

    def project(p, held):
        weights.arrive(p)
        for seq in range(2):
            tokens = X[2 * seq : 2 * seq + 2].reshape(2 * rows, model)
            product = dot(tokens, matrix(p * width, width), NN)
            if p != 1:
                here = pl.ds(pl.multiple_of(k.t * width, width), width)
                product = product + VEC[p // 2 : p // 2 + 1, here]
            held[seq] = product.astype(BF16)

    def head_mask(h):
        lane = lax.broadcasted_iota(jnp.int32, (1, width), 1)
        inside = (lane >= h * HEAD_DIM) & (lane < (h + 1) * HEAD_DIM)
        return jnp.where(inside, 1.0, 0.0).astype(BF16)

    def attend(seq, between=lambda: None):
        ACC[0] = jnp.zeros_like(ACC[0])

        def head(h, carry):
            mask = head_mask(h)
            scores = dot(K[seq], Q[seq] * mask, NT) * scale
            raised = jnp.exp(scores - jnp.max(scores, axis=0, keepdims=True))
            probs = (raised * (1.0 / jnp.sum(raised, axis=0, keepdims=True))).astype(BF16)
            PT[seq, h] = probs
            ACC[0] += dot(probs, V[seq] * mask, TN)
            return carry

        lax.fori_loop(0, heads // 2, head, 0)
        between()
        lax.fori_loop(heads // 2, heads, head, 0)
        C[seq] = ACC[0].astype(BF16)

    def out_block(seq, core):
        return dot(C[seq, part_rows(core), :], matrix(3 * width, width), NT)

    relay(0)
    weights.forward(0)
    relay(1)
    weights.forward(1)
    relay(2)
    s0.pass_on()
    s0.own()
    s0.other()
    project(0, Q)
    weights.forward(2)
    project(1, K)
    relay(3)
    if not stepped:
        weights.forward(3)
    project(2, V)
    r0 = reduce(0)
    attend(theirs, lambda: relay(4))
    weights.forward(4)
    weights.arrive(3)
    r0.across(out_block(theirs, 1 - k.c))
    r0.theirs(out_block(theirs, k.c))
    relay(5)
    attend(mine, lambda: weights.forward(5))
    relay(6)
    r0.partner(out_block(mine, 1 - k.c))
    r0.mine(out_block(mine, k.c))
    weights.forward(6)
    relay(7)
    if stepped:
        down_w.forward(0)
        down_w.start(1)
        down_w.start(2)
        down_w.start(3)
    r0.wait()

    def first_norm(r):
        first = X[k.t, r, :].astype(F32) + r0.total(r) + vector(2)
        center = first - mean(first)
        scaling = lax.rsqrt(mean(center * center) + EPSILON)
        normed = center * scaling
        hidden = normed * vector(4) + vector(5)
        N1[r, :] = normed
        R1[r, :] = jnp.broadcast_to(scaling, (CHUNK, R1.shape[1]))
        HID[r, :] = hidden
        H[k.t, r, :] = hidden.astype(BF16)

    norm_loop(first_norm)
    s1 = spread(H, 1)
    s1.start()
    weights.forward(7)
    if not stepped:
        weights.forward(8)
    s1.own()
    for p in range(up_piece, down_piece):
        weights.arrive(p)

    def up(seq):
        def part(n, carry):
            cols = pl.ds(pl.multiple_of(n * width, width), width)
            wide = pl.ds(pl.multiple_of((up_piece + n) * width, width), width)
            upper = dot(pair(H, seq), W[:, :, :, wide].reshape(model, width), NN)
            upper = upper + VEC[8:9, pl.ds(pl.multiple_of(k.t * inner + n * width, width), width)]
            erf_part = 1.0 + lax.erf(upper * (1.0 / ROOT_TWO))
            ACT[seq, :, cols] = (0.5 * upper * erf_part).astype(BF16)
            SL[seq, :, cols] = 0.5 * erf_part + upper * jnp.exp(-0.5 * upper * upper) * (
                1.0 / ROOT_TWO_PI
            )
            return carry

        lax.fori_loop(0, steps, part, 0)

    def down_block(seq, core):
        return dot(ACT[seq, part_rows(core), :], matrix(down_piece * width, inner), NT)

    if stepped:
        up(mine)
        down_w.forward(1)
        s1.pass_on()
        down_w.forward(2)
        s1.other()
        up(theirs)
        r1 = ReduceColumns(k, OUTBOX, INBOX, OWN, r_send, r_recv, 1, outer, rc_sems)
        places = {
            "across": (theirs, 1 - k.c),
            "theirs": (theirs, k.c),
            "partner": (mine, 1 - k.c),
            "mine": (mine, k.c),
        }

        def down_chunk(n):
            shard = W[w_chunks[n], :, :, pl.ds(down_piece * width, inner)]
            shard = shard.reshape(model // outer, inner)

            def block(name):
                seq, core = places[name]
                return dot(ACT[seq, part_rows(core), :], shard, NT)

            r1.step(n, w_chunks[n], block)

        down_w.arrive(0)
        down_chunk(0)
        down_w.forward(3)
        for n in range(1, outer):
            down_w.arrive(n)
            down_chunk(n)
        r1.wait_columns(w_chunks)
    else:
        up(mine)
        weights.forward(9)
        s1.pass_on()
        s1.other()
        up(theirs)
        weights.forward(10)
        weights.forward(11)
        for p in range(down_piece, pieces):
            weights.arrive(p)
        r1 = reduce(1)
        r1.across(down_block(theirs, 1 - k.c))
        r1.theirs(down_block(theirs, k.c))
        r1.partner(down_block(mine, 1 - k.c))
        r1.mine(down_block(mine, k.c))
        r1.wait()

    def norm_back(d, gain, normed, scaling):
        e = d * gain
        return scaling * (e - mean(e) - normed * mean(e * normed))

    def second_norm(r):
        second = HID[r, :] + r1.total(r) + vector(3)
        center = second - mean(second)
        scaling = lax.rsqrt(mean(center * center) + EPSILON)
        normed = center * scaling
        result = normed * vector(6) + vector(7)
        out_ref[r, :] = result.astype(BF16)
        diff = result - TEACH[r, :].astype(F32)
        grad = norm_back(diff, vector(6), normed, scaling)
        GS[r, :] = grad
        MX[k.t, r, :] = grad.astype(BF16)
        SUMS[0] += fold(grad)
        SUMS[1] += fold(diff * normed)
        SUMS[2] += fold(diff)
        SUMS[3] += fold(diff * diff)

    norm_loop(second_norm)
    if stepped:
        s2 = SpreadColumns(k, MX, s_send, s_recv, 2, outer, sc_sems)
        s2.start_columns(g_chunks)
    else:
        s2 = spread(MX, 2)
        s2.start()
    s2.own()

    def back_up(seq):
        def part(n, carry):
            cols = pl.ds(pl.multiple_of(n * width, width), width)
            wide = pl.ds(pl.multiple_of((down_piece + n) * width, width), width)
            grad = dot(pair(MX, seq), W[:, :, :, wide].reshape(model, width), NN)
            grad = (grad * SL[seq, :, cols]).astype(BF16)
            GU[seq, :, cols] = grad
            SUMS[7, :, cols] += fold(grad.astype(F32))
            return carry

        lax.fori_loop(0, steps, part, 0)

    def hidden_block(seq, core):
        return dot(GU[seq, part_rows(core), :], matrix(up_piece * width, inner), NT)

    def weight_grad(left, right, first, begin, end):
        def piece(n, carry):
            cols = pl.ds(pl.multiple_of(n * width, width), width)
            tokens = 4 * rows
            grad = dot(
                left[...].reshape(tokens, model), right[:, :, cols].reshape(tokens, width), TN
            )
            wide = pl.ds(pl.multiple_of((first + n) * width, width), width)
            G[:, :, :, wide] = grad.astype(BF16).reshape(outer, 2, model // (2 * outer), width)

            @pl.when(n > begin)
            def _():
                grads.start(first + n - 1)

            return carry

        lax.fori_loop(begin, end, piece, 0)

    r2 = reduce(2)
    if stepped:
        r1.drain_columns(w_chunks)
        r2.phase_free = False
    back_up(mine)
    r2.partner(hidden_block(mine, 1 - k.c))
    r2.mine(hidden_block(mine, k.c))
    if stepped:

        def down_grad_chunk(n):
            tokens, size = 4 * rows, model // outer
            cols = pl.ds(pl.multiple_of(g_chunks[n] * size, size), size)
            grad = dot(
                MX[:, :, cols].reshape(tokens, size), ACT[...].reshape(tokens, inner), TN
            )
            G[g_chunks[n], :, :, pl.ds(down_piece * width, inner)] = grad.astype(BF16).reshape(
                2, size // 2, inner
            )

        for n in range(outer):
            s2.pass_part(n, g_chunks[n])
            s2.other_part(n, g_chunks[n])
            down_grad_chunk(n)
            down_g.start(n)
        down_g.forward(0)
        back_up(theirs)
        r2.across(hidden_block(theirs, 1 - k.c))
        r2.theirs(hidden_block(theirs, k.c))
        down_g.forward(1)
        weight_grad(H, GU, up_piece, steps - 1, steps)
        crossed[7].start()
        weight_grad(H, GU, up_piece, 0, steps - 1)
        grads.start(up_piece + steps - 2)
        down_g.forward(2)
        down_g.forward(3)
    else:
        s2.pass_on()
        s2.other()
        weight_grad(MX, ACT, down_piece, 0, 2)
        back_up(theirs)
        grads.start(down_piece + 1)
        r2.across(hidden_block(theirs, 1 - k.c))
        r2.theirs(hidden_block(theirs, k.c))
        weight_grad(MX, ACT, down_piece, 2, steps)
        grads.forward(8)
        grads.start(down_piece + steps - 1)
        weight_grad(H, GU, up_piece, 0, steps)
        grads.start(up_piece + steps - 1)
        grads.forward(9)
        grads.forward(10)
    r2.wait()

    def first_back(r):
        grad_hidden = GS[r, :] + r2.total(r)
        normed = N1[r, :]
        grad = norm_back(grad_hidden, vector(4), normed, R1[r, :][:, :1])
        GS[r, :] = grad
        GF[k.t, r, :] = grad.astype(BF16)
        SUMS[4] += fold(grad)
        SUMS[5] += fold(grad_hidden * normed)
        SUMS[6] += fold(grad_hidden)

    norm_loop(first_back)
    s3 = spread(GF, 3)
    s3.start()
    early = Early(k, EA, EC, EX, EZ, ET, early_sems)
    for n, row in ((4, 2), (0, 7), (5, 8), (6, 9), (1, 10), (2, 11), (3, 12)):
        group, place = EARLY_ROWS[row]
        EA[0, group, place : place + 1, :] = jnp.sum(SUMS[n], axis=0, keepdims=True)
    EA[0, 1, pl.ds(k.t, 1), :] = jnp.sum(SUMS[7], axis=0, keepdims=True)
    early.hop(0).start()
    s3.own()

    def attend_back(seq, between=lambda: None):
        GC[...] = dot(pair(GF, seq), matrix(3 * width, width), NN).astype(BF16)
        ACC[...] = jnp.zeros_like(ACC)

        def head(h, carry):
            mask = head_mask(h)
            context = GC[...] * mask
            low = PT[seq, h]
            ACC[2] += dot(low, context, NN)
            probs = low.astype(F32)
            grad = dot(V[seq], context, NT)
            across = jnp.sum(probs * grad, axis=0, keepdims=True)
            grad = (probs * (grad - across)).astype(BF16)
            ACC[1] += dot(grad, Q[seq] * mask, NN)
            ACC[0] += dot(grad, K[seq] * mask, TN)
            return carry

        lax.fori_loop(0, heads // 2, head, 0)
        between()
        lax.fori_loop(heads // 2, heads, head, 0)
        for n in range(3):
            grad = ACC[n] if n == 2 else ACC[n] * scale
            DQKV[seq, :, n * width : (n + 1) * width] = grad.astype(BF16)

    def input_block(seq, core):
        return dot(DQKV[seq, part_rows(core), :], matrix(0, 3 * width), NT)

    if stepped:
        crossed[7].relay()
        grads.forward(4)
        attend_back(mine)
        early.add(0)
        early.hop(1).start()
        grads.forward(5)
        relay_back(4)
        s3.pass_on()
        crossed[7].forward()
        s3.other()
        weight_grad(GF, C, 3, 0, 1)
        grads.forward(6)
        early.add(1)
        early.over().start()
        grads.start(3)
        relay_back(5)
        attend_back(theirs)
        relay_back(6)
    else:
        attend_back(mine)
        early.add(0)
        early.hop(1).start()
        grads.forward(11)
        s3.pass_on()
        grads.forward(4)
        s3.other()
        weight_grad(GF, C, 3, 0, 1)
        grads.forward(5)
        early.add(1)
        early.over().start()
        attend_back(theirs)
        grads.start(3)

    here = pl.ds(pl.multiple_of(k.t * width, width), width)
    for row, n in ((0, 0), (1, 2)):
        grad = DQKV[:, :, n * width : (n + 1) * width].reshape(4 * rows, width).astype(F32)
        VA[0, row : row + 1, here] = jnp.sum(grad, axis=0, keepdims=True)

    two_rows = pl.ds(0, 2)

    def vector_hop(n, peer):
        return remote(
            VA.at[n, two_rows], VR.at[n, two_rows], v_send.at[n], v_recv.at[n], peer
        )

    def vector_last(step):
        return remote(
            VA.at[3, two_rows], VZ.at[k.z, two_rows], v_send.at[3], v_recv.at[3], k.z_peer(step)
        )

    hops = [vector_hop(n, peer) for n, peer in enumerate((k.c_peer, k.y_peer, k.x_peer))]

    def hop_in(n):
        hops[n].wait_recv()
        VA[n + 1, 0:2, :] = VA[n, 0:2, :] + VR[n, 0:2, :]

    if stepped:
        weight_grad(X, DQKV, 0, 2, 3)
        hops[0].start()
        crossed[2].start()
        weight_grad(X, DQKV, 0, 0, 1)
        hop_in(0)
        hops[1].start()
        grads.start(0)
        weight_grad(X, DQKV, 0, 1, 2)
        early.add_over()
        grads.forward(3)
    else:
        weight_grad(X, DQKV, 0, 0, 1)
        hops[0].start()
        weight_grad(X, DQKV, 0, 1, 2)
        grads.start(0)
        hop_in(0)
        hops[1].start()
        weight_grad(X, DQKV, 0, 2, 3)
        grads.start(1)
        grads.forward(6)
    r3 = reduce(3)
    r3.across(input_block(theirs, 1 - k.c))
    if stepped:
        grads.start(1)
        crossed[2].relay()
    r3.theirs(input_block(theirs, k.c))
    hop_in(1)
    hops[2].start()
    if stepped:
        relay_back(3)
        grads.forward(0)
    else:
        early.add_over()
        grads.start(2)
        grads.forward(7)
    r3.partner(input_block(mine, 1 - k.c))
    r3.mine(input_block(mine, k.c))

    def send_last(step, carry):
        vector_last(step).start()
        return carry

    def vectors_along():
        hop_in(2)
        VZ[k.z, 0:2, :] = VA[3, 0:2, :]
        lax.fori_loop(1, outer, send_last, 0)

    early.add_along()
    if stepped:
        relay_back(0)
        grads.forward(1)
        vectors_along()
        crossed[2].forward()
        relay_back(1)
    else:
        for p in (8, 9, 10):
            grads.finish(p)
        grads.forward(3)
        grads.forward(0)
        grads.forward(1)
        vectors_along()
        grads.forward(2)
    r3.wait()

    def last(r):
        gin_ref[r, :] = GS[r, :] + r3.total(r)

    norm_loop(last)
    vz_all = VZ.at[pl.ds(0, outer - 1), two_rows]
    every = remote(vz_all, vz_all, v_send.at[3], v_recv.at[3], k.x_peer)

    def add(i, total):
        return total + VZ[i, 0:2, :]

    def vectors_out():
        every.wait_recv()
        gvec_ref[0:2, :] = lax.fori_loop(1, outer, add, VZ[0, 0:2, :])
        early.finish()
        for row, (group, place) in EARLY_ROWS.items():
            gvec_ref[row : row + 1, :] = ET[group, place : place + 1, :]

    if stepped:
        down_g.finish(gd_ref)
        for p in (4, 5, 6):
            grads.finish(p)
        crossed[7].finish()
        for p in (3, 0):
            grads.finish(p)
        crossed[2].finish()
        vectors_out()
        grads.finish(1)
    else:
        for p in (11, 4, 5, 6, 7, 3, 0, 1):
            grads.finish(p)
        vectors_out()
        grads.finish(2)

    weights.drain(simple)
    grads.drain(simple)
    if stepped:
        down_w.drain()
        down_g.drain()
        for gradient in crossed.values():
            gradient.drain()
        s2.drain_columns(g_chunks)
    for s in (s0, s1, s3) if stepped else (s0, s1, s2, s3):
        s.drain()
    r3.drain()
    for hop in hops:
        hop.wait_send()
    every.wait_send()
    early.drain()


def layer(outer, arrays):
    inputs, query_weight, up_weight = arrays[0], arrays[2], arrays[6]
    rows, model = inputs.shape
    shard_rows, width = query_weight.shape
    inner = up_weight.shape[1]
    heads = width // HEAD_DIM
    columns_all = 4 * width + 2 * inner
    pieces = columns_all // width
    seq = 2 * rows
    vmem = pl.BlockSpec(memory_space=pltpu.VMEM)
    anywhere = pl.BlockSpec(memory_space=pl.ANY)
    full = (outer, 2, shard_rows, columns_all)
    dma = pltpu.SemaphoreType.DMA
    outs = (
        jax.ShapeDtypeStruct((rows, model), BF16),
        jax.ShapeDtypeStruct((rows, model), F32),
        jax.ShapeDtypeStruct((shard_rows, width), F32),
        jax.ShapeDtypeStruct((shard_rows, width), F32),
        jax.ShapeDtypeStruct((shard_rows, width), F32),
        jax.ShapeDtypeStruct((width, shard_rows), F32),
        jax.ShapeDtypeStruct((shard_rows, inner), F32),
        jax.ShapeDtypeStruct((inner, shard_rows), F32),
        jax.ShapeDtypeStruct((VECTORS, model), F32),
    )
    return pl.pallas_call(
        functools.partial(body, outer),
        out_shape=outs,
        in_specs=[anywhere] * len(arrays),
        out_specs=(vmem,) * len(outs),
        scratch_shapes=[
            pltpu.VMEM(full, BF16),
            pltpu.VMEM(full, BF16),
            pltpu.VMEM((outer, shard_rows, columns_all), BF16),
            pltpu.VMEM((outer - 1, shard_rows, columns_all), BF16),
            pltpu.VMEM((4, rows, model), BF16),
            pltpu.VMEM((4, rows, model), BF16),
            pltpu.VMEM((4, rows, model), BF16),
            pltpu.VMEM((4, rows, model), BF16),
            pltpu.VMEM((2, seq, width), BF16),
            pltpu.VMEM((2, seq, width), BF16),
            pltpu.VMEM((2, seq, width), BF16),
            pltpu.VMEM((2, seq, width), BF16),
            pltpu.VMEM((seq, width), BF16),
            pltpu.VMEM((2, seq, 3 * width), BF16),
            pltpu.VMEM((2, heads, seq, seq), BF16),
            pltpu.VMEM((2, seq, inner), F32),
            pltpu.VMEM((2, seq, inner), BF16),
            pltpu.VMEM((2, seq, inner), BF16),
            pltpu.VMEM((rows, model), F32),
            pltpu.VMEM((rows, model), F32),
            pltpu.VMEM((rows, model), F32),
            pltpu.VMEM((rows, 128), F32),
            pltpu.VMEM((rows, model), F32),
            pltpu.VMEM((8, 8, model), F32),
            pltpu.VMEM((3, seq, width), F32),
            pltpu.VMEM((3, rows, model), BF16),
            pltpu.VMEM((3, rows, model), BF16),
            pltpu.VMEM((4, 8, model), F32),
            pltpu.VMEM((3, 8, model), F32),
            pltpu.VMEM((outer, 8, model), F32),
            pltpu.VMEM((3, 4, 8, model), F32),
            pltpu.VMEM((2, 4, 8, model), F32),
            pltpu.VMEM((2, 8, model), F32),
            pltpu.VMEM((outer, 8, model), F32),
            pltpu.VMEM((4, 8, model), F32),
            pltpu.VMEM((rows, model), BF16),
            pltpu.VMEM((width, shard_rows), BF16),
            pltpu.VMEM((inner, shard_rows), BF16),
            pltpu.VMEM((9, 4 * inner), F32),
            dma((4, pieces)),
            dma((4, pieces)),
            dma((4, pieces)),
            dma((4, pieces)),
            dma((4, 3)),
            dma((4, 3)),
            dma((4, 3)),
            dma((4, 3)),
            dma((4,)),
            dma((4,)),
            dma((len(arrays),)),
            pltpu.VMEM((shard_rows, columns_all), BF16),
            pltpu.VMEM((len(CROSSED_BACK), 3, 2, shard_rows, width), BF16),
            pltpu.VMEM((len(CROSSED_BACK), 2, shard_rows, width), BF16),
            pltpu.VMEM((len(CROSSED_BACK), shard_rows, width), BF16),
            dma((4, pieces)),
            dma((4, pieces)),
            (dma((7,)),) * 2,
            (dma((outer, 2)),) * 4,
            (dma((outer,)),) * 4,
            (dma((3, outer)),) * 2,
            (dma((outer,)),) * 4,
        ],
        compiler_params=pltpu.CompilerParams(
            collective_id=0, has_side_effects=True, vmem_limit_bytes=67043328
        ),
        name="layer",
    )(*arrays)


def write_body(count, factor, *refs):
    ins, outs, sem = refs[:9], refs[9 : 9 + count], refs[-1]
    vec = ins[8]
    pairs = list(zip(ins[:8], outs[:8]))
    single = [(0, 8), (1, 9), (2, 10), (7, 12), (8, 13), (9, 14), (10, 15), (11, 16)]
    pairs += [(vec.at[pl.ds(row, 1), :], outs[place]) for row, place in single]
    model = vec.shape[1]
    parts = outs[11].shape[1] // model
    for n in range(parts):
        pairs.append((vec.at[pl.ds(3 + n, 1), :], outs[11].at[:, pl.ds(n * model, model)]))
    copies = [pltpu.make_async_copy(src, dst, sem.at[n]) for n, (src, dst) in enumerate(pairs)]
    for copy in copies:
        copy.start()
    outs[17][0, 0] = jnp.sum(vec[12:13, :]) * factor
    for copy in copies:
        copy.wait()


def write(values, up_length, factor):
    model = values[8].shape[1]
    line = jax.ShapeDtypeStruct((1, model), F32)
    outs = [jax.ShapeDtypeStruct(v.shape, v.dtype) for v in values[:8]] + [line] * 10
    outs[11] = jax.ShapeDtypeStruct((1, up_length), F32)
    outs[17] = jax.ShapeDtypeStruct((1, 1), F32)
    copies = 16 + up_length // model
    return pl.pallas_call(
        functools.partial(write_body, len(outs), factor),
        out_shape=tuple(outs),
        in_specs=[pl.BlockSpec(memory_space=pltpu.VMEM)] * len(values),
        out_specs=(pl.BlockSpec(memory_space=pl.ANY),) * 17
        + (pl.BlockSpec(memory_space=pltpu.SMEM),),
        scratch_shapes=[pltpu.SemaphoreType.DMA((copies,))],
        name="write",
    )(*values)


def shards(*arrays):
    inputs = arrays[0]
    outer = lax.axis_size("dp") // 2
    arrays = arrays[:8] + tuple(v.reshape(1, -1) for v in arrays[8:])
    up_length = arrays[11].shape[1]
    token_total = inputs.shape[0] * lax.axis_size("dp") * lax.axis_size("tensor")
    values = write(layer(outer, arrays), up_length, 0.5 / token_total)
    loss = values[17].reshape(())
    output, grad_inputs, gq, gk, gv, go, gu, gd = values[:8]
    return (output, loss, grad_inputs, gq, gk, gv, go, gu, gd) + tuple(
        v.reshape(-1) for v in values[8:17]
    )


def solution(mesh):
    tokens = P(("dp", "tensor"), None)
    across, down = P("dp", "tensor"), P("tensor", "dp")
    in_specs = (tokens, tokens, across, across, across, down, across, down) + (P(),) * 9
    out_specs = (tokens, P(), tokens, across, across, across, down, across, down) + (P(),) * 9
    return jax.shard_map(shards, mesh=mesh, in_specs=in_specs, out_specs=out_specs, check_vma=False)
```

```python
import functools
import math

import jax
import jax.numpy as jnp
from jax import lax
from jax.experimental import pallas as pl
from jax.experimental.pallas import tpu as pltpu
from jax.sharding import PartitionSpec as P

HEAD_DIM = 64
SEQ = 512
EPSILON = 1e-05
MESH = pl.DeviceIdType.MESH
F32 = jnp.float32
BF16 = jnp.bfloat16
NN = ((1,), (0,))
NT = ((1,), (1,))
TN = ((0,), (0,))
CHUNK = 128
WINDOW = 2
CROSSED = (3, 7)
CROSSED_BACK = (2, 7)
ROOT_TWO = math.sqrt(2.0)
ROOT_TWO_PI = math.sqrt(2.0 * math.pi)
VECTORS = 16


def dot(left, right, dims):
    return lax.dot_general(left, right, (dims, ((), ())), preferred_element_type=F32)


def remote(src, dst, send, recv, peer):
    return pltpu.make_async_remote_copy(
        src_ref=src, dst_ref=dst, send_sem=send, recv_sem=recv, device_id=peer, device_id_type=MESH
    )


class Place:
    def __init__(self, outer):
        self.outer = outer
        self.dp = lax.axis_index("dp")
        self.t = lax.axis_index("tensor")
        self.z, self.x = self.dp // 2, self.dp % 2
        self.y, self.c = self.t // 2, self.t % 2
        self.x_peer = (self.z * 2 + 1 - self.x, self.t)
        self.y_peer = (self.dp, (1 - self.y) * 2 + self.c)
        self.c_peer = (self.dp, self.y * 2 + 1 - self.c)
        self.diag = (1 - self.y) * 2 + 1 - self.c
        self.diag_peer = (self.dp, self.diag)

    def z_peer(self, step):
        return (lax.rem(self.z + step, self.outer) * 2 + self.x, self.t)

    def greet(self):
        barrier = pltpu.get_barrier_semaphore()

        def one(step, carry):
            pl.semaphore_signal(barrier, inc=1, device_id=self.z_peer(step), device_id_type=MESH)
            return carry

        lax.fori_loop(1, self.outer, one, 0)
        for peer in (self.x_peer, self.y_peer, self.diag_peer, self.c_peer):
            pl.semaphore_signal(barrier, inc=1, device_id=peer, device_id_type=MESH)

    def enter(self):
        pl.semaphore_wait(pltpu.get_barrier_semaphore(), self.outer + 3)


def columns(piece, width):
    start = piece * width
    if not isinstance(start, int):
        start = pl.multiple_of(start, width)
    return pl.ds(start, width)


class Weights:
    def __init__(self, k, full, send, recv, width, pieces):
        self.k, self.full, self.send, self.recv, self.width = k, full, send, recv, width
        self.pieces = pieces

    def first(self, p, step):
        block = self.full.at[self.k.z, self.k.x, :, columns(p, self.width)]
        return remote(block, block, self.send.at[0, p], self.recv.at[0, p], self.k.z_peer(step))

    def all_first(self, p):
        block = self.full.at[pl.ds(0, self.k.outer - 1), 0, :, columns(p, self.width)]
        return remote(block, block, self.send.at[0, p], self.recv.at[0, p], self.k.x_peer)

    def second(self, p):
        block = self.full.at[:, self.k.x, :, columns(p, self.width)]
        return remote(block, block, self.send.at[1, p], self.recv.at[1, p], self.k.x_peer)

    def start(self, p):
        def one(step, carry):
            self.first(p, step).start()
            return carry

        lax.fori_loop(1, self.k.outer, one, 0)

    def forward(self, p):
        self.all_first(p).wait_recv()
        self.second(p).start()
        if p + WINDOW < self.pieces:
            self.start(p + WINDOW)

    def arrive(self, p):
        self.second(p).wait_recv()

    def drain(self, pieces):
        def piece(p, carry):
            self.all_first(p).wait_send()
            self.second(p).wait_send()
            return carry

        lax.fori_loop(0, pieces, piece, 0)


class Gradients:
    def __init__(self, k, part, near, far, out, send, recv, width):
        self.k, self.part, self.near, self.far, self.out = k, part, near, far, out
        self.send, self.recv, self.width = send, recv, width

    def one(self, p):
        k, cols = self.k, columns(p, self.width)
        return remote(
            self.part.at[:, 1 - k.x, :, cols],
            self.near.at[:, :, cols],
            self.send.at[0, p],
            self.recv.at[0, p],
            k.x_peer,
        )

    def two(self, p, step):
        k, cols = self.k, columns(p, self.width)
        return remote(
            self.part.at[lax.rem(k.z + step, k.outer), k.x, :, cols],
            self.far.at[step - 1, :, cols],
            self.send.at[1, p],
            self.recv.at[1, p],
            k.z_peer(step),
        )

    def all_two(self, p):
        block = self.far.at[:, :, columns(p, self.width)]
        return remote(block, block, self.send.at[1, p], self.recv.at[1, p], self.k.x_peer)

    def start(self, p):
        self.one(p).start()

    def forward(self, p):
        k, cols = self.k, columns(p, self.width)
        self.one(p).wait_recv()
        here = self.part[:, k.x, :, cols].astype(F32)
        self.part[:, k.x, :, cols] = (here + self.near[:, :, cols].astype(F32)).astype(BF16)

        def send(step, carry):
            self.two(p, step).start()
            return carry

        lax.fori_loop(1, k.outer, send, 0)

    def finish(self, p):
        k, cols = self.k, columns(p, self.width)
        self.all_two(p).wait_recv()

        def add(i, total):
            return total + self.far[i, :, cols].astype(F32)

        total = self.part[k.z, k.x, :, cols].astype(F32)
        total = lax.fori_loop(0, k.outer - 1, add, total)
        self.out(p, total)

    def drain(self, pieces):
        def piece(p, carry):
            self.one(p).wait_send()
            self.all_two(p).wait_send()
            return carry

        lax.fori_loop(0, pieces, piece, 0)


class Line:
    def __init__(self, k):
        self.k = k
        self.two = lax.rem(k.z + 2, 4)
        self.next = k.z + 1 - 2 * lax.rem(k.z, 2)
        self.third = 3 - k.z
        self.middle = (k.z == 1) | (k.z == 2)
        self.end = (k.z == 0) | (k.z == 3)

    def peer(self, z):
        return (z * 2 + self.k.x, self.k.t)


class LineWeights(Weights):
    def __init__(self, line, *rest):
        super().__init__(line.k, *rest)
        self.line = line

    def shards(self, z, p):
        return self.full.at[z, slice(None) if p in CROSSED else self.k.x, :, columns(p, self.width)]

    def send_to(self, z, source, send, recv, p):
        block = self.shards(source, p)
        return remote(
            block, block, self.send.at[send, p], self.recv.at[recv, p], self.line.peer(z)
        )

    def some(self, count, send, recv, p):
        block = self.shards(pl.ds(0, count), p)
        return remote(block, block, self.send.at[send, p], self.recv.at[recv, p], self.k.x_peer)

    def crossing(self, p):
        block = self.full.at[self.k.z, self.k.x, :, columns(p, self.width)]
        return remote(block, block, self.send.at[1, p], self.recv.at[1, p], self.k.x_peer)

    def cross(self):
        for p in CROSSED:
            self.crossing(p).start()

    def over(self, z, p):
        block = self.full.at[z, self.k.x, :, columns(p, self.width)]
        return remote(block, block, self.send.at[1, p], self.recv.at[1, p], self.k.x_peer)

    def start(self, p):
        line = self.line
        if p in CROSSED:
            self.crossing(p).wait_recv()
        else:
            self.over(self.k.z, p).start()
        self.send_to(line.two, self.k.z, 0, 0, p).start()
        self.send_to(line.next, self.k.z, 0, 0, p).start()

        @pl.when(line.middle)
        def _():
            self.send_to(line.third, self.k.z, 2, 2, p).start()

    def relay(self, p):
        line = self.line
        self.some(2, 0, 0, p).wait_recv()

        @pl.when(line.middle)
        def _():
            self.send_to(line.next, line.two, 3, 2, p).start()

        if p not in CROSSED:
            self.over(line.two, p).start()
            self.over(line.next, p).start()
        if p + WINDOW < self.pieces:
            self.start(p + WINDOW)

    def forward(self, p):
        if p not in CROSSED:
            self.some(1, 2, 2, p).wait_recv()
            self.over(self.line.third, p).start()

    def arrive(self, p):
        if p in CROSSED:
            self.some(1, 2, 2, p).wait_recv()
        else:
            self.second(p).wait_recv()

    def drain(self, pieces):
        for p in range(pieces):
            self.some(2, 0, 0, p).wait_send()
            (self.crossing(p) if p in CROSSED else self.second(p)).wait_send()

        @pl.when(self.line.middle)
        def _():
            for p in range(pieces):
                self.some(1, 2, 2, p).wait_send()
                self.some(1, 3, 2, p).wait_send()


class CrossedGradient:
    def __init__(self, line, part, far, hop, last, out, send, recv, width, p, place):
        self.line, self.k, self.part, self.out, self.p = line, line.k, part, out, p
        self.far, self.hop, self.last = far.at[place], hop.at[place], last.at[place]
        self.cols = columns(p, width)
        self.send, self.recv = send, recv

    def along(self, z, dst, send, recv, peer):
        return remote(
            self.part.at[z, :, :, self.cols],
            dst,
            self.send.at[send, self.p],
            self.recv.at[recv, self.p],
            self.line.peer(peer),
        )

    def to(self, z, slot, send, recv):
        return self.along(z, self.far.at[slot], send, recv, z)

    def to_hop(self):
        return self.along(self.line.third, self.hop, 2, 3, self.line.next)

    def over(self):
        return remote(
            self.part.at[self.k.z, 1 - self.k.x, :, self.cols],
            self.last,
            self.send.at[0, self.p],
            self.recv.at[0, self.p],
            self.k.x_peer,
        )

    def start(self):
        line = self.line

        @pl.when(line.end)
        def _():
            self.to_hop().start()
            self.to(line.two, 0, 3, 1).start()

        @pl.when(line.middle)
        def _():
            self.to(line.third, 2, 2, 2).start()

        self.to(line.next, 1, 1, 1).start()

    def relay(self):
        line = self.line

        @pl.when(line.middle)
        def _():
            self.to_hop().wait_recv()
            here = self.part[line.two, :, :, self.cols].astype(F32) + self.hop[...].astype(F32)
            self.part[line.two, :, :, self.cols] = here.astype(BF16)
            self.to(line.two, 0, 3, 1).start()

    def total(self, x):
        total = self.part[self.k.z, x, :, self.cols].astype(F32)
        for n in range(3):
            total = total + self.far[n, x].astype(F32)
        return total

    def forward(self):
        line = self.line
        both = self.far.at[pl.ds(0, 2)]
        remote(both, both, self.send.at[1, self.p], self.recv.at[1, self.p], self.k.x_peer).wait_recv()

        @pl.when(line.middle)
        def _():
            self.to(line.third, 2, 2, 2).wait_recv()

        x = 1 - self.k.x
        self.part[self.k.z, x, :, self.cols] = self.total(x).astype(BF16)
        self.over().start()

    def finish(self):
        self.over().wait_recv()
        self.out(self.p, self.total(self.k.x) + self.last[...].astype(F32))

    def drain(self):
        line = self.line
        self.over().wait_send()
        for z, sem in ((line.next, 1), (line.third, 2), (line.two, 3)):
            self.to(z, 0, sem, 1).wait_send()


class LineGradients(Gradients):
    def __init__(self, line, hop, x_send, x_recv, *rest):
        super().__init__(line.k, *rest)
        self.line, self.hop, self.x_send, self.x_recv = line, hop, x_send, x_recv
        self.targets = (line.third, line.two, line.next, line.k.z)

    def over(self, p, n):
        k, z, cols = self.k, self.targets[n], columns(p, self.width)
        return remote(
            self.part.at[z, 1 - k.x, :, cols],
            self.near.at[z, :, cols],
            self.x_send.at[n, p],
            self.x_recv.at[n, p],
            k.x_peer,
        )

    def start(self, p):
        for n in range(4):
            self.over(p, n).start()

    def to(self, z, dst, send, recv, p):
        cols = columns(p, self.width)
        return remote(
            self.part.at[z, self.k.x, :, cols],
            dst.at[:, cols],
            self.send.at[send, p],
            self.recv.at[recv, p],
            self.line.peer(z),
        )

    def to_hop(self, p):
        cols = columns(p, self.width)
        return remote(
            self.part.at[self.line.third, self.k.x, :, cols],
            self.hop.at[:, cols],
            self.send.at[2, p],
            self.recv.at[3, p],
            self.line.peer(self.line.next),
        )

    def forward(self, p):
        k, line, cols = self.k, self.line, columns(p, self.width)
        for n in range(4):
            z = self.targets[n]
            self.over(p, n).wait_recv()
            here = self.part[z, k.x, :, cols].astype(F32)
            self.part[z, k.x, :, cols] = (here + self.near[z, :, cols].astype(F32)).astype(BF16)
            if n == 0:

                @pl.when(line.end)
                def _():
                    self.to_hop(p).start()

                @pl.when(line.middle)
                def _():
                    self.to(line.third, self.far.at[2], 2, 2, p).start()

            elif n == 1:

                @pl.when(line.end)
                def _():
                    self.to(line.two, self.far.at[0], 3, 1, p).start()

            elif n == 2:
                self.to(line.next, self.far.at[1], 1, 1, p).start()

    def relay(self, p):
        line, cols = self.line, columns(p, self.width)

        @pl.when(line.middle)
        def _():
            self.to_hop(p).wait_recv()
            here = self.part[line.two, self.k.x, :, cols].astype(F32)
            here = here + self.hop[:, cols].astype(F32)
            self.part[line.two, self.k.x, :, cols] = here.astype(BF16)
            self.to(line.two, self.far.at[0], 3, 1, p).start()

    def finish(self, p):
        k, line, cols = self.k, self.line, columns(p, self.width)
        both = self.far.at[pl.ds(0, 2), :, cols]
        remote(both, both, self.send.at[1, p], self.recv.at[1, p], k.x_peer).wait_recv()

        @pl.when(line.middle)
        def _():
            self.to(line.third, self.far.at[2], 2, 2, p).wait_recv()

        total = self.part[k.z, k.x, :, cols].astype(F32)
        for n in range(3):
            total = total + self.far[n, :, cols].astype(F32)
        self.out(p, total)

    def drain(self, pieces):
        line = self.line
        for p in range(pieces):
            if p in CROSSED_BACK:
                continue
            for n in range(4):
                self.over(p, n).wait_send()
            for z, sem in ((line.next, 1), (line.third, 2), (line.two, 3)):
                self.to(z, self.far.at[0], sem, 1, p).wait_send()


class Spread:
    def __init__(self, k, blocks, send, recv, phase):
        self.k, self.blocks, self.send, self.recv, self.phase = k, blocks, send, recv, phase

    def copy(self, number, block, peer):
        ref = self.blocks.at[block]
        return remote(
            ref, ref, self.send.at[self.phase, number], self.recv.at[self.phase, number], peer
        )

    def near(self):
        return self.copy(0, self.k.t, self.k.c_peer)

    def far(self):
        return self.copy(1, self.k.t, self.k.diag_peer)

    def relay(self):
        return self.copy(2, self.k.diag, self.k.c_peer)

    def start(self):
        self.far().start()
        self.near().start()

    def own(self):
        self.near().wait_recv()

    def pass_on(self):
        self.far().wait_recv()
        self.relay().start()

    def other(self):
        self.relay().wait_recv()

    def drain(self):
        self.near().wait_send()
        self.far().wait_send()
        self.relay().wait_send()


class SpreadColumns(Spread):
    def __init__(self, k, blocks, send, recv, phase, chunks, far_sems):
        super().__init__(k, blocks, send, recv, phase)
        self.chunks = chunks
        self.far_send, self.far_recv, self.relay_send, self.relay_recv = far_sems

    def cols(self, chunk):
        width = self.blocks.shape[2] // self.chunks
        return pl.ds(pl.multiple_of(chunk * width, width), width)

    def far_part(self, n, chunk):
        ref = self.blocks.at[self.k.t, :, self.cols(chunk)]
        return remote(ref, ref, self.far_send.at[n], self.far_recv.at[n], self.k.diag_peer)

    def relay_part(self, n, chunk):
        ref = self.blocks.at[self.k.diag, :, self.cols(chunk)]
        return remote(ref, ref, self.relay_send.at[n], self.relay_recv.at[n], self.k.c_peer)

    def start_columns(self, order):
        self.near().start()
        for n, chunk in enumerate(order):
            self.far_part(n, chunk).start()

    def pass_part(self, n, chunk):
        self.far_part(n, chunk).wait_recv()
        self.relay_part(n, chunk).start()

    def other_part(self, n, chunk):
        self.relay_part(n, chunk).wait_recv()

    def drain_columns(self, order):
        self.near().wait_send()
        for n, chunk in enumerate(order):
            self.far_part(n, chunk).wait_send()
            self.relay_part(n, chunk).wait_send()


class Reduce:
    def __init__(self, k, out, inbox, keep, send, recv, phase):
        self.k, self.out, self.inbox, self.keep = k, out, inbox, keep
        self.send, self.recv, self.phase = send, recv, phase

    def copy(self, number, phase=None):
        peer = self.k.y_peer if number == 2 else self.k.c_peer
        phase = self.phase if phase is None else phase
        return remote(
            self.out.at[number],
            self.inbox.at[number],
            self.send.at[phase, number],
            self.recv.at[phase, number],
            peer,
        )

    phase_free = True

    def free(self, number):
        if self.phase > 0 and self.phase_free:
            self.copy(number, self.phase - 1).wait_send()

    def across(self, value):
        self.free(0)
        self.out[0] = value.astype(BF16)
        self.copy(0).start()

    def theirs(self, value):
        self.free(2)
        self.copy(0).wait_recv()
        self.out[2] = (value + self.inbox[0].astype(F32)).astype(BF16)
        self.copy(2).start()

    def partner(self, value):
        self.free(1)
        self.out[1] = value.astype(BF16)
        self.copy(1).start()

    def mine(self, value):
        self.keep[...] = value

    def wait(self):
        self.copy(1).wait_recv()
        self.copy(2).wait_recv()

    def total(self, rows):
        return self.keep[rows, :] + (
            self.inbox[1, rows, :].astype(F32) + self.inbox[2, rows, :].astype(F32)
        )

    def drain(self):
        for number in range(3):
            self.copy(number).wait_send()


class ReduceColumns(Reduce):
    def __init__(self, k, out, inbox, keep, send, recv, phase, chunks, sems):
        super().__init__(k, out, inbox, keep, send, recv, phase)
        self.chunks, self.part_send, self.part_recv = chunks, sems[0], sems[1]

    def cols(self, chunk):
        width = self.keep.shape[1] // self.chunks
        return pl.ds(pl.multiple_of(chunk * width, width), width)

    def part(self, number, n, chunk):
        cols = self.cols(chunk)
        return remote(
            self.out.at[number, :, cols],
            self.inbox.at[number, :, cols],
            self.part_send.at[number, n],
            self.part_recv.at[number, n],
            self.k.y_peer if number == 2 else self.k.c_peer,
        )

    def step(self, n, chunk, block):
        cols = self.cols(chunk)
        if n == 0:
            for number in range(3):
                self.free(number)
        self.out[0, :, cols] = block("across").astype(BF16)
        self.part(0, n, chunk).start()
        self.out[1, :, cols] = block("partner").astype(BF16)
        self.part(1, n, chunk).start()
        value = block("theirs")
        self.part(0, n, chunk).wait_recv()
        self.out[2, :, cols] = (value + self.inbox[0, :, cols].astype(F32)).astype(BF16)
        self.part(2, n, chunk).start()
        self.keep[:, cols] = block("mine")

    def wait_columns(self, order):
        for n, chunk in enumerate(order):
            self.part(1, n, chunk).wait_recv()
            self.part(2, n, chunk).wait_recv()

    def drain_columns(self, order):
        for n, chunk in enumerate(order):
            for number in range(3):
                self.part(number, n, chunk).wait_send()


EARLY_ROWS = {2: (0, 0), 7: (0, 1), 8: (0, 2), 9: (0, 3), 10: (2, 0), 11: (2, 1), 12: (2, 2)}
EARLY_ROWS.update({3 + n: (1, n) for n in range(4)})


class Early:
    def __init__(self, k, sums, inbox, cross, along, total, sems):
        self.k, self.sums, self.inbox, self.cross = k, sums, inbox, cross
        self.along, self.total, (self.send, self.recv) = along, total, sems

    def copy(self, n, src, dst, peer):
        return remote(src, dst, self.send.at[n], self.recv.at[n], peer)

    def hop(self, n):
        peer = self.k.c_peer if n == 0 else self.k.y_peer
        rows = pl.ds(0, 4)
        return self.copy(n, self.sums.at[n, :, rows], self.inbox.at[n, :, rows], peer)

    def over(self):
        rows = pl.ds(0, 4)
        return self.copy(
            2, self.sums.at[2, self.k.t, rows], self.cross.at[0, rows], self.k.x_peer
        )

    def last(self, step):
        rows = pl.ds(0, 4)
        return self.copy(
            3, self.cross.at[1, rows], self.along.at[self.k.z, rows], self.k.z_peer(step)
        )

    def every(self):
        block = self.along.at[pl.ds(0, self.k.outer - 1), pl.ds(0, 4)]
        return self.copy(3, block, block, self.k.x_peer)

    def share(self, n):
        k = self.k
        block = self.total.at[k.t, pl.ds(0, 4)]
        return self.copy(4 + n, block, block, (k.c_peer, k.y_peer, k.diag_peer)[n])

    def add(self, n):
        self.hop(n).wait_recv()
        self.sums[n + 1, :, 0:4, :] = self.sums[n, :, 0:4, :] + self.inbox[n, :, 0:4, :]

    def add_over(self):
        k = self.k
        self.over().wait_recv()
        total = self.sums[2, k.t, 0:4, :] + self.cross[0, 0:4, :]
        self.cross[1, 0:4, :] = total
        self.along[k.z, 0:4, :] = total

        def send(step, carry):
            self.last(step).start()
            return carry

        lax.fori_loop(1, k.outer, send, 0)

    def add_along(self):
        self.every().wait_recv()

        def add(i, total):
            return total + self.along[i, 0:4, :]

        first = self.along[0, 0:4, :]
        self.total[self.k.t, 0:4, :] = lax.fori_loop(1, self.k.outer, add, first)
        for n in range(3):
            self.share(n).start()

    def finish(self):
        for n in range(3):
            self.share(n).wait_recv()

    def drain(self):
        self.hop(0).wait_send()
        self.hop(1).wait_send()
        self.over().wait_send()
        self.every().wait_send()
        for n in range(3):
            self.share(n).wait_send()


class DownWeights:
    HALVES = 2

    def __init__(self, line, full, start, size, sems):
        self.line, self.k = line, line.k
        self.full, self.start_at, self.half = full, start, size // self.HALVES
        self.z_send, self.z_recv, self.x_send, self.x_recv = sems
        self.sources = (self.k.z, line.two, line.next, line.third)

    def shard(self, z, x, half):
        return self.full.at[z, x, :, pl.ds(self.start_at + half * self.half, self.half)]

    def along(self, z, source, send, recv, half):
        block = self.shard(source, self.k.x, half)
        sems = (self.z_send.at[send, half], self.z_recv.at[recv, half])
        return remote(block, block, *sems, self.line.peer(z))

    def across(self, step, half, x):
        block = self.shard(self.sources[step], x, half)
        sems = (self.x_send.at[step, half], self.x_recv.at[step, half])
        return remote(block, block, *sems, self.k.x_peer)

    def start(self, step):
        z = self.sources[step]
        for half in range(self.HALVES):
            if step < 3:
                self.along(z, self.k.z, step, step, half).start()
            else:

                @pl.when(self.line.middle)
                def _():
                    self.along(z, self.k.z, 3, 3, half).start()

    def forward(self, step):
        for half in range(self.HALVES):
            if step > 0:
                self.along(self.line.next, self.k.z, step, step, half).wait_recv()
            if step == 1:

                @pl.when(self.line.middle)
                def _():
                    self.along(self.line.next, self.line.two, 0, 3, half).start()

            self.across(step, half, self.k.x).start()

    def arrive(self, step):
        for half in range(self.HALVES):
            self.across(step, half, 1 - self.k.x).wait_recv()

    def drain(self):
        for half in range(self.HALVES):
            for step in range(4):
                self.across(step, half, self.k.x).wait_send()
            for step in (1, 2):
                self.along(self.line.next, self.k.z, step, step, half).wait_send()

            @pl.when(self.line.middle)
            def _():
                for sem in (3, 0):
                    self.along(self.line.next, self.k.z, sem, 3, half).wait_send()


class DownGradient:
    def __init__(self, line, part, near, far, hop, start, size, sems):
        self.line, self.k = line, line.k
        self.part, self.near, self.far, self.hop = part, near, far, hop
        self.cols = pl.ds(start, size)
        self.x_send, self.x_recv, self.z_send, self.z_recv = sems
        self.targets = (line.third, line.next, line.two, self.k.z)

    def one(self, step):
        z = self.targets[step]
        return remote(
            self.part.at[z, 1 - self.k.x, :, self.cols],
            self.near.at[z, :, self.cols],
            self.x_send.at[step],
            self.x_recv.at[step],
            self.k.x_peer,
        )

    def along(self, step, dst, recv, peer):
        return remote(
            self.part.at[self.targets[step], self.k.x, :, self.cols],
            dst.at[:, self.cols],
            self.z_send.at[step],
            self.z_recv.at[recv],
            self.line.peer(peer),
        )

    def start(self, step):
        self.one(step).start()

    def forward(self, step):
        k, line, z = self.k, self.line, self.targets[step]
        self.one(step).wait_recv()
        here = self.part[z, k.x, :, self.cols].astype(F32)
        here = here + self.near[z, :, self.cols].astype(F32)
        if step != 2:
            self.part[z, k.x, :, self.cols] = here.astype(BF16)
        if step == 0:

            @pl.when(line.end)
            def _():
                self.along(0, self.hop, 3, line.next).start()

            @pl.when(line.middle)
            def _():
                self.along(0, self.far.at[2], 0, line.third).start()

        if step == 1:
            self.along(1, self.far.at[1], 1, line.next).start()
        if step == 2:

            @pl.when(line.end)
            def _():
                self.part[z, k.x, :, self.cols] = here.astype(BF16)

            @pl.when(line.middle)
            def _():
                self.along(0, self.hop, 3, line.next).wait_recv()
                both = here + self.hop[:, self.cols].astype(F32)
                self.part[z, k.x, :, self.cols] = both.astype(BF16)

            self.along(2, self.far.at[0], 2, line.two).start()

    def finish(self, out):
        k = self.k

        @pl.when(self.line.middle)
        def _():
            self.along(0, self.far.at[2], 0, k.z).wait_recv()

        total = self.part[k.z, k.x, :, self.cols].astype(F32)
        for n in range(3):
            if n < 2:
                self.along(0, self.far.at[n], 2 - n, k.z).wait_recv()
            total = total + self.far[n, :, self.cols].astype(F32)
        out[...] = total.T

    def drain(self):
        for step in range(4):
            self.one(step).wait_send()
            if step < 3:
                self.along(step, self.far.at[0], 0, self.k.z).wait_send()


def fold(values):
    rows, width = values.shape
    return jnp.sum(values.reshape(rows // 8, 8, width), axis=0)


def mean(values):
    return jnp.sum(values, axis=-1, keepdims=True) * (1.0 / values.shape[-1])


def body(
    outer,
    x_in,
    teacher_in,
    qw_in,
    kw_in,
    vw_in,
    ow_in,
    uw_in,
    dw_in,
    qb_in,
    vb_in,
    ob_in,
    ub_in,
    db_in,
    g1_in,
    b1_in,
    g2_in,
    b2_in,
    out_hbm,
    gin_hbm,
    gq_hbm,
    gk_hbm,
    gv_hbm,
    go_hbm,
    gu_hbm,
    gd_hbm,
    gvec_hbm,
    out_ref,
    gin_ref,
    gq_ref,
    gk_ref,
    gv_ref,
    go_ref,
    gu_ref,
    gd_ref,
    gvec_ref,
    W,
    G,
    near,
    far,
    X,
    H,
    MX,
    GF,
    Q,
    K,
    V,
    C,
    GC,
    DQKV,
    PT,
    SL,
    ACT,
    GU,
    OWN,
    N1,
    R1,
    SUMS,
    ACC,
    OUTBOX,
    INBOX,
    VA,
    VR,
    VZ,
    EA,
    EC,
    EX,
    EZ,
    ET,
    TEACH,
    OT,
    DT,
    VEC,
    w_send,
    w_recv,
    g_send,
    g_recv,
    s_send,
    s_recv,
    r_send,
    r_recv,
    v_send,
    v_recv,
    load_sem,
    flush_sem,
    HOP,
    CFAR,
    CHOP,
    CLAST,
    gx_send,
    gx_recv,
    early_sems,
    dw_sems,
    dg_sems,
    rc_sems,
    sc_sems,
):
    k = Place(outer)
    rows, model = x_in.shape
    width = Q.shape[2]
    inner = ACT.shape[2]
    heads = width // HEAD_DIM
    steps = inner // width
    up_piece = 4
    down_piece = 4 + steps
    pieces = 4 + 2 * steps
    scale = 1.0 / math.sqrt(HEAD_DIM)
    mine, theirs = k.y, 1 - k.y

    own = W.at[k.z, k.x]
    loads = []

    def load(src, dst):
        copy = pltpu.make_async_copy(src, dst, load_sem.at[len(loads)])
        copy.start()
        loads.append(copy)

    load(x_in, X.at[k.t])
    load(qw_in, own.at[:, columns(0, width)])
    load(kw_in, own.at[:, columns(1, width)])
    load(vw_in, own.at[:, columns(2, width)])
    load(ow_in, OT)
    load(uw_in, own.at[:, pl.ds(4 * width, inner)])
    load(dw_in, DT)
    load(teacher_in, TEACH)
    for row, ref in enumerate((qb_in, vb_in, ob_in, db_in, g1_in, b1_in, g2_in, b2_in)):
        load(ref, VEC.at[pl.ds(row, 1), pl.ds(0, model)])
    load(ub_in, VEC.at[pl.ds(8, 1), :])
    k.greet()


    results = (
        (out_ref, out_hbm),
        (gin_ref, gin_hbm),
        (gq_ref, gq_hbm),
        (gk_ref, gk_hbm),
        (gv_ref, gv_hbm),
        (go_ref, go_hbm),
        (gu_ref, gu_hbm),
        (gd_ref, gd_hbm),
        (gvec_ref, gvec_hbm),
    )

    def flush(n):
        return pltpu.make_async_copy(*results[n], flush_sem.at[n])

    def keep(p, total):
        if p < 3:
            (gq_ref, gk_ref, gv_ref)[p][...] = total
            flush(2 + p).start()
        elif p == 3:
            go_ref[...] = total.T
            flush(5).start()
        elif p < down_piece:
            gu_ref[:, (p - up_piece) * width : (p - up_piece + 1) * width] = total
        else:
            gd_ref[(p - down_piece) * width : (p - down_piece + 1) * width, :] = total.T

    stepped = outer == 4 and (model // outer) % 128 == 0
    simple = down_piece if stepped else pieces
    if stepped:
        line = Line(k)
        weights = LineWeights(line, W, w_send, w_recv, width, simple)
        grads = LineGradients(line, HOP, gx_send, gx_recv, G, near, far, keep, g_send, g_recv, width)
        crossed = {
            p: CrossedGradient(
                line, G, CFAR, CHOP, CLAST, keep, g_send, g_recv, width, p, place
            )
            for place, p in enumerate(CROSSED_BACK)
        }
        down_w = DownWeights(line, W, down_piece * width, inner, dw_sems)
        down_g = DownGradient(line, G, near, far, HOP, down_piece * width, inner, dg_sems)
        w_chunks, g_chunks = down_w.sources, down_g.targets
    else:
        weights = Weights(k, W, w_send, w_recv, width, simple)
        grads = Gradients(k, G, near, far, keep, g_send, g_recv, width)

    def relay(p):
        if stepped and p < simple:
            weights.relay(p)

    def relay_back(p):
        if stepped:
            grads.relay(p)

    def spread(blocks, phase):
        return Spread(k, blocks, s_send, s_recv, phase)

    def reduce(phase):
        return Reduce(k, OUTBOX, INBOX, OWN, r_send, r_recv, phase)

    def matrix(start, size):
        return W[:, :, :, pl.ds(start, size)].reshape(model, size)

    def vector(row):
        return VEC[row : row + 1, 0:model]

    def pair(blocks, seq):
        return blocks[pl.ds(2 * seq, 2)].reshape(2 * rows, model)

    def part_rows(core):
        return pl.ds(pl.multiple_of(core * rows, rows), rows)

    def norm_loop(step):
        def one(i, carry):
            step(pl.ds(pl.multiple_of(i * CHUNK, CHUNK), CHUNK))
            return carry

        lax.fori_loop(0, rows // CHUNK, one, 0)

    SUMS[...] = jnp.zeros_like(SUMS)
    VA[0] = jnp.zeros_like(VA[0])
    EA[0] = jnp.zeros_like(EA[0])
    if stepped:
        far[2] = jnp.zeros_like(far[2])
        for place in range(len(CROSSED_BACK)):
            CFAR[place, 2] = jnp.zeros_like(CFAR[place, 2])
    for copy in loads[:4]:
        copy.wait()
    s0 = spread(X, 0)
    k.enter()
    for p in range(WINDOW):
        weights.start(p)
    s0.start()
    for copy in loads[4:]:
        copy.wait()
    own[:, columns(3, width)] = OT[...].T
    own[:, pl.ds(4 * width + inner, inner)] = DT[...].T
    if stepped:
        weights.cross()

    def project(p, held):
        weights.arrive(p)
        for seq in range(2):
            tokens = X[2 * seq : 2 * seq + 2].reshape(2 * rows, model)
            product = dot(tokens, matrix(p * width, width), NN)
            if p != 1:
                here = pl.ds(pl.multiple_of(k.t * width, width), width)
                product = product + VEC[p // 2 : p // 2 + 1, here]
            held[seq] = product.astype(BF16)

    def head_mask(h):
        lane = lax.broadcasted_iota(jnp.int32, (1, width), 1)
        inside = (lane >= h * HEAD_DIM) & (lane < (h + 1) * HEAD_DIM)
        return jnp.where(inside, 1.0, 0.0).astype(BF16)

    def attend(seq, between=lambda: None):
        ACC[0] = jnp.zeros_like(ACC[0])

        def head(h, carry):
            mask = head_mask(h)
            scores = dot(K[seq], Q[seq] * mask, NT) * scale
            raised = jnp.exp(scores - jnp.max(scores, axis=0, keepdims=True))
            probs = (raised * (1.0 / jnp.sum(raised, axis=0, keepdims=True))).astype(BF16)
            PT[seq, h] = probs
            ACC[0] += dot(probs, V[seq] * mask, TN)
            return carry

        lax.fori_loop(0, heads // 2, head, 0)
        between()
        lax.fori_loop(heads // 2, heads, head, 0)
        C[seq] = ACC[0].astype(BF16)

    def out_block(seq, core):
        return dot(C[seq, part_rows(core), :], matrix(3 * width, width), NT)

    relay(0)
    weights.forward(0)
    relay(1)
    weights.forward(1)
    relay(2)
    s0.pass_on()
    s0.own()
    s0.other()
    project(0, Q)
    weights.forward(2)
    project(1, K)
    relay(3)
    if not stepped:
        weights.forward(3)
    project(2, V)
    r0 = reduce(0)
    attend(theirs, lambda: relay(4))
    weights.forward(4)
    weights.arrive(3)
    r0.across(out_block(theirs, 1 - k.c))
    r0.theirs(out_block(theirs, k.c))
    relay(5)
    attend(mine, lambda: weights.forward(5))
    relay(6)
    r0.partner(out_block(mine, 1 - k.c))
    r0.mine(out_block(mine, k.c))
    weights.forward(6)
    relay(7)
    if stepped:
        down_w.forward(0)
        down_w.start(1)
        down_w.start(2)
        down_w.start(3)
    r0.wait()

    def first_norm(r):
        first = X[k.t, r, :].astype(F32) + r0.total(r) + vector(2)
        center = first - mean(first)
        scaling = lax.rsqrt(mean(center * center) + EPSILON)
        normed = center * scaling
        hidden = normed * vector(4) + vector(5)
        N1[r, :] = normed
        R1[r, :] = jnp.broadcast_to(scaling, (CHUNK, R1.shape[1]))
        gin_ref[r, :] = hidden
        H[k.t, r, :] = hidden.astype(BF16)

    norm_loop(first_norm)
    s1 = spread(H, 1)
    s1.start()
    weights.forward(7)
    if not stepped:
        weights.forward(8)
    s1.own()
    for p in range(up_piece, down_piece):
        weights.arrive(p)

    def up(seq):
        def part(n, carry):
            cols = pl.ds(pl.multiple_of(n * width, width), width)
            wide = pl.ds(pl.multiple_of((up_piece + n) * width, width), width)
            upper = dot(pair(H, seq), W[:, :, :, wide].reshape(model, width), NN)
            upper = upper + VEC[8:9, pl.ds(pl.multiple_of(k.t * inner + n * width, width), width)]
            erf_part = 1.0 + lax.erf(upper * (1.0 / ROOT_TWO))
            ACT[seq, :, cols] = (0.5 * upper * erf_part).astype(BF16)
            SL[seq, :, cols] = 0.5 * erf_part + upper * jnp.exp(-0.5 * upper * upper) * (
                1.0 / ROOT_TWO_PI
            )
            return carry

        lax.fori_loop(0, steps, part, 0)

    def down_block(seq, core):
        return dot(ACT[seq, part_rows(core), :], matrix(down_piece * width, inner), NT)

    if stepped:
        up(mine)
        down_w.forward(1)
        s1.pass_on()
        down_w.forward(2)
        s1.other()
        up(theirs)
        r1 = ReduceColumns(k, OUTBOX, INBOX, OWN, r_send, r_recv, 1, outer, rc_sems)
        places = {
            "across": (theirs, 1 - k.c),
            "theirs": (theirs, k.c),
            "partner": (mine, 1 - k.c),
            "mine": (mine, k.c),
        }

        def down_chunk(n):
            shard = W[w_chunks[n], :, :, pl.ds(down_piece * width, inner)]
            shard = shard.reshape(model // outer, inner)

            def block(name):
                seq, core = places[name]
                return dot(ACT[seq, part_rows(core), :], shard, NT)

            r1.step(n, w_chunks[n], block)

        down_w.arrive(0)
        down_chunk(0)
        down_w.forward(3)
        for n in range(1, outer):
            down_w.arrive(n)
            down_chunk(n)
        r1.wait_columns(w_chunks)
    else:
        up(mine)
        weights.forward(9)
        s1.pass_on()
        s1.other()
        up(theirs)
        weights.forward(10)
        weights.forward(11)
        for p in range(down_piece, pieces):
            weights.arrive(p)
        r1 = reduce(1)
        r1.across(down_block(theirs, 1 - k.c))
        r1.theirs(down_block(theirs, k.c))
        r1.partner(down_block(mine, 1 - k.c))
        r1.mine(down_block(mine, k.c))
        r1.wait()

    def norm_back(d, gain, normed, scaling):
        e = d * gain
        return scaling * (e - mean(e) - normed * mean(e * normed))

    def second_norm(r):
        second = gin_ref[r, :] + r1.total(r) + vector(3)
        center = second - mean(second)
        scaling = lax.rsqrt(mean(center * center) + EPSILON)
        normed = center * scaling
        result = normed * vector(6) + vector(7)
        out_ref[r, :] = result.astype(BF16)
        diff = result - TEACH[r, :].astype(F32)
        grad = norm_back(diff, vector(6), normed, scaling)
        gin_ref[r, :] = grad
        MX[k.t, r, :] = grad.astype(BF16)
        SUMS[0] += fold(grad)
        SUMS[1] += fold(diff * normed)
        SUMS[2] += fold(diff)
        SUMS[3] += fold(diff * diff)

    norm_loop(second_norm)
    flush(0).start()
    if stepped:
        s2 = SpreadColumns(k, MX, s_send, s_recv, 2, outer, sc_sems)
        s2.start_columns(g_chunks)
    else:
        s2 = spread(MX, 2)
        s2.start()
    s2.own()

    def back_up(seq):
        def part(n, carry):
            cols = pl.ds(pl.multiple_of(n * width, width), width)
            wide = pl.ds(pl.multiple_of((down_piece + n) * width, width), width)
            grad = dot(pair(MX, seq), W[:, :, :, wide].reshape(model, width), NN)
            grad = (grad * SL[seq, :, cols]).astype(BF16)
            GU[seq, :, cols] = grad
            SUMS[7, :, cols] += fold(grad.astype(F32))
            return carry

        lax.fori_loop(0, steps, part, 0)

    def hidden_block(seq, core):
        return dot(GU[seq, part_rows(core), :], matrix(up_piece * width, inner), NT)

    def weight_grad(left, right, first, begin, end):
        def piece(n, carry):
            cols = pl.ds(pl.multiple_of(n * width, width), width)
            tokens = 4 * rows
            grad = dot(
                left[...].reshape(tokens, model), right[:, :, cols].reshape(tokens, width), TN
            )
            wide = pl.ds(pl.multiple_of((first + n) * width, width), width)
            G[:, :, :, wide] = grad.astype(BF16).reshape(outer, 2, model // (2 * outer), width)

            @pl.when(n > begin)
            def _():
                grads.start(first + n - 1)

            return carry

        lax.fori_loop(begin, end, piece, 0)

    r2 = reduce(2)
    if stepped:
        r1.drain_columns(w_chunks)
        r2.phase_free = False
    back_up(mine)
    r2.partner(hidden_block(mine, 1 - k.c))
    r2.mine(hidden_block(mine, k.c))
    if stepped:

        def down_grad_chunk(n):
            tokens, size = 4 * rows, model // outer
            cols = pl.ds(pl.multiple_of(g_chunks[n] * size, size), size)
            grad = dot(
                MX[:, :, cols].reshape(tokens, size), ACT[...].reshape(tokens, inner), TN
            )
            G[g_chunks[n], :, :, pl.ds(down_piece * width, inner)] = grad.astype(BF16).reshape(
                2, size // 2, inner
            )

        for n in range(outer):
            s2.pass_part(n, g_chunks[n])
            s2.other_part(n, g_chunks[n])
            down_grad_chunk(n)
            down_g.start(n)
        down_g.forward(0)
        back_up(theirs)
        r2.across(hidden_block(theirs, 1 - k.c))
        r2.theirs(hidden_block(theirs, k.c))
        down_g.forward(1)
        weight_grad(H, GU, up_piece, steps - 1, steps)
        crossed[7].start()
        weight_grad(H, GU, up_piece, 0, steps - 1)
        grads.start(up_piece + steps - 2)
        down_g.forward(2)
        down_g.forward(3)
    else:
        s2.pass_on()
        s2.other()
        weight_grad(MX, ACT, down_piece, 0, 2)
        back_up(theirs)
        grads.start(down_piece + 1)
        r2.across(hidden_block(theirs, 1 - k.c))
        r2.theirs(hidden_block(theirs, k.c))
        weight_grad(MX, ACT, down_piece, 2, steps)
        grads.forward(8)
        grads.start(down_piece + steps - 1)
        weight_grad(H, GU, up_piece, 0, steps)
        grads.start(up_piece + steps - 1)
        grads.forward(9)
        grads.forward(10)
    r2.wait()

    def first_back(r):
        grad_hidden = gin_ref[r, :] + r2.total(r)
        normed = N1[r, :]
        grad = norm_back(grad_hidden, vector(4), normed, R1[r, :][:, :1])
        gin_ref[r, :] = grad
        GF[k.t, r, :] = grad.astype(BF16)
        SUMS[4] += fold(grad)
        SUMS[5] += fold(grad_hidden * normed)
        SUMS[6] += fold(grad_hidden)

    norm_loop(first_back)
    s3 = spread(GF, 3)
    s3.start()
    early = Early(k, EA, EC, EX, EZ, ET, early_sems)
    for n, row in ((4, 2), (0, 7), (5, 8), (6, 9), (1, 10), (2, 11), (3, 12)):
        group, place = EARLY_ROWS[row]
        EA[0, group, place : place + 1, :] = jnp.sum(SUMS[n], axis=0, keepdims=True)
    EA[0, 1, pl.ds(k.t, 1), :] = jnp.sum(SUMS[7], axis=0, keepdims=True)
    early.hop(0).start()
    s3.own()

    def attend_back(seq, between=lambda: None):
        GC[...] = dot(pair(GF, seq), matrix(3 * width, width), NN).astype(BF16)
        ACC[...] = jnp.zeros_like(ACC)

        def head(h, carry):
            mask = head_mask(h)
            context = GC[...] * mask
            low = PT[seq, h]
            ACC[2] += dot(low, context, NN)
            probs = low.astype(F32)
            grad = dot(V[seq], context, NT)
            across = jnp.sum(probs * grad, axis=0, keepdims=True)
            grad = (probs * (grad - across)).astype(BF16)
            ACC[1] += dot(grad, Q[seq] * mask, NN)
            ACC[0] += dot(grad, K[seq] * mask, TN)
            return carry

        lax.fori_loop(0, heads // 2, head, 0)
        between()
        lax.fori_loop(heads // 2, heads, head, 0)
        for n in range(3):
            grad = ACC[n] if n == 2 else ACC[n] * scale
            DQKV[seq, :, n * width : (n + 1) * width] = grad.astype(BF16)

    def input_block(seq, core):
        return dot(DQKV[seq, part_rows(core), :], matrix(0, 3 * width), NT)

    if stepped:
        crossed[7].relay()
        grads.forward(4)
        attend_back(mine)
        early.add(0)
        early.hop(1).start()
        grads.forward(5)
        relay_back(4)
        s3.pass_on()
        crossed[7].forward()
        s3.other()
        weight_grad(GF, C, 3, 0, 1)
        grads.forward(6)
        early.add(1)
        early.over().start()
        grads.start(3)
        relay_back(5)
        attend_back(theirs)
        relay_back(6)
    else:
        attend_back(mine)
        early.add(0)
        early.hop(1).start()
        grads.forward(11)
        s3.pass_on()
        grads.forward(4)
        s3.other()
        weight_grad(GF, C, 3, 0, 1)
        grads.forward(5)
        early.add(1)
        early.over().start()
        attend_back(theirs)
        grads.start(3)

    here = pl.ds(pl.multiple_of(k.t * width, width), width)
    for row, n in ((0, 0), (1, 2)):
        grad = DQKV[:, :, n * width : (n + 1) * width].reshape(4 * rows, width).astype(F32)
        VA[0, row : row + 1, here] = jnp.sum(grad, axis=0, keepdims=True)

    two_rows = pl.ds(0, 2)

    def vector_hop(n, peer):
        return remote(
            VA.at[n, two_rows], VR.at[n, two_rows], v_send.at[n], v_recv.at[n], peer
        )

    def vector_last(step):
        return remote(
            VA.at[3, two_rows], VZ.at[k.z, two_rows], v_send.at[3], v_recv.at[3], k.z_peer(step)
        )

    hops = [vector_hop(n, peer) for n, peer in enumerate((k.c_peer, k.y_peer, k.x_peer))]

    def hop_in(n):
        hops[n].wait_recv()
        VA[n + 1, 0:2, :] = VA[n, 0:2, :] + VR[n, 0:2, :]

    if stepped:
        weight_grad(X, DQKV, 0, 2, 3)
        hops[0].start()
        crossed[2].start()
        weight_grad(X, DQKV, 0, 0, 1)
        hop_in(0)
        hops[1].start()
        grads.start(0)
        weight_grad(X, DQKV, 0, 1, 2)
        early.add_over()
        grads.forward(3)
    else:
        weight_grad(X, DQKV, 0, 0, 1)
        hops[0].start()
        weight_grad(X, DQKV, 0, 1, 2)
        grads.start(0)
        hop_in(0)
        hops[1].start()
        weight_grad(X, DQKV, 0, 2, 3)
        grads.start(1)
        grads.forward(6)
    r3 = reduce(3)
    r3.across(input_block(theirs, 1 - k.c))
    if stepped:
        grads.start(1)
        crossed[2].relay()
    r3.theirs(input_block(theirs, k.c))
    hop_in(1)
    hops[2].start()
    if stepped:
        relay_back(3)
        grads.forward(0)
    else:
        early.add_over()
        grads.start(2)
        grads.forward(7)
    r3.partner(input_block(mine, 1 - k.c))
    r3.mine(input_block(mine, k.c))

    def send_last(step, carry):
        vector_last(step).start()
        return carry

    def vectors_along():
        hop_in(2)
        VZ[k.z, 0:2, :] = VA[3, 0:2, :]
        lax.fori_loop(1, outer, send_last, 0)

    early.add_along()
    if stepped:
        relay_back(0)
        grads.forward(1)
        vectors_along()
        crossed[2].forward()
        relay_back(1)
    else:
        for p in (8, 9, 10):
            grads.finish(p)
        grads.forward(3)
        grads.forward(0)
        grads.forward(1)
        vectors_along()
        grads.forward(2)
    r3.wait()

    def last(r):
        gin_ref[r, :] = gin_ref[r, :] + r3.total(r)

    norm_loop(last)
    flush(1).start()
    vz_all = VZ.at[pl.ds(0, outer - 1), two_rows]
    every = remote(vz_all, vz_all, v_send.at[3], v_recv.at[3], k.x_peer)

    def add(i, total):
        return total + VZ[i, 0:2, :]

    def vectors_out():
        every.wait_recv()
        gvec_ref[0:2, :] = lax.fori_loop(1, outer, add, VZ[0, 0:2, :])
        early.finish()
        for row, (group, place) in EARLY_ROWS.items():
            gvec_ref[row : row + 1, :] = ET[group, place : place + 1, :]
        flush(8).start()

    if stepped:
        down_g.finish(gd_ref)
        flush(7).start()
        for p in (4, 5, 6):
            grads.finish(p)
        crossed[7].finish()
        flush(6).start()
        for p in (3, 0):
            grads.finish(p)
        crossed[2].finish()
        vectors_out()
        grads.finish(1)
    else:
        for p in (11, 4, 5, 6, 7, 3, 0, 1):
            grads.finish(p)
        flush(6).start()
        flush(7).start()
        vectors_out()
        grads.finish(2)

    weights.drain(simple)
    grads.drain(simple)
    if stepped:
        down_w.drain()
        down_g.drain()
        for gradient in crossed.values():
            gradient.drain()
        s2.drain_columns(g_chunks)
    for s in (s0, s1, s3) if stepped else (s0, s1, s2, s3):
        s.drain()
    r3.drain()
    for hop in hops:
        hop.wait_send()
    every.wait_send()
    early.drain()
    for n in range(len(results)):
        flush(n).wait()


def layer(outer, arrays):
    inputs, query_weight, up_weight = arrays[0], arrays[2], arrays[6]
    rows, model = inputs.shape
    shard_rows, width = query_weight.shape
    inner = up_weight.shape[1]
    heads = width // HEAD_DIM
    columns_all = 4 * width + 2 * inner
    pieces = columns_all // width
    seq = 2 * rows
    anywhere = pl.BlockSpec(memory_space=pl.ANY)
    full = (outer, 2, shard_rows, columns_all)
    dma = pltpu.SemaphoreType.DMA
    outs = (
        jax.ShapeDtypeStruct((rows, model), BF16),
        jax.ShapeDtypeStruct((rows, model), F32),
        jax.ShapeDtypeStruct((shard_rows, width), F32),
        jax.ShapeDtypeStruct((shard_rows, width), F32),
        jax.ShapeDtypeStruct((shard_rows, width), F32),
        jax.ShapeDtypeStruct((width, shard_rows), F32),
        jax.ShapeDtypeStruct((shard_rows, inner), F32),
        jax.ShapeDtypeStruct((inner, shard_rows), F32),
        jax.ShapeDtypeStruct((VECTORS, model), F32),
    )
    return pl.pallas_call(
        functools.partial(body, outer),
        out_shape=outs,
        in_specs=[anywhere] * len(arrays),
        out_specs=(anywhere,) * len(outs),
        scratch_shapes=[pltpu.VMEM(out.shape, out.dtype) for out in outs]
        + [
            pltpu.VMEM(full, BF16),
            pltpu.VMEM(full, BF16),
            pltpu.VMEM((outer, shard_rows, columns_all), BF16),
            pltpu.VMEM((outer - 1, shard_rows, columns_all), BF16),
            pltpu.VMEM((4, rows, model), BF16),
            pltpu.VMEM((4, rows, model), BF16),
            pltpu.VMEM((4, rows, model), BF16),
            pltpu.VMEM((4, rows, model), BF16),
            pltpu.VMEM((2, seq, width), BF16),
            pltpu.VMEM((2, seq, width), BF16),
            pltpu.VMEM((2, seq, width), BF16),
            pltpu.VMEM((2, seq, width), BF16),
            pltpu.VMEM((seq, width), BF16),
            pltpu.VMEM((2, seq, 3 * width), BF16),
            pltpu.VMEM((2, heads, seq, seq), BF16),
            pltpu.VMEM((2, seq, inner), F32),
            pltpu.VMEM((2, seq, inner), BF16),
            pltpu.VMEM((2, seq, inner), BF16),
            pltpu.VMEM((rows, model), F32),
            pltpu.VMEM((rows, model), F32),
            pltpu.VMEM((rows, 128), F32),
            pltpu.VMEM((8, 8, model), F32),
            pltpu.VMEM((3, seq, width), F32),
            pltpu.VMEM((3, rows, model), BF16),
            pltpu.VMEM((3, rows, model), BF16),
            pltpu.VMEM((4, 8, model), F32),
            pltpu.VMEM((3, 8, model), F32),
            pltpu.VMEM((outer, 8, model), F32),
            pltpu.VMEM((3, 4, 8, model), F32),
            pltpu.VMEM((2, 4, 8, model), F32),
            pltpu.VMEM((2, 8, model), F32),
            pltpu.VMEM((outer, 8, model), F32),
            pltpu.VMEM((4, 8, model), F32),
            pltpu.VMEM((rows, model), BF16),
            pltpu.VMEM((width, shard_rows), BF16),
            pltpu.VMEM((inner, shard_rows), BF16),
            pltpu.VMEM((9, 4 * inner), F32),
            dma((4, pieces)),
            dma((4, pieces)),
            dma((4, pieces)),
            dma((4, pieces)),
            dma((4, 3)),
            dma((4, 3)),
            dma((4, 3)),
            dma((4, 3)),
            dma((4,)),
            dma((4,)),
            dma((len(arrays),)),
            dma((len(outs),)),
            pltpu.VMEM((shard_rows, columns_all), BF16),
            pltpu.VMEM((len(CROSSED_BACK), 3, 2, shard_rows, width), BF16),
            pltpu.VMEM((len(CROSSED_BACK), 2, shard_rows, width), BF16),
            pltpu.VMEM((len(CROSSED_BACK), shard_rows, width), BF16),
            dma((4, pieces)),
            dma((4, pieces)),
            (dma((7,)),) * 2,
            (dma((outer, 2)),) * 4,
            (dma((outer,)),) * 4,
            (dma((3, outer)),) * 2,
            (dma((outer,)),) * 4,
        ],
        compiler_params=pltpu.CompilerParams(
            collective_id=0, has_side_effects=True, vmem_limit_bytes=67043328
        ),
        name="layer",
    )(*arrays)


def write_body(count, factor, *refs):
    ins, outs = refs[:9], refs[9 : 9 + count]
    held, load_sem, sem = refs[9 + count : 18 + count], refs[-2], refs[-1]
    loads = [
        pltpu.make_async_copy(src, dst, load_sem.at[n]) for n, (src, dst) in enumerate(zip(ins, held))
    ]
    vec = held[8]
    pairs = list(zip(held[:8], outs[:8]))
    single = [(0, 8), (1, 9), (2, 10), (7, 12), (8, 13), (9, 14), (10, 15), (11, 16)]
    pairs += [(vec.at[pl.ds(row, 1), :], outs[place]) for row, place in single]
    model = vec.shape[1]
    parts = outs[11].shape[1] // model
    for n in range(parts):
        pairs.append((vec.at[pl.ds(3 + n, 1), :], outs[11].at[:, pl.ds(n * model, model)]))
    copies = [pltpu.make_async_copy(src, dst, sem.at[n]) for n, (src, dst) in enumerate(pairs)]
    order = (8, 5, 2, 3, 4, 6, 7, 0, 1)
    for n in order:
        loads[n].start()
    for n in order:
        loads[n].wait()
        for copy in copies[8:] if n == 8 else copies[n : n + 1]:
            copy.start()
    outs[17][0, 0] = jnp.sum(vec[12:13, :]) * factor
    for copy in copies:
        copy.wait()


def write(values, up_length, factor):
    model = values[8].shape[1]
    line = jax.ShapeDtypeStruct((1, model), F32)
    outs = [jax.ShapeDtypeStruct(v.shape, v.dtype) for v in values[:8]] + [line] * 10
    outs[11] = jax.ShapeDtypeStruct((1, up_length), F32)
    outs[17] = jax.ShapeDtypeStruct((1, 1), F32)
    copies = 16 + up_length // model
    anywhere = pl.BlockSpec(memory_space=pl.ANY)
    return pl.pallas_call(
        functools.partial(write_body, len(outs), factor),
        out_shape=tuple(outs),
        in_specs=[anywhere] * len(values),
        out_specs=(anywhere,) * 17 + (pl.BlockSpec(memory_space=pltpu.SMEM),),
        scratch_shapes=[pltpu.VMEM(v.shape, v.dtype) for v in values]
        + [pltpu.SemaphoreType.DMA((len(values),)), pltpu.SemaphoreType.DMA((copies,))],
        name="write",
    )(*values)


def shards(*arrays):
    inputs = arrays[0]
    outer = lax.axis_size("dp") // 2
    arrays = arrays[:8] + tuple(v.reshape(1, -1) for v in arrays[8:])
    up_length = arrays[11].shape[1]
    token_total = inputs.shape[0] * lax.axis_size("dp") * lax.axis_size("tensor")
    values = write(layer(outer, arrays), up_length, 0.5 / token_total)
    loss = values[17].reshape(())
    output, grad_inputs, gq, gk, gv, go, gu, gd = values[:8]
    return (output, loss, grad_inputs, gq, gk, gv, go, gu, gd) + tuple(
        v.reshape(-1) for v in values[8:17]
    )


def solution(mesh):
    tokens = P(("dp", "tensor"), None)
    across, down = P("dp", "tensor"), P("tensor", "dp")
    in_specs = (tokens, tokens, across, across, across, down, across, down) + (P(),) * 9
    out_specs = (tokens, P(), tokens, across, across, across, down, across, down) + (P(),) * 9
    return jax.shard_map(shards, mesh=mesh, in_specs=in_specs, out_specs=out_specs, check_vma=False)
```
